256 devices in a mesh: gx: 4 (over z_hi), gy: 16 (over x, z_lo, core), gz: 4 (over y).
Axes of the slice: x: 4, y: 4, z: 8 (z_hi: 4, z_lo: 2; z = z_hi * 2 + z_lo), core: 2. Of those that a mesh axis runs over, the one named last changes fastest.
Arguments:
- old_fields: float32 [2, 32, 64, 16, 1024], P(None, 'gy', 'gz', None, 'gx'), may hold values from -6 to 6
- old_coef: bfloat16 [4, 32, 64, 16, 1024], P(None, 'gy', 'gz', None, 'gx'), may hold values from 0.25 to 4
- held_slabs: int32 [32, 4, 4], P('gy', 'gz', 'gx'), may hold values from 0 to 24, as said below
Outputs:
- solution: float32 [64, 384, 1024], P('gz', 'gy', 'gx')
- residual: float32 [64, 384, 1024], P('gz', 'gy', 'gx')
The draws below stay inside these ranges and needn't reach their ends.
Inputs may be any that keep to these rules, and one draw needn't show every extreme that they name: `held_slabs`: in every column of bricks and for every p below 8, rows 4p to 4p + 3 hold the old slabs 3p, 3p + 1, 3p + 2 once each and one entry 24, which marks an empty slot.
All inputs are finite; a program needn't handle non-finite values.
Results may differ from the reference program's by a relative error of at most 0.0003.
Values may be sent and summed in bfloat16 or wider, within the bound.
A program may use at most 64 MiB of HBM per device.

```python
import math
import jax
import jax.numpy as jnp

UNIT = 8
CZ = 16
CX = 256
SWEEPS = 4
SLOTS = 2
NX = 1024
NY = 384
NZ = 64
OLD_Y = 24
N_GX = 4
N_GY = 16
N_GZ = 4


def draw_held_slabs(key, part):
    pair_count = N_GY // 2
    slot_scores = jax.random.randint(key, (pair_count, N_GZ, N_GX, 4), 0, 1 << 20) * 4 + jnp.arange(4, dtype=jnp.int32)
    slot_order = jnp.argsort(slot_scores, axis=-1)
    slot_rank = jnp.argsort(slot_order, axis=-1).astype(jnp.int32)
    first_slab = (3 * jnp.arange(pair_count, dtype=jnp.int32))[:, None, None, None]
    slab_values = jnp.where(slot_rank < 3, first_slab + slot_rank, OLD_Y)
    slab_values = jnp.transpose(slab_values, (0, 3, 1, 2))
    return slab_values.reshape(2 * N_GY, N_GZ, N_GX).astype(jnp.int32)


def steps_of(own_key, dims, cuts, least, high):
    gain, own = 1.0, jax.random.fold_in(own_key, 6)
    for dim, blocks in cuts:
        draws = jnp.exp(jax.random.uniform(jax.random.fold_in(own, dim), (blocks,), jnp.float32, least / len(cuts), high / len(cuts)))
        gain = gain * jnp.repeat(draws, dims[dim] // blocks).reshape([-1 if axis == dim else 1 for axis in range(len(dims))])
    return gain


def noise(own_key, extent, deviation, most, pieces=(), kind=jnp.bfloat16):
    entries = deviation * jax.random.normal(own_key, extent, jnp.float32)
    if pieces:
        entries = entries * steps_of(own_key, extent, pieces, -0.22, 0.18)
    return jnp.clip(entries, -most, most).astype(kind)


def setup_inputs(seed: int = 0) -> dict:
    key_of = jax.random.split(jax.random.key(seed), 4)
    return {
        "old_fields": noise(key_of[0], (2, SLOTS * N_GY, NZ, 2 * UNIT, NX), 1.0, 6.0, ((1, 16), (2, 4), (4, 4)), jnp.float32),
        "old_coef": jnp.clip(jnp.exp(math.log(4.0) - 2.7725887 * jax.random.uniform(key_of[1], (4, SLOTS * N_GY, NZ, 2 * UNIT, NX), jnp.float32) ** steps_of(key_of[1], (4, SLOTS * N_GY, NZ, 2 * UNIT, NX), ((1, 16), (2, 4), (4, 4)), -0.2, 0.2)), 0.25, 4.0).astype(jnp.bfloat16),
        "held_slabs": draw_held_slabs(jax.random.fold_in(key_of[3], 71), 0),
    }


def chebyshev_weights(count):
    low_bound = 0.25
    high_bound = 2.0
    centre_value = 0.5 * (high_bound + low_bound)
    half_width = 0.5 * (high_bound - low_bound)
    ratio_value = centre_value / half_width
    damping = 1.0 / ratio_value
    first_list = [0.0]
    second_list = [1.0 / centre_value]
    for step_index in range(1, count):
        damping_next = 1.0 / (2.0 * ratio_value - damping)
        first_list.append(damping_next * damping)
        second_list.append(2.0 * damping_next / half_width)
        damping = damping_next
    return first_list, second_list


def assemble(old_array, held_slabs):
    field_count = old_array.shape[0]
    slot_total = old_array.shape[1]
    grouped = old_array.reshape(field_count, slot_total, N_GZ, CZ, 2 * UNIT, N_GX, CX)
    grouped = jnp.transpose(grouped, (1, 2, 5, 0, 3, 4, 6))
    slab_numbers = jnp.arange(OLD_Y, dtype=jnp.int32)
    slot_rows = jnp.arange(slot_total, dtype=jnp.int32)
    matches = held_slabs[None, :, :, :] == slab_numbers[:, None, None, None]
    holder_rows = jnp.sum(jnp.where(matches, slot_rows[None, :, None, None], 0), axis=1).astype(jnp.int32)
    column_z = jnp.arange(N_GZ, dtype=jnp.int32)[None, :, None]
    column_x = jnp.arange(N_GX, dtype=jnp.int32)[None, None, :]
    picked = grouped[holder_rows, column_z, column_x]
    picked = jnp.transpose(picked, (3, 1, 4, 0, 5, 2, 6))
    return picked.reshape(field_count, NZ, NY, NX)


def operator_apply(field, face_terms):
    cell_alpha, beta_x, upper_x, beta_y, upper_y, beta_z, upper_z = face_terms
    result = cell_alpha * field
    result = result + beta_x * (field - jnp.roll(field, 1, 2)) + upper_x * (field - jnp.roll(field, -1, 2))
    result = result + beta_y * (field - jnp.roll(field, 1, 1)) + upper_y * (field - jnp.roll(field, -1, 1))
    result = result + beta_z * (field - jnp.roll(field, 1, 0)) + upper_z * (field - jnp.roll(field, -1, 0))
    return result


def reference(old_fields, old_coef, held_slabs):
    grid_fields = assemble(old_fields, held_slabs)
    grid_coef = assemble(old_coef, held_slabs)
    solution = grid_fields[0]
    rhs_field = grid_fields[1]
    cell_alpha = grid_coef[0].astype(jnp.float32)
    beta_x = grid_coef[1].astype(jnp.float32)
    beta_y = grid_coef[2].astype(jnp.float32)
    beta_z = grid_coef[3].astype(jnp.float32)
    upper_x = jnp.roll(beta_x, -1, 2)
    upper_y = jnp.roll(beta_y, -1, 1)
    upper_z = jnp.roll(beta_z, -1, 0)
    face_terms = (cell_alpha, beta_x, upper_x, beta_y, upper_y, beta_z, upper_z)
    diagonal = cell_alpha + beta_x + upper_x + beta_y + upper_y + beta_z + upper_z
    inverse = 1.0 / diagonal
    first_list, second_list = chebyshev_weights(SWEEPS)
    residual = rhs_field - operator_apply(solution, face_terms)
    direction = jnp.zeros_like(solution)
    for sweep_index in range(SWEEPS):
        direction = first_list[sweep_index] * direction + second_list[sweep_index] * (inverse * residual)
        solution = solution + direction
        residual = residual - operator_apply(direction, face_terms)
    return solution, residual
```

```python
import functools
import jax
import jax.numpy as jnp
from jax import lax
from jax.experimental import pallas as pl
from jax.experimental.pallas import tpu as pltpu
from jax.sharding import PartitionSpec as P

SWEEPS = 4
NZ = 16
NY = 24
NX = 256
ROWS = 8
LANES = 128
GROUPS = NY // ROWS
PLANES = 4
MESH = pl.DeviceIdType.MESH
F32 = jnp.float32
BF16 = jnp.bfloat16


def chebyshev_weights(count):
    low_bound = 0.25
    high_bound = 2.0
    centre_value = 0.5 * (high_bound + low_bound)
    half_width = 0.5 * (high_bound - low_bound)
    ratio_value = centre_value / half_width
    damping = 1.0 / ratio_value
    first_list = [0.0]
    second_list = [1.0 / centre_value]
    for step_index in range(1, count):
        damping_next = 1.0 / (2.0 * ratio_value - damping)
        first_list.append(damping_next * damping)
        second_list.append(2.0 * damping_next / half_width)
        damping = damping_next
    return first_list, second_list


FIRST, SECOND = chebyshev_weights(SWEEPS)


def ring(axis):
    count = lax.axis_size(axis)
    me = lax.axis_index(axis)
    low = {axis: lax.rem(me + count - 1, count)}
    high = {axis: lax.rem(me + 1, count)}
    return low, high


def kernel(
    fields_hbm, coef_hbm, held_ref, x_hbm, r_hbm,
    slots_f, slots_c, send_f, send_c, recv_f, recv_c,
    field, alpha, bx, by, bz, rhs, near, diag, scaled, total, resid,
    pack, face_y, halo_x, halo_y, rim_pack, rim_face, rim_x, rim_y,
    load_sem, pair_send, pair_recv, halo_send, halo_recv, rim_send, rim_recv, out_sem,
):
    loads_f = [pltpu.make_async_copy(fields_hbm.at[c], slots_f.at[c], load_sem.at[c]) for c in range(2)]
    loads_c = [pltpu.make_async_copy(coef_hbm.at[c], slots_c.at[c], load_sem.at[2 + c]) for c in range(4)]
    loads_f[0].start()
    for c in (1, 2, 3, 0):
        loads_c[c].start()
    loads_f[1].start()

    group = lax.axis_index("gy")
    half = lax.rem(group, 2)
    first_slab = 3 * (group // 2)
    partner = {"gy": group + 1 - 2 * half}
    x_low, x_high = ring("gx")
    y_low, y_high = ring("gy")
    z_low, z_high = ring("gz")

    barrier = pltpu.get_barrier_semaphore()
    for neighbour in (x_low, x_high, y_low, y_high, z_low, z_high):
        pl.semaphore_signal(barrier, inc=1, device_id=neighbour, device_id_type=MESH)

    id0 = held_ref[0, 0, 0]
    id1 = held_ref[1, 0, 0]
    mine = [first_slab + (3 * half + g) // 2 for g in range(GROUPS)]
    theirs = [first_slab + (3 * (1 - half) + g) // 2 for g in range(GROUPS)]
    my_part = [lax.rem(half + g, 2) for g in range(GROUPS)]
    their_part = [lax.rem(1 - half + g, 2) for g in range(GROUPS)]

    row = lax.broadcasted_iota(jnp.int32, (NY, LANES), 0)
    lane = lax.broadcasted_iota(jnp.int32, (NY, LANES), 1)
    lane8 = lax.broadcasted_iota(jnp.int32, (ROWS, LANES), 1)
    top_row = row == 0
    end_row = row == NY - 1
    first_lane = lane == 0
    last_lane = lane == LANES - 1

    def copy_to(source, target, send_sem, recv_sem, device):
        return pltpu.make_async_remote_copy(
            src_ref=source, dst_ref=target, send_sem=send_sem, recv_sem=recv_sem,
            device_id=device, device_id_type=MESH,
        )

    pair_f = [copy_to(send_f.at[c], recv_f.at[c], pair_send.at[c], pair_recv.at[c], partner) for c in range(2)]
    pair_c = [
        copy_to(send_c.at[c], recv_c.at[c], pair_send.at[2 + c], pair_recv.at[2 + c], partner) for c in range(4)
    ]

    def halo_copies(k):
        return [
            copy_to(pack.at[k], halo_x.at[k, 1], halo_send.at[k, 0], halo_recv.at[k, 0], x_low),
            copy_to(pack.at[k], halo_x.at[k, 0], halo_send.at[k, 1], halo_recv.at[k, 1], x_high),
            copy_to(face_y.at[k, 0], halo_y.at[k, 1], halo_send.at[k, 2], halo_recv.at[k, 2], y_low),
            copy_to(face_y.at[k, 1], halo_y.at[k, 0], halo_send.at[k, 3], halo_recv.at[k, 3], y_high),
            copy_to(field.at[k, 1], field.at[k, NZ + 1], halo_send.at[k, 4], halo_recv.at[k, 4], z_low),
            copy_to(field.at[k, NZ], field.at[k, 0], halo_send.at[k, 5], halo_recv.at[k, 5], z_high),
        ]

    halos = [halo_copies(k) for k in range(SWEEPS + 1)]
    rims = [
        copy_to(rim_pack, rim_x, rim_send.at[0], rim_recv.at[0], x_low),
        copy_to(rim_face, rim_y, rim_send.at[1], rim_recv.at[1], y_low),
        copy_to(bz.at[0], bz.at[NZ], rim_send.at[2], rim_recv.at[2], z_low),
    ]

    def planes(body, carry=None):
        def step(i, carry):
            for j in range(PLANES):
                carry = body(i * PLANES + j, carry)
            return carry

        return lax.fori_loop(0, NZ // PLANES, step, carry)

    def prepare(slots, out):
        def body(z, carry):
            for g in range(GROUPS):
                out[z, g] = lax.select(id0 == theirs[g], slots[0, z, their_part[g]], slots[1, z, their_part[g]])
            return carry

        planes(body, 0)

    def assembled(slots, received, z, g):
        return lax.select(
            id0 == mine[g],
            slots[0, z, my_part[g]],
            lax.select(id1 == mine[g], slots[1, z, my_part[g]], received[z, g]),
        ).astype(F32)

    def packed(k_index, tile_low, tile_high, carry, g):
        spot = k_index * GROUPS + g
        both = jnp.where(lane8 == 0, tile_low, tile_high)
        moved = pltpu.roll(both, 2 * spot + 1, 1)
        return jnp.where(lane8 // 2 == spot, moved, carry)

    loads_f[0].wait()
    prepare(slots_f.at[0], send_f.at[0])
    pl.semaphore_wait(barrier, 6)
    pair_f[0].start()
    for c in (1, 2, 3, 0):
        loads_c[c].wait()
        prepare(slots_c.at[c], send_c.at[c])
        pair_c[c].start()
    loads_f[1].wait()
    prepare(slots_f.at[1], send_f.at[1])
    pair_f[1].start()

    zero_pack = jnp.zeros((ROWS, LANES), F32)

    pair_f[0].wait_recv()

    def start_body(z, carry):
        for g in range(GROUPS):
            value = assembled(slots_f.at[0], recv_f.at[0], z, g)
            field[0, z + 1, g * ROWS : (g + 1) * ROWS, :] = value
            total[z, g * ROWS : (g + 1) * ROWS, :] = value
            if g == 0:
                face_y[0, 0, z] = value[0:1, :]
            if g == GROUPS - 1:
                face_y[0, 1, z] = value[ROWS - 1 : ROWS, :]
            carry = packed(z, value[:, :LANES], value[:, LANES:], carry, g)
        return carry

    pack[0] = planes(start_body, zero_pack)
    for copy in halos[0]:
        copy.start()

    pair_c[1].wait_recv()

    def bx_body(z, carry):
        for g in range(GROUPS):
            value = assembled(slots_c.at[1], recv_c.at[1], z, g)
            bx[z, g * ROWS : (g + 1) * ROWS, :] = value
            carry = packed(z, value[:, :LANES], value[:, LANES:], carry, g)
        return carry

    rim_pack[...] = planes(bx_body, zero_pack)
    rims[0].start()
    pair_c[2].wait_recv()

    def by_body(z, carry):
        for g in range(GROUPS):
            value = assembled(slots_c.at[2], recv_c.at[2], z, g)
            by[z, g * ROWS : (g + 1) * ROWS, :] = value
            if g == 0:
                rim_face[z] = value[0:1, :]
        return carry

    planes(by_body, 0)
    rims[1].start()
    pair_c[3].wait_recv()

    def bz_body(z, carry):
        for g in range(GROUPS):
            bz[z, g * ROWS : (g + 1) * ROWS, :] = assembled(slots_c.at[3], recv_c.at[3], z, g)
        return carry

    planes(bz_body, 0)
    rims[2].start()
    pair_c[0].wait_recv()

    def alpha_body(z, carry):
        for g in range(GROUPS):
            alpha[z, g * ROWS : (g + 1) * ROWS, :] = assembled(slots_c.at[0], recv_c.at[0], z, g)
        return carry

    planes(alpha_body, 0)
    pair_f[1].wait_recv()

    def rhs_body(z, carry):
        for g in range(GROUPS):
            rhs[z, g * ROWS : (g + 1) * ROWS, :] = assembled(slots_f.at[1], recv_f.at[1], z, g)
        return carry

    planes(rhs_body, 0)
    for copy in rims:
        copy.wait_recv()

    def spread(source, z, from_right):
        pieces = []
        for g in range(GROUPS):
            spot = z * GROUPS + g
            shift = 126 - 2 * spot if from_right else lax.rem(LANES - 2 * spot, LANES)
            pieces.append(pltpu.roll(source, shift, 1))
        return jnp.concatenate(pieces, axis=0)

    def shifted_left(low, high, edge):
        low_rolled = pltpu.roll(low, LANES - 1, 1)
        high_rolled = pltpu.roll(high, LANES - 1, 1)
        return jnp.where(last_lane, high_rolled, low_rolled), jnp.where(last_lane, edge, high_rolled)

    def shifted_right(low, high, edge):
        low_rolled = pltpu.roll(low, 1, 1)
        high_rolled = pltpu.roll(high, 1, 1)
        return jnp.where(first_lane, edge, low_rolled), jnp.where(first_lane, low_rolled, high_rolled)

    def up_rows(tile, edge):
        return jnp.where(end_row, jnp.broadcast_to(edge, (NY, LANES)), pltpu.roll(tile, NY - 1, 0))

    def down_rows(tile, edge):
        return jnp.where(top_row, jnp.broadcast_to(edge, (NY, LANES)), pltpu.roll(tile, 1, 0))

    halves = (slice(0, LANES), slice(LANES, NX))

    rim_values = rim_x[...]

    def scale_body(z, carry):
        upper_x = shifted_left(bx[z, :, :LANES], bx[z, :, LANES:], spread(rim_values, z, True))
        for j, part in enumerate(halves):
            faces = [bx[z, :, part], upper_x[j], by[z, :, part]]
            faces.append(up_rows(faces[2], rim_y[z, :, part]))
            faces.append(bz[z, :, part])
            faces.append(bz[z + 1, :, part])
            centre = alpha[z, :, part]
            for face in faces:
                centre = centre + face
            inverse = 1.0 / centre
            diag[z, :, part] = centre
            for i, face in enumerate(faces):
                near[i, z, :, part] = inverse * face
            scaled[z, :, part] = inverse * rhs[z, :, part]
        return carry

    planes(scale_body, 0)

    def apply(k):
        for copy in halos[k]:
            copy.wait_recv()
        from_low = halo_x[k, 0]
        from_high = halo_x[k, 1]
        last = k == SWEEPS

        def body(z, carry):
            low, high = field[k, z + 1, :, :LANES], field[k, z + 1, :, LANES:]
            x_before = shifted_right(low, high, spread(from_low, z, False))
            x_after = shifted_left(low, high, spread(from_high, z, True))
            fresh = []
            for j, part in enumerate(halves):
                here = (low, high)[j]
                value = scaled[z, :, part] - here
                value = value + near[0, z, :, part] * x_before[j] + near[1, z, :, part] * x_after[j]
                value = value + near[2, z, :, part] * down_rows(here, halo_y[k, 0, z, :, part])
                value = value + near[3, z, :, part] * up_rows(here, halo_y[k, 1, z, :, part])
                value = value + near[4, z, :, part] * field[k, z, :, part]
                value = value + near[5, z, :, part] * field[k, z + 2, :, part]
                if last:
                    resid[z, :, part] = diag[z, :, part] * value
                    continue
                scaled[z, :, part] = value
                step = SECOND[k] * value
                if k > 0:
                    step = step + FIRST[k] * here
                field[k + 1, z + 1, :, part] = step
                total[z, :, part] = total[z, :, part] + step
                face_y[k + 1, 0, z, :, part] = step[0:1, :]
                face_y[k + 1, 1, z, :, part] = step[NY - 1 : NY, :]
                fresh.append(step)
            if last:
                return carry
            for g in range(GROUPS):
                rows = slice(g * ROWS, (g + 1) * ROWS)
                carry = packed(z, fresh[0][rows], fresh[1][rows], carry, g)
            return carry

        return planes(body, zero_pack)

    for k in range(SWEEPS):
        pack[k + 1] = apply(k)
        for copy in halos[k + 1]:
            copy.start()
    x_out = pltpu.make_async_copy(total, x_hbm, out_sem.at[0])
    x_out.start()
    apply(SWEEPS)
    r_out = pltpu.make_async_copy(resid, r_hbm, out_sem.at[1])
    r_out.start()
    for copy in pair_f + pair_c + rims:
        copy.wait_send()
    for copies in halos:
        for copy in copies:
            copy.wait_send()
    x_out.wait()
    r_out.wait()


def local(old_fields, old_coef, held_slabs):
    slots = old_fields.shape[1]
    fields = old_fields.reshape(2, slots, NZ, 2, ROWS, NX)
    coef = old_coef.reshape(4, slots, NZ, 2, ROWS, NX)
    brick = (NZ, NY, NX)
    rounds = SWEEPS + 1
    dma = pltpu.SemaphoreType.DMA
    anywhere = pl.BlockSpec(memory_space=pl.ANY)
    return pl.pallas_call(
        kernel,
        out_shape=(jax.ShapeDtypeStruct(brick, F32), jax.ShapeDtypeStruct(brick, F32)),
        in_specs=[anywhere, anywhere, pl.BlockSpec(memory_space=pltpu.SMEM)],
        out_specs=(anywhere, anywhere),
        scratch_shapes=[
            pltpu.VMEM((2, slots, NZ, 2, ROWS, NX), F32),
            pltpu.VMEM((4, slots, NZ, 2, ROWS, NX), BF16),
            pltpu.VMEM((2, NZ, GROUPS, ROWS, NX), F32),
            pltpu.VMEM((4, NZ, GROUPS, ROWS, NX), BF16),
            pltpu.VMEM((2, NZ, GROUPS, ROWS, NX), F32),
            pltpu.VMEM((4, NZ, GROUPS, ROWS, NX), BF16),
            pltpu.VMEM((rounds, NZ + 2, NY, NX), F32),
            pltpu.VMEM(brick, F32),
            pltpu.VMEM(brick, F32),
            pltpu.VMEM(brick, F32),
            pltpu.VMEM((NZ + 1, NY, NX), F32),
            pltpu.VMEM(brick, F32),
            pltpu.VMEM((6, NZ, NY, NX), F32),
            pltpu.VMEM(brick, F32),
            pltpu.VMEM(brick, F32),
            pltpu.VMEM(brick, F32),
            pltpu.VMEM(brick, F32),
            pltpu.VMEM((rounds, ROWS, LANES), F32),
            pltpu.VMEM((rounds, 2, NZ, 1, NX), F32),
            pltpu.VMEM((rounds, 2, ROWS, LANES), F32),
            pltpu.VMEM((rounds, 2, NZ, 1, NX), F32),
            pltpu.VMEM((ROWS, LANES), F32),
            pltpu.VMEM((NZ, 1, NX), F32),
            pltpu.VMEM((ROWS, LANES), F32),
            pltpu.VMEM((NZ, 1, NX), F32),
            dma((6,)),
            dma((6,)),
            dma((6,)),
            dma((rounds, 6)),
            dma((rounds, 6)),
            dma((3,)),
            dma((3,)),
            dma((2,)),
        ],
        compiler_params=pltpu.CompilerParams(
            collective_id=0, has_side_effects=True, vmem_limit_bytes=48 << 20
        ),
        name="smooth",
    )(fields, coef, held_slabs)


def solution(mesh):
    in_specs = (
        P(None, "gy", "gz", None, "gx"),
        P(None, "gy", "gz", None, "gx"),
        P("gy", "gz", "gx"),
    )
    out_specs = (P("gz", "gy", "gx"), P("gz", "gy", "gx"))
    return jax.shard_map(local, mesh=mesh, in_specs=in_specs, out_specs=out_specs, check_vma=False)
```

```python
import functools
import jax
import jax.numpy as jnp
from jax import lax
from jax.experimental import pallas as pl
from jax.experimental.pallas import tpu as pltpu
from jax.sharding import PartitionSpec as P

SWEEPS = 4
NZ = 16
NY = 24
NX = 256
ROWS = 8
LANES = 128
GROUPS = NY // ROWS
MESH = pl.DeviceIdType.MESH
F32 = jnp.float32
BF16 = jnp.bfloat16


def chebyshev_weights(count):
    low_bound = 0.25
    high_bound = 2.0
    centre_value = 0.5 * (high_bound + low_bound)
    half_width = 0.5 * (high_bound - low_bound)
    ratio_value = centre_value / half_width
    damping = 1.0 / ratio_value
    first_list = [0.0]
    second_list = [1.0 / centre_value]
    for step_index in range(1, count):
        damping_next = 1.0 / (2.0 * ratio_value - damping)
        first_list.append(damping_next * damping)
        second_list.append(2.0 * damping_next / half_width)
        damping = damping_next
    return first_list, second_list


FIRST, SECOND = chebyshev_weights(SWEEPS)


def ring(axis):
    count = lax.axis_size(axis)
    me = lax.axis_index(axis)
    low = {axis: lax.rem(me + count - 1, count)}
    high = {axis: lax.rem(me + 1, count)}
    return low, high


def kernel(
    fields_hbm, coef_hbm, held_hbm, x_hbm, r_hbm,
    slots_f, slots_c, send_f, send_c, recv_f, recv_c,
    field, alpha, bx, by, bz, rhs, near, edge_y, edge_x, diag, scaled, total, resid,
    pack, face_y, halo_x, halo_y, rim_pack, rim_face, rim_x, rim_y, held_ref,
    load_sem, held_sem, pair_send, pair_recv, halo_send, halo_recv, rim_send, rim_recv, out_sem,
):
    group = lax.axis_index("gy")
    half = lax.rem(group, 2)
    first_slab = 3 * (group // 2)
    partner = {"gy": group + 1 - 2 * half}
    x_low, x_high = ring("gx")
    y_low, y_high = ring("gy")
    z_low, z_high = ring("gz")

    barrier = pltpu.get_barrier_semaphore()
    for neighbour in (x_low, x_high, y_low, y_high, z_low, z_high):
        pl.semaphore_signal(barrier, inc=1, device_id=neighbour, device_id_type=MESH)

    load_held = pltpu.make_async_copy(held_hbm, held_ref, held_sem.at[0])
    loads_f = [pltpu.make_async_copy(fields_hbm.at[c], slots_f.at[c], load_sem.at[c]) for c in range(2)]
    loads_c = [pltpu.make_async_copy(coef_hbm.at[c], slots_c.at[c], load_sem.at[2 + c]) for c in range(4)]
    load_held.start()
    loads_f[0].start()
    for c in (1, 2, 3, 0):
        loads_c[c].start()
    loads_f[1].start()
    load_held.wait()

    id0 = held_ref[0, 0, 0]
    id1 = held_ref[0, 0, 1]
    mine = [first_slab + (3 * half + g) // 2 for g in range(GROUPS)]
    theirs = [first_slab + (3 * (1 - half) + g) // 2 for g in range(GROUPS)]
    my_part = [lax.rem(half + g, 2) for g in range(GROUPS)]
    their_part = [lax.rem(1 - half + g, 2) for g in range(GROUPS)]

    row8 = lax.broadcasted_iota(jnp.int32, (ROWS, LANES), 0)
    row = lax.broadcasted_iota(jnp.int32, (NY, LANES), 0)
    lane = lax.broadcasted_iota(jnp.int32, (NY, LANES), 1)
    lane8 = lax.broadcasted_iota(jnp.int32, (ROWS, LANES), 1)
    end_row = row == NY - 1
    first_lane = lane == 0
    last_lane = lane == LANES - 1
    spots = lane8 // 2

    def copy_to(source, target, send_sem, recv_sem, device):
        return pltpu.make_async_remote_copy(
            src_ref=source, dst_ref=target, send_sem=send_sem, recv_sem=recv_sem,
            device_id=device, device_id_type=MESH,
        )

    pair_f = [copy_to(send_f.at[c], recv_f.at[c], pair_send.at[c], pair_recv.at[c], partner) for c in range(2)]
    pair_c = [
        copy_to(send_c.at[c], recv_c.at[c], pair_send.at[2 + c], pair_recv.at[2 + c], partner) for c in range(4)
    ]

    def halo_copies(k):
        return [
            copy_to(field.at[k, 1], field.at[k, NZ + 1], halo_send.at[k, 4], halo_recv.at[k, 4], z_low),
            copy_to(field.at[k, NZ], field.at[k, 0], halo_send.at[k, 5], halo_recv.at[k, 5], z_high),
            copy_to(face_y.at[k, 0], halo_y.at[k, 1], halo_send.at[k, 2], halo_recv.at[k, 2], y_low),
            copy_to(face_y.at[k, 1], halo_y.at[k, 0], halo_send.at[k, 3], halo_recv.at[k, 3], y_high),
            copy_to(pack.at[k], halo_x.at[k, 1], halo_send.at[k, 0], halo_recv.at[k, 0], x_low),
            copy_to(pack.at[k], halo_x.at[k, 0], halo_send.at[k, 1], halo_recv.at[k, 1], x_high),
        ]

    halos = [halo_copies(k) for k in range(SWEEPS + 1)]
    rims = [
        copy_to(rim_pack, rim_x, rim_send.at[0], rim_recv.at[0], x_low),
        copy_to(rim_face, rim_y, rim_send.at[1], rim_recv.at[1], y_low),
        copy_to(bz.at[0], bz.at[NZ], rim_send.at[2], rim_recv.at[2], z_low),
    ]

    def planes(body, carry=0, first=0, last=NZ):
        return lax.fori_loop(first, last, body, carry, unroll=True)

    def prepare(slots, out):
        def body(z, carry):
            for g in range(GROUPS):
                out[z, g] = lax.select(id0 == theirs[g], slots[0, z, their_part[g]], slots[1, z, their_part[g]])
            return carry

        planes(body)

    def assembled(slots, received, z, g):
        return lax.select(
            id0 == mine[g],
            slots[0, z, my_part[g]],
            lax.select(id1 == mine[g], slots[1, z, my_part[g]], received[z, g]),
        ).astype(F32)

    def packed(z, g, tile_low, tile_high, carry):
        spot = z * GROUPS + g
        both = jnp.where(lane8 == 0, tile_low, tile_high)
        moved = pltpu.roll(both, 2 * spot + 1, 1)
        return jnp.where(spots == spot, moved, carry)

    loads_f[0].wait()
    prepare(slots_f.at[0], send_f.at[0])
    pl.semaphore_wait(barrier, 6)
    pair_f[0].start()
    for c in (1, 2, 3, 0):
        loads_c[c].wait()
        prepare(slots_c.at[c], send_c.at[c])
        pair_c[c].start()
    loads_f[1].wait()
    prepare(slots_f.at[1], send_f.at[1])
    pair_f[1].start()

    zero_pack = jnp.zeros((ROWS, LANES), F32)

    pair_f[0].wait_recv()

    def start_body(z, carry):
        for g in range(GROUPS):
            value = assembled(slots_f.at[0], recv_f.at[0], z, g)
            field[0, z + 1, g * ROWS : (g + 1) * ROWS, :] = value
            total[z, g * ROWS : (g + 1) * ROWS, :] = value
            if g == 0:
                face_y[0, 0, z] = value[0:1, :]
            if g == GROUPS - 1:
                face_y[0, 1, z] = value[ROWS - 1 : ROWS, :]
            carry = packed(z, g, value[:, :LANES], value[:, LANES:], carry)
        return carry

    pack[0] = planes(start_body, zero_pack)
    for copy in halos[0]:
        copy.start()

    pair_c[1].wait_recv()

    def bx_body(z, carry):
        for g in range(GROUPS):
            value = assembled(slots_c.at[1], recv_c.at[1], z, g)
            bx[z, g * ROWS : (g + 1) * ROWS, :] = value
            carry = packed(z, g, value[:, :LANES], value[:, LANES:], carry)
        return carry

    rim_pack[...] = planes(bx_body, zero_pack)
    rims[0].start()
    pair_c[2].wait_recv()

    def by_body(z, carry):
        for g in range(GROUPS):
            value = assembled(slots_c.at[2], recv_c.at[2], z, g)
            by[z, g * ROWS : (g + 1) * ROWS, :] = value
            if g == 0:
                rim_face[z] = value[0:1, :]
        return carry

    planes(by_body)
    rims[1].start()

    def plain(slots, received, out):
        def body(z, carry):
            for g in range(GROUPS):
                out[z, g * ROWS : (g + 1) * ROWS, :] = assembled(slots, received, z, g)
            return carry

        planes(body)

    pair_c[3].wait_recv()
    plain(slots_c.at[3], recv_c.at[3], bz)
    rims[2].start()
    pair_c[0].wait_recv()
    plain(slots_c.at[0], recv_c.at[0], alpha)
    pair_f[1].wait_recv()
    plain(slots_f.at[1], recv_f.at[1], rhs)
    for copy in rims:
        copy.wait_recv()

    halves = (slice(0, LANES), slice(LANES, NX))
    group_rows = [slice(g * ROWS, (g + 1) * ROWS) for g in range(GROUPS)]
    rim_values = rim_x[...]

    def scale_body(z, carry):
        low_rolled = pltpu.roll(bx[z, :, :LANES], LANES - 1, 1)
        high_rolled = pltpu.roll(bx[z, :, LANES:], LANES - 1, 1)
        edge = jnp.concatenate(
            [pltpu.roll(rim_values, 126 - 2 * (z * GROUPS + g), 1) for g in range(GROUPS)], axis=0
        )
        upper_x = (jnp.where(last_lane, high_rolled, low_rolled), jnp.where(last_lane, edge, high_rolled))
        before = []
        after = []
        for j, part in enumerate(halves):
            here_y = by[z, :, part]
            upper_y = jnp.where(
                end_row, jnp.broadcast_to(rim_y[z, :, part], (NY, LANES)), pltpu.roll(here_y, NY - 1, 0)
            )
            faces = [bx[z, :, part], upper_x[j], here_y, upper_y, bz[z, :, part], bz[z + 1, :, part]]
            centre = alpha[z, :, part]
            for face in faces:
                centre = centre + face
            inverse = 1.0 / centre
            diag[z, :, part] = centre
            scaled[z, :, part] = inverse * rhs[z, :, part]
            weights = [inverse * face for face in faces]
            before.append(weights[0])
            after.append(weights[1])
            if j == 0:
                weights[0] = jnp.where(first_lane, 0.0, weights[0])
            else:
                weights[1] = jnp.where(last_lane, 0.0, weights[1])
            edge_y[0, z, :, part] = jnp.where(row8 == 0, weights[2][:ROWS], 0.0)
            edge_y[1, z, :, part] = jnp.where(row8 == ROWS - 1, weights[3][NY - ROWS :], 0.0)
            weights[2] = jnp.where(row == 0, 0.0, weights[2])
            weights[3] = jnp.where(end_row, 0.0, weights[3])
            for i, weight in enumerate(weights):
                near[i, z, :, part] = weight
        for g, rows in enumerate(group_rows):
            carry = packed(z, g, before[0][rows], after[1][rows], carry)
        return carry

    edge_x[...] = planes(scale_body, zero_pack)

    def inner(k, z, first, last):
        low, high = field[k, z + 1, :, :LANES], field[k, z + 1, :, LANES:]
        low_after, high_after = pltpu.roll(low, LANES - 1, 1), pltpu.roll(high, LANES - 1, 1)
        low_before, high_before = pltpu.roll(low, 1, 1), pltpu.roll(high, 1, 1)
        x_before = (low_before, jnp.where(first_lane, low_before, high_before))
        x_after = (jnp.where(last_lane, high_after, low_after), high_after)
        for j, part in enumerate(halves):
            here = (low, high)[j]
            value = scaled[z, :, part] - here
            value = value + near[0, z, :, part] * x_before[j] + near[1, z, :, part] * x_after[j]
            value = value + near[2, z, :, part] * pltpu.roll(here, 1, 0)
            value = value + near[3, z, :, part] * pltpu.roll(here, NY - 1, 0)
            if not first:
                value = value + near[4, z, :, part] * field[k, z, :, part]
            if not last:
                value = value + near[5, z, :, part] * field[k, z + 2, :, part]
            scaled[z, :, part] = value

    def outer(k, z, first, last, sides, carry):
        fresh = [[], []]
        for g, rows in enumerate(group_rows):
            moved = pltpu.roll(sides, LANES - 1 - 2 * (z * GROUPS + g), 1)
            for j, part in enumerate(halves):
                value = scaled[z, rows, part] + jnp.where(lane8 == (0, LANES - 1)[j], moved, 0.0)
                if g == 0:
                    value = value + edge_y[0, z, :, part] * jnp.broadcast_to(halo_y[k, 0, z, :, part], (ROWS, LANES))
                if g == GROUPS - 1:
                    value = value + edge_y[1, z, :, part] * jnp.broadcast_to(halo_y[k, 1, z, :, part], (ROWS, LANES))
                if first:
                    value = value + near[4, z, rows, part] * field[k, z, rows, part]
                if last:
                    value = value + near[5, z, rows, part] * field[k, z + 2, rows, part]
                if k == SWEEPS:
                    resid[z, rows, part] = diag[z, rows, part] * value
                    continue
                scaled[z, rows, part] = value
                step = SECOND[k] * value
                if k > 0:
                    step = step + FIRST[k] * field[k, z + 1, rows, part]
                field[k + 1, z + 1, rows, part] = step
                total[z, rows, part] = total[z, rows, part] + step
                if g == 0:
                    face_y[k + 1, 0, z, :, part] = step[0:1, :]
                if g == GROUPS - 1:
                    face_y[k + 1, 1, z, :, part] = step[ROWS - 1 : ROWS, :]
                fresh[j].append(step)
            if k < SWEEPS:
                carry = packed(z, g, fresh[0][g], fresh[1][g], carry)
        return carry

    def apply(k):
        inner(k, 0, True, False)

        def inner_body(z, carry):
            inner(k, z, False, False)
            return carry

        planes(inner_body, 0, 1, NZ - 1)
        inner(k, NZ - 1, False, True)
        for copy in halos[k]:
            copy.wait_recv()
        from_low = pltpu.roll(halo_x[k, 0], 1, 1)
        from_high = pltpu.roll(halo_x[k, 1], LANES - 1, 1)
        sides = edge_x[...] * jnp.where(lane8 - 2 * spots == 1, from_low, from_high)
        carry = outer(k, 0, True, False, sides, zero_pack)
        carry = planes(lambda z, carry: outer(k, z, False, False, sides, carry), carry, 1, NZ - 1)
        return outer(k, NZ - 1, False, True, sides, carry)

    for k in range(SWEEPS):
        pack[k + 1] = apply(k)
        for copy in halos[k + 1]:
            copy.start()
    x_out = pltpu.make_async_copy(total, x_hbm, out_sem.at[0])
    x_out.start()
    apply(SWEEPS)
    r_out = pltpu.make_async_copy(resid, r_hbm, out_sem.at[1])
    r_out.start()
    for copy in pair_f + pair_c + rims:
        copy.wait_send()
    for copies in halos:
        for copy in copies:
            copy.wait_send()
    x_out.wait()
    r_out.wait()


def emit(x_ref, r_ref, x_out, r_out, sem):
    first = pltpu.make_async_copy(x_ref, x_out, sem.at[0])
    second = pltpu.make_async_copy(r_ref, r_out, sem.at[1])
    first.start()
    second.start()
    first.wait()
    second.wait()


def local(old_fields, old_coef, held_slabs):
    slots = old_fields.shape[1]
    fields = old_fields.reshape(2, slots, NZ, 2, ROWS, NX)
    coef = old_coef.reshape(4, slots, NZ, 2, ROWS, NX)
    brick = (NZ, NY, NX)
    rounds = SWEEPS + 1
    dma = pltpu.SemaphoreType.DMA
    anywhere = pl.BlockSpec(memory_space=pl.ANY)
    hbm = pl.BlockSpec(memory_space=pltpu.HBM)
    held = jnp.transpose(held_slabs, (1, 2, 0))
    results = pl.pallas_call(
        kernel,
        out_shape=(jax.ShapeDtypeStruct(brick, F32), jax.ShapeDtypeStruct(brick, F32)),
        in_specs=[hbm, hbm, hbm],
        out_specs=(anywhere, anywhere),
        scratch_shapes=[
            pltpu.VMEM((2, slots, NZ, 2, ROWS, NX), F32),
            pltpu.VMEM((4, slots, NZ, 2, ROWS, NX), BF16),
            pltpu.VMEM((2, NZ, GROUPS, ROWS, NX), F32),
            pltpu.VMEM((4, NZ, GROUPS, ROWS, NX), BF16),
            pltpu.VMEM((2, NZ, GROUPS, ROWS, NX), F32),
            pltpu.VMEM((4, NZ, GROUPS, ROWS, NX), BF16),
            pltpu.VMEM((rounds, NZ + 2, NY, NX), F32),
            pltpu.VMEM(brick, F32),
            pltpu.VMEM(brick, F32),
            pltpu.VMEM(brick, F32),
            pltpu.VMEM((NZ + 1, NY, NX), F32),
            pltpu.VMEM(brick, F32),
            pltpu.VMEM((6, NZ, NY, NX), F32),
            pltpu.VMEM((2, NZ, ROWS, NX), F32),
            pltpu.VMEM((ROWS, LANES), F32),
            pltpu.VMEM(brick, F32),
            pltpu.VMEM(brick, F32),
            pltpu.VMEM(brick, F32),
            pltpu.VMEM(brick, F32),
            pltpu.VMEM((rounds, ROWS, LANES), F32),
            pltpu.VMEM((rounds, 2, NZ, 1, NX), F32),
            pltpu.VMEM((rounds, 2, ROWS, LANES), F32),
            pltpu.VMEM((rounds, 2, NZ, 1, NX), F32),
            pltpu.VMEM((ROWS, LANES), F32),
            pltpu.VMEM((NZ, 1, NX), F32),
            pltpu.VMEM((ROWS, LANES), F32),
            pltpu.VMEM((NZ, 1, NX), F32),
            pltpu.SMEM((1, 1, slots), jnp.int32),
            dma((6,)),
            dma((1,)),
            dma((6,)),
            dma((6,)),
            dma((rounds, 6)),
            dma((rounds, 6)),
            dma((3,)),
            dma((3,)),
            dma((2,)),
        ],
        compiler_params=pltpu.CompilerParams(
            collective_id=0, has_side_effects=True, vmem_limit_bytes=55767040
        ),
        name="smooth",
    )(fields, coef, held)
    return pl.pallas_call(
        emit,
        out_shape=(jax.ShapeDtypeStruct(brick, F32), jax.ShapeDtypeStruct(brick, F32)),
        in_specs=[anywhere, anywhere],
        out_specs=(hbm, hbm),
        scratch_shapes=[dma((2,))],
        compiler_params=pltpu.CompilerParams(vmem_limit_bytes=1 << 20),
        name="emit",
    )(*results)


def solution(mesh):
    in_specs = (
        P(None, "gy", "gz", None, "gx"),
        P(None, "gy", "gz", None, "gx"),
        P("gy", "gz", "gx"),
    )
    out_specs = (P("gz", "gy", "gx"), P("gz", "gy", "gx"))
    return jax.shard_map(local, mesh=mesh, in_specs=in_specs, out_specs=out_specs, check_vma=False)
```

```python
import functools
import jax
import jax.numpy as jnp
from jax import lax
from jax.experimental import pallas as pl
from jax.experimental.pallas import tpu as pltpu
from jax.sharding import PartitionSpec as P

SWEEPS = 4
NZ = 16
NY = 24
NX = 256
ROWS = 8
LANES = 128
GROUPS = NY // ROWS
MESH = pl.DeviceIdType.MESH
F32 = jnp.float32
BF16 = jnp.bfloat16


def chebyshev_weights(count):
    low_bound = 0.25
    high_bound = 2.0
    centre_value = 0.5 * (high_bound + low_bound)
    half_width = 0.5 * (high_bound - low_bound)
    ratio_value = centre_value / half_width
    damping = 1.0 / ratio_value
    first_list = [0.0]
    second_list = [1.0 / centre_value]
    for step_index in range(1, count):
        damping_next = 1.0 / (2.0 * ratio_value - damping)
        first_list.append(damping_next * damping)
        second_list.append(2.0 * damping_next / half_width)
        damping = damping_next
    return first_list, second_list


FIRST, SECOND = chebyshev_weights(SWEEPS)


def ring(axis):
    count = lax.axis_size(axis)
    me = lax.axis_index(axis)
    low = {axis: lax.rem(me + count - 1, count)}
    high = {axis: lax.rem(me + 1, count)}
    return low, high


def kernel(
    fields_hbm, coef_hbm, held_hbm, x_hbm, r_hbm,
    slots_f, slots_c, send_f, send_c, recv_f, recv_c,
    field, alpha, bx, by, bz, rhs, near, edge_y, edge_x, diag, inverse_ref, scaled, total, resid,
    pack, face_y, halo_x, halo_y, rim_pack, rim_face, rim_x, rim_y, beta_pack,
    sent_z, got_z, sent_y, got_y, sent_x, got_x, sent_yz, got_yz, sent_q, got_xz, got_xy, held_ref,
    load_sem, held_sem, pair_send, pair_recv, halo_send, halo_recv, rim_send, rim_recv, out_sem,
    both_send, both_recv,
):
    group = lax.axis_index("gy")
    half = lax.rem(group, 2)
    first_slab = 3 * (group // 2)
    partner = {"gy": group + 1 - 2 * half}
    x_low, x_high = ring("gx")
    y_low, y_high = ring("gy")
    z_low, z_high = ring("gz")

    barrier = pltpu.get_barrier_semaphore()
    x_sides, y_sides, z_sides = (x_low, x_high), (y_low, y_high), (z_low, z_high)
    faces = [x_low, x_high, y_low, y_high, z_low, z_high]
    edges = [{**a, **b} for a in z_sides for b in y_sides]
    edges += [{**a, **b} for a in x_sides for b in z_sides]
    edges += [{**a, **b} for a in x_sides for b in y_sides]
    for neighbour in faces + edges:
        pl.semaphore_signal(barrier, inc=1, device_id=neighbour, device_id_type=MESH)

    load_held = pltpu.make_async_copy(held_hbm, held_ref, held_sem.at[0])
    loads_f = [pltpu.make_async_copy(fields_hbm.at[c], slots_f.at[c], load_sem.at[c]) for c in range(2)]
    loads_c = [pltpu.make_async_copy(coef_hbm.at[c], slots_c.at[c], load_sem.at[2 + c]) for c in range(4)]
    load_held.start()
    loads_f[0].start()
    for c in (1, 2, 3, 0):
        loads_c[c].start()
    loads_f[1].start()
    load_held.wait()

    id0 = held_ref[0, 0, 0]
    id1 = held_ref[0, 0, 1]
    mine = [first_slab + (3 * half + g) // 2 for g in range(GROUPS)]
    theirs = [first_slab + (3 * (1 - half) + g) // 2 for g in range(GROUPS)]
    my_part = [lax.rem(half + g, 2) for g in range(GROUPS)]
    their_part = [lax.rem(1 - half + g, 2) for g in range(GROUPS)]

    row8 = lax.broadcasted_iota(jnp.int32, (ROWS, LANES), 0)
    row = lax.broadcasted_iota(jnp.int32, (NY, LANES), 0)
    lane = lax.broadcasted_iota(jnp.int32, (NY, LANES), 1)
    lane8 = lax.broadcasted_iota(jnp.int32, (ROWS, LANES), 1)
    end_row = row == NY - 1
    first_lane = lane == 0
    last_lane = lane == LANES - 1
    spots = lane8 // 2

    def copy_to(source, target, send_sem, recv_sem, device):
        return pltpu.make_async_remote_copy(
            src_ref=source, dst_ref=target, send_sem=send_sem, recv_sem=recv_sem,
            device_id=device, device_id_type=MESH,
        )

    pair_f = [copy_to(send_f.at[c], recv_f.at[c], pair_send.at[c], pair_recv.at[c], partner) for c in range(2)]
    pair_c = [
        copy_to(send_c.at[c], recv_c.at[c], pair_send.at[2 + c], pair_recv.at[2 + c], partner) for c in range(4)
    ]

    def halo_copies(k):
        return [
            copy_to(field.at[k, 1], field.at[k, NZ + 1], halo_send.at[k, 4], halo_recv.at[k, 4], z_low),
            copy_to(field.at[k, NZ], field.at[k, 0], halo_send.at[k, 5], halo_recv.at[k, 5], z_high),
            copy_to(face_y.at[k, 0], halo_y.at[k, 1], halo_send.at[k, 2], halo_recv.at[k, 2], y_low),
            copy_to(face_y.at[k, 1], halo_y.at[k, 0], halo_send.at[k, 3], halo_recv.at[k, 3], y_high),
            copy_to(pack.at[k], halo_x.at[k, 1], halo_send.at[k, 0], halo_recv.at[k, 0], x_low),
            copy_to(pack.at[k], halo_x.at[k, 0], halo_send.at[k, 1], halo_recv.at[k, 1], x_high),
        ]

    first_halos = halo_copies(0)

    def edge_copies(r):
        copies = []
        for a in range(2):
            for b in range(2):
                copies.append((sent_q.at[r], got_xy.at[r, 1 - a, 1 - b], {**x_sides[a], **y_sides[b]}))
        for a in range(2):
            for b in range(2):
                copies.append((sent_q.at[r], got_xz.at[r, 1 - a, 1 - b], {**x_sides[a], **z_sides[b]}))
        for a in range(2):
            for b in range(2):
                copies.append((sent_yz.at[r, a, b], got_yz.at[r, 1 - a, 1 - b], {**z_sides[a], **y_sides[b]}))
        return [copy_to(m[0], m[1], both_send.at[r, i], both_recv.at[r, i], m[2]) for i, m in enumerate(copies)]

    def face_copies(r):
        count = 3 - r
        copies = [
            (sent_x.at[r, pl.ds(0, count)], got_x.at[r, 1 - a, pl.ds(0, count)], x_sides[a]) for a in range(2)
        ]
        copies += [
            (sent_y.at[r, a, pl.ds(0, count)], got_y.at[r, 1 - a, pl.ds(0, count)], y_sides[a]) for a in range(2)
        ]
        copies += [
            (sent_z.at[r, a, pl.ds(0, count)], got_z.at[r, 1 - a, pl.ds(0, count)], z_sides[a]) for a in range(2)
        ]
        return [
            copy_to(m[0], m[1], both_send.at[r, 12 + i], both_recv.at[r, 12 + i], m[2]) for i, m in enumerate(copies)
        ]
    rims = [
        copy_to(rim_pack, rim_x, rim_send.at[0], rim_recv.at[0], x_low),
        copy_to(rim_face, rim_y, rim_send.at[1], rim_recv.at[1], y_low),
        copy_to(bz.at[0], bz.at[NZ], rim_send.at[2], rim_recv.at[2], z_low),
    ]

    def planes(body, carry=0, first=0, last=NZ):
        return lax.fori_loop(first, last, body, carry, unroll=True)

    def prepare(slots, out):
        def body(z, carry):
            for g in range(GROUPS):
                out[z, g] = lax.select(id0 == theirs[g], slots[0, z, their_part[g]], slots[1, z, their_part[g]])
            return carry

        planes(body)

    def assembled(slots, received, z, g):
        return lax.select(
            id0 == mine[g],
            slots[0, z, my_part[g]],
            lax.select(id1 == mine[g], slots[1, z, my_part[g]], received[z, g]),
        ).astype(F32)

    def packed(z, g, tile_low, tile_high, carry):
        spot = z * GROUPS + g
        both = jnp.where(lane8 == 0, tile_low, tile_high)
        moved = pltpu.roll(both, 2 * spot + 1, 1)
        return jnp.where(spots == spot, moved, carry)

    loads_f[0].wait()
    prepare(slots_f.at[0], send_f.at[0])
    pl.semaphore_wait(barrier, len(faces) + len(edges))
    pair_f[0].start()
    for c in (1, 2, 3, 0):
        loads_c[c].wait()
        prepare(slots_c.at[c], send_c.at[c])
        pair_c[c].start()
    loads_f[1].wait()
    prepare(slots_f.at[1], send_f.at[1])
    pair_f[1].start()

    zero_pack = jnp.zeros((ROWS, LANES), F32)

    pair_f[0].wait_recv()

    def start_body(z, carry):
        for g in range(GROUPS):
            value = assembled(slots_f.at[0], recv_f.at[0], z, g)
            field[0, z + 1, g * ROWS : (g + 1) * ROWS, :] = value
            if g == 0:
                face_y[0, 0, z] = value[0:1, :]
            if g == GROUPS - 1:
                face_y[0, 1, z] = value[ROWS - 1 : ROWS, :]
            carry = packed(z, g, value[:, :LANES], value[:, LANES:], carry)
        return carry

    pack[0] = planes(start_body, zero_pack)
    for copy in first_halos:
        copy.start()

    pair_c[1].wait_recv()

    def bx_body(z, carry):
        for g in range(GROUPS):
            value = assembled(slots_c.at[1], recv_c.at[1], z, g)
            bx[z, g * ROWS : (g + 1) * ROWS, :] = value
            carry = packed(z, g, value[:, :LANES], value[:, LANES:], carry)
        return carry

    rim_pack[...] = planes(bx_body, zero_pack)
    rims[0].start()
    pair_c[2].wait_recv()

    def by_body(z, carry):
        for g in range(GROUPS):
            value = assembled(slots_c.at[2], recv_c.at[2], z, g)
            by[z, g * ROWS : (g + 1) * ROWS, :] = value
            if g == 0:
                rim_face[z] = value[0:1, :]
        return carry

    planes(by_body)
    rims[1].start()

    def plain(slots, received, out):
        def body(z, carry):
            for g in range(GROUPS):
                out[z, g * ROWS : (g + 1) * ROWS, :] = assembled(slots, received, z, g)
            return carry

        planes(body)

    pair_c[3].wait_recv()
    plain(slots_c.at[3], recv_c.at[3], bz)
    rims[2].start()
    pair_c[0].wait_recv()
    plain(slots_c.at[0], recv_c.at[0], alpha)
    pair_f[1].wait_recv()
    plain(slots_f.at[1], recv_f.at[1], rhs)
    for copy in rims:
        copy.wait_recv()

    halves = (slice(0, LANES), slice(LANES, NX))
    group_rows = [slice(g * ROWS, (g + 1) * ROWS) for g in range(GROUPS)]
    rim_values = rim_x[...]

    def scale_body(z, carry):
        low_rolled = pltpu.roll(bx[z, :, :LANES], LANES - 1, 1)
        high_rolled = pltpu.roll(bx[z, :, LANES:], LANES - 1, 1)
        edge = jnp.concatenate(
            [pltpu.roll(rim_values, 126 - 2 * (z * GROUPS + g), 1) for g in range(GROUPS)], axis=0
        )
        upper_x = (jnp.where(last_lane, high_rolled, low_rolled), jnp.where(last_lane, edge, high_rolled))
        before = []
        after = []
        inverses = []
        uppers = []
        for j, part in enumerate(halves):
            here_y = by[z, :, part]
            upper_y = jnp.where(
                end_row, jnp.broadcast_to(rim_y[z, :, part], (NY, LANES)), pltpu.roll(here_y, NY - 1, 0)
            )
            faces = [bx[z, :, part], upper_x[j], here_y, upper_y, bz[z, :, part], bz[z + 1, :, part]]
            centre = alpha[z, :, part]
            for face in faces:
                centre = centre + face
            inverse = 1.0 / centre
            inverses.append(inverse)
            inverse_ref[z, :, part] = inverse
            sent_y[0, 0, 2, z, :, part] = inverse[:1]
            sent_y[0, 1, 2, z, :, part] = inverse[NY - 1 :]
            uppers.append(upper_y[NY - ROWS :])
            diag[z, :, part] = centre
            scaled[z, :, part] = inverse * rhs[z, :, part]
            weights = [inverse * face for face in faces]
            before.append(weights[0])
            after.append(weights[1])
            if j == 0:
                weights[0] = jnp.where(first_lane, 0.0, weights[0])
            else:
                weights[1] = jnp.where(last_lane, 0.0, weights[1])
            edge_y[0, z, :, part] = jnp.where(row8 == 0, weights[2][:ROWS], 0.0)
            edge_y[1, z, :, part] = jnp.where(row8 == ROWS - 1, weights[3][NY - ROWS :], 0.0)
            weights[2] = jnp.where(row == 0, 0.0, weights[2])
            weights[3] = jnp.where(end_row, 0.0, weights[3])
            for i, weight in enumerate(weights):
                near[i, z, :, part] = weight
        edge_pack, inverse_pack, y_pack = carry
        for g, rows in enumerate(group_rows):
            edge_pack = packed(z, g, before[0][rows], after[1][rows], edge_pack)
            inverse_pack = packed(z, g, inverses[0][rows], inverses[1][rows], inverse_pack)
        y_pack = packed(z, 0, by[z, :ROWS, :LANES], by[z, :ROWS, LANES:], y_pack)
        y_pack = packed(z, GROUPS - 1, uppers[0], uppers[1], y_pack)
        return edge_pack, inverse_pack, y_pack

    edge_x[...], sent_x[0, 2], y_pack = planes(scale_body, (zero_pack, zero_pack, zero_pack))
    odd = lane8 - 2 * spots == 1
    spot_group = spots - GROUPS * (spots // GROUPS)
    low_rim = (spot_group == 0) & (row8 == 0)
    high_rim = (spot_group == GROUPS - 1) & (row8 == ROWS - 1)
    low_spots = spots < GROUPS
    high_spots = (spots >= GROUPS * (NZ - 1)) & (spots < GROUPS * NZ)
    z_pack = zero_pack
    for g, rows in enumerate(group_rows):
        z_pack = packed(0, g, bz[0, rows, :LANES], bz[0, rows, LANES:], z_pack)
        z_pack = packed(NZ - 1, g, bz[NZ, rows, :LANES], bz[NZ, rows, LANES:], z_pack)
    beta_pack[0] = jnp.where(odd, rim_pack[...], pltpu.roll(rim_values, LANES - 1, 1))
    beta_pack[1] = jnp.where(low_rim | high_rim, y_pack, 0.0)
    beta_pack[2] = z_pack
    sent_z[0, 0, 2] = inverse_ref[0]
    sent_z[0, 1, 2] = inverse_ref[NZ - 1]

    def swapped(value):
        return jnp.where(odd, pltpu.roll(value, 1, 1), pltpu.roll(value, LANES - 1, 1))

    def halo_z_of(k, side):
        return got_z.at[k // 2, side, 0] if k % 2 else field.at[k, side * (NZ + 1)]

    def halo_y_of(k, side):
        return got_y.at[k // 2, side, 0] if k % 2 else halo_y.at[k, side]

    def inner(k, z, first, last, carry):
        low, high = field[k, z + 1, :, :LANES], field[k, z + 1, :, LANES:]
        low_after, high_after = pltpu.roll(low, LANES - 1, 1), pltpu.roll(high, LANES - 1, 1)
        low_before, high_before = pltpu.roll(low, 1, 1), pltpu.roll(high, 1, 1)
        x_before = (low_before, jnp.where(first_lane, low_before, high_before))
        x_after = (jnp.where(last_lane, high_after, low_after), high_after)
        values = []
        for j, part in enumerate(halves):
            here = (low, high)[j]
            value = scaled[z, :, part] - here
            value = value + near[0, z, :, part] * x_before[j] + near[1, z, :, part] * x_after[j]
            value = value + near[2, z, :, part] * pltpu.roll(here, 1, 0)
            value = value + near[3, z, :, part] * pltpu.roll(here, NY - 1, 0)
            if not first:
                value = value + near[4, z, :, part] * field[k, z, :, part]
            if not last:
                value = value + near[5, z, :, part] * field[k, z + 2, :, part]
            scaled[z, :, part] = value
            values.append(value)
            if k % 2:
                ahead = SECOND[k] * value + FIRST[k] * here
                sent_y[k // 2, 0, 1, z, :, part] = ahead[:1]
                sent_y[k // 2, 1, 1, z, :, part] = ahead[NY - 1 :]
                if first:
                    sent_z[k // 2, 0, 1, :, part] = ahead
                if last:
                    sent_z[k // 2, 1, 1, :, part] = ahead
        if k % 2:
            for g, rows in enumerate(group_rows):
                carry = packed(z, g, values[0][rows], values[1][rows], carry)
        return carry

    def outer(k, z, first, last, sides, carry):
        fresh = [[], []]
        sending = k % 2 == 0 and k < SWEEPS
        for g, rows in enumerate(group_rows):
            moved = pltpu.roll(sides, LANES - 1 - 2 * (z * GROUPS + g), 1)
            for j, part in enumerate(halves):
                value = scaled[z, rows, part] + jnp.where(lane8 == (0, LANES - 1)[j], moved, 0.0)
                if g == 0:
                    value = value + edge_y[0, z, :, part] * jnp.broadcast_to(
                        halo_y_of(k, 0)[z, :, part], (ROWS, LANES)
                    )
                if g == GROUPS - 1:
                    value = value + edge_y[1, z, :, part] * jnp.broadcast_to(
                        halo_y_of(k, 1)[z, :, part], (ROWS, LANES)
                    )
                if first:
                    value = value + near[4, z, rows, part] * halo_z_of(k, 0)[rows, part]
                if last:
                    value = value + near[5, z, rows, part] * halo_z_of(k, 1)[rows, part]
                if k == SWEEPS:
                    resid[z, rows, part] = diag[z, rows, part] * value
                    continue
                scaled[z, rows, part] = value
                step = SECOND[k] * value
                if k > 0:
                    step = step + FIRST[k] * field[k, z + 1, rows, part]
                field[k + 1, z + 1, rows, part] = step
                if k == SWEEPS - 1:
                    total[z, rows, part] = total[z, rows, part] + step
                if not sending:
                    continue
                if first:
                    sent_z[k // 2, 0, 0, rows, part] = step
                if last:
                    sent_z[k // 2, 1, 0, rows, part] = step
                if g == 0:
                    sent_y[k // 2, 0, 0, z, :, part] = step[:1]
                if g == GROUPS - 1:
                    sent_y[k // 2, 1, 0, z, :, part] = step[ROWS - 1 :]
                fresh[j].append(step)
            if sending:
                carry = packed(z, g, fresh[0][g], fresh[1][g], carry)
        return carry

    def run_inner(k):
        carry = inner(k, 0, True, False, zero_pack)
        carry = planes(lambda z, carry: inner(k, z, False, False, carry), carry, 1, NZ - 1)
        return inner(k, NZ - 1, False, True, carry)

    def run_outer(k, x_halo):
        sides = edge_x[...] * swapped(x_halo)
        carry = outer(k, 0, True, False, sides, zero_pack)
        carry = planes(lambda z, carry: outer(k, z, False, False, sides, carry), carry, 1, NZ - 1)
        return outer(k, NZ - 1, False, True, sides, carry)

    def spread_low(source, spot):
        return pltpu.roll(source, (LANES - 2 * spot) % LANES, 1)

    def spread_high(source, spot):
        return pltpu.roll(source, 126 - 2 * spot, 1)

    def ahead_z(r, k, side):
        own = side * (NZ - 1)
        sender = NZ - 1 - own
        for j, part in enumerate(halves):
            value = bz[side * NZ, :, part] * field[k, own + 1, :, part]
            for b, at in ((0, 0), (1, NY - 1)):
                line = jnp.broadcast_to(got_yz[r, side, b, 0, :, part], (NY, LANES))
                value = value + jnp.where(row == at, line, 0.0)
            source = got_xz[r, j, side, 0]
            move = (spread_low, spread_high)[j]
            column = jnp.concatenate([move(source, sender * GROUPS + g) for g in range(GROUPS)], axis=0)
            value = value + jnp.where((first_lane, last_lane)[j], column, 0.0)
            value = got_z[r, side, 1, :, part] + SECOND[k] * got_z[0, side, 2, :, part] * value
            field[k + 1, side * (NZ + 1), :, part] = value

    def ahead_y(r, k, side):
        sender_group = (GROUPS - 1) * (1 - side)
        sender_row = (ROWS - 1) * (1 - side)
        face = (rim_face, rim_y)[side]
        sources = [got_xy[r, j, side, 0] for j in range(2)]
        for z in range(NZ):
            for j, part in enumerate(halves):
                value = face[z, :, part] * sent_y[r, side, 0, z, :, part]
                if z == 0:
                    value = value + got_yz[r, 0, side, 1, :, part]
                if z == NZ - 1:
                    value = value + got_yz[r, 1, side, 1, :, part]
                column = (spread_low, spread_high)[j](sources[j], z * GROUPS + sender_group)
                column = jnp.where(lane8 == (0, LANES - 1)[j], column, 0.0)
                value = value + column[sender_row : sender_row + 1]
                value = got_y[r, side, 1, z, :, part] + SECOND[k] * got_y[0, side, 2, z, :, part] * value
                halo_y[k + 1, side, z, :, part] = value

    def either(ref_low, ref_high):
        return jnp.where(odd, ref_high, ref_low)

    def ahead_x(r, k):
        value = swapped(sent_q[r, 0])
        below = either(got_xy[r, 0, 0, 1], got_xy[r, 1, 0, 1])
        above = either(got_xy[r, 0, 1, 1], got_xy[r, 1, 1, 1])
        shift = 2 * (GROUPS - 1)
        value = value + jnp.where(low_rim, pltpu.roll(pltpu.roll(below, 1, 0), LANES - shift, 1), 0.0)
        value = value + jnp.where(high_rim, pltpu.roll(pltpu.roll(above, ROWS - 1, 0), shift, 1), 0.0)
        below = either(got_xz[r, 0, 0, 2], got_xz[r, 1, 0, 2])
        above = either(got_xz[r, 0, 1, 2], got_xz[r, 1, 1, 2])
        shift = 2 * GROUPS * (NZ - 1)
        value = value + jnp.where(low_spots, pltpu.roll(below, LANES - shift, 1), 0.0)
        value = value + jnp.where(high_spots, pltpu.roll(above, shift, 1), 0.0)
        partial = either(got_x[r, 0, 1], got_x[r, 1, 1])
        return partial + SECOND[k] * either(got_x[0, 0, 2], got_x[0, 1, 2]) * value

    def apply_two(r):
        k = 2 * r + 1
        own = sent_x[r, 0]
        for i in range(3):
            sent_q[r, i] = beta_pack[i] * own
        for a in range(2):
            z = a * (NZ - 1)
            for b in range(2):
                line = sent_y[r, b, 0, z]
                at = b * (NY - 1)
                sent_yz[r, a, b, 0] = (rim_face, rim_y)[b][z] * line
                sent_yz[r, a, b, 1] = bz[a * NZ, at : at + 1, :] * line
        copies = edge_copies(r)
        for copy in copies:
            copy.start()
        sent_x[r, 1] = SECOND[k] * run_inner(k) + FIRST[k] * own
        more = face_copies(r)
        for copy in more:
            copy.start()

        def sum_body(z, carry):
            for part in halves:
                if r == 0:
                    total[z, :, part] = field[0, z + 1, :, part] + field[1, z + 1, :, part]
                else:
                    total[z, :, part] = (
                        total[z, :, part] + field[2, z + 1, :, part] + field[3, z + 1, :, part]
                    )
            return carry

        planes(sum_body)
        for copy in copies + more:
            copy.wait_recv()
        run_outer(k, either(got_x[r, 0, 0], got_x[r, 1, 0]))
        if k == SWEEPS - 1:
            x_out.start()
        x_halo = ahead_x(r, k)
        for side in range(2):
            ahead_z(r, k, side)
            ahead_y(r, k, side)
        run_inner(k + 1)
        return copies + more, run_outer(k + 1, x_halo)

    x_out = pltpu.make_async_copy(total, x_hbm, out_sem.at[0])
    run_inner(0)
    for copy in first_halos:
        copy.wait_recv()
    sent_x[0, 0] = run_outer(0, either(halo_x[0, 0], halo_x[0, 1]))
    first_copies, sent_x[1, 0] = apply_two(0)
    second_copies, unused = apply_two(1)
    r_out = pltpu.make_async_copy(resid, r_hbm, out_sem.at[1])
    r_out.start()
    for copy in pair_f + pair_c + rims + first_halos + first_copies + second_copies:
        copy.wait_send()
    x_out.wait()
    r_out.wait()


def emit(x_ref, r_ref, x_out, r_out, sem):
    first = pltpu.make_async_copy(x_ref, x_out, sem.at[0])
    second = pltpu.make_async_copy(r_ref, r_out, sem.at[1])
    first.start()
    second.start()
    first.wait()
    second.wait()


def local(old_fields, old_coef, held_slabs):
    slots = old_fields.shape[1]
    fields = old_fields.reshape(2, slots, NZ, 2, ROWS, NX)
    coef = old_coef.reshape(4, slots, NZ, 2, ROWS, NX)
    brick = (NZ, NY, NX)
    rounds = SWEEPS + 1
    dma = pltpu.SemaphoreType.DMA
    anywhere = pl.BlockSpec(memory_space=pl.ANY)
    hbm = pl.BlockSpec(memory_space=pltpu.HBM)
    held = pltpu.with_memory_space_constraint(jnp.transpose(held_slabs, (1, 2, 0)), pltpu.HBM)
    results = pl.pallas_call(
        kernel,
        out_shape=(jax.ShapeDtypeStruct(brick, F32), jax.ShapeDtypeStruct(brick, F32)),
        in_specs=[hbm, hbm, hbm],
        out_specs=(anywhere, anywhere),
        scratch_shapes=[
            pltpu.VMEM((2, slots, NZ, 2, ROWS, NX), F32),
            pltpu.VMEM((4, slots, NZ, 2, ROWS, NX), BF16),
            pltpu.VMEM((2, NZ, GROUPS, ROWS, NX), F32),
            pltpu.VMEM((4, NZ, GROUPS, ROWS, NX), BF16),
            pltpu.VMEM((2, NZ, GROUPS, ROWS, NX), F32),
            pltpu.VMEM((4, NZ, GROUPS, ROWS, NX), BF16),
            pltpu.VMEM((rounds, NZ + 2, NY, NX), F32),
            pltpu.VMEM(brick, F32),
            pltpu.VMEM(brick, F32),
            pltpu.VMEM(brick, F32),
            pltpu.VMEM((NZ + 1, NY, NX), F32),
            pltpu.VMEM(brick, F32),
            pltpu.VMEM((6, NZ, NY, NX), F32),
            pltpu.VMEM((2, NZ, ROWS, NX), F32),
            pltpu.VMEM((ROWS, LANES), F32),
            pltpu.VMEM(brick, F32),
            pltpu.VMEM(brick, F32),
            pltpu.VMEM(brick, F32),
            pltpu.VMEM(brick, F32),
            pltpu.VMEM(brick, F32),
            pltpu.VMEM((rounds, ROWS, LANES), F32),
            pltpu.VMEM((rounds, 2, NZ, 1, NX), F32),
            pltpu.VMEM((rounds, 2, ROWS, LANES), F32),
            pltpu.VMEM((rounds, 2, NZ, 1, NX), F32),
            pltpu.VMEM((ROWS, LANES), F32),
            pltpu.VMEM((NZ, 1, NX), F32),
            pltpu.VMEM((ROWS, LANES), F32),
            pltpu.VMEM((NZ, 1, NX), F32),
            pltpu.VMEM((3, ROWS, LANES), F32),
            pltpu.VMEM((2, 2, 3, NY, NX), F32),
            pltpu.VMEM((2, 2, 3, NY, NX), F32),
            pltpu.VMEM((2, 2, 3, NZ, 1, NX), F32),
            pltpu.VMEM((2, 2, 3, NZ, 1, NX), F32),
            pltpu.VMEM((2, 3, ROWS, LANES), F32),
            pltpu.VMEM((2, 2, 3, ROWS, LANES), F32),
            pltpu.VMEM((2, 2, 2, 2, 1, NX), F32),
            pltpu.VMEM((2, 2, 2, 2, 1, NX), F32),
            pltpu.VMEM((2, 3, ROWS, LANES), F32),
            pltpu.VMEM((2, 2, 2, 3, ROWS, LANES), F32),
            pltpu.VMEM((2, 2, 2, 3, ROWS, LANES), F32),
            pltpu.SMEM((1, 1, slots), jnp.int32),
            dma((6,)),
            dma((1,)),
            dma((6,)),
            dma((6,)),
            dma((rounds, 6)),
            dma((rounds, 6)),
            dma((3,)),
            dma((3,)),
            dma((2,)),
            dma((2, 18)),
            dma((2, 18)),
        ],
        compiler_params=pltpu.CompilerParams(
            collective_id=0, has_side_effects=True, vmem_limit_bytes=55767040
        ),
        name="smooth",
    )(fields, coef, held)
    return pl.pallas_call(
        emit,
        out_shape=(jax.ShapeDtypeStruct(brick, F32), jax.ShapeDtypeStruct(brick, F32)),
        in_specs=[anywhere, anywhere],
        out_specs=(hbm, hbm),
        scratch_shapes=[dma((2,))],
        compiler_params=pltpu.CompilerParams(vmem_limit_bytes=1 << 20),
        name="emit",
    )(*results)


def solution(mesh):
    in_specs = (
        P(None, "gy", "gz", None, "gx"),
        P(None, "gy", "gz", None, "gx"),
        P("gy", "gz", "gx"),
    )
    out_specs = (P("gz", "gy", "gx"), P("gz", "gy", "gx"))
    return jax.shard_map(local, mesh=mesh, in_specs=in_specs, out_specs=out_specs, check_vma=False)
```

```python
import functools
import jax
import jax.numpy as jnp
from jax import lax
from jax.experimental import pallas as pl
from jax.experimental.pallas import tpu as pltpu
from jax.sharding import PartitionSpec as P

SWEEPS = 4
NZ = 16
NY = 24
NX = 256
ROWS = 8
LANES = 128
GROUPS = NY // ROWS
MESH = pl.DeviceIdType.MESH
F32 = jnp.float32
BF16 = jnp.bfloat16


def chebyshev_weights(count):
    low_bound = 0.25
    high_bound = 2.0
    centre_value = 0.5 * (high_bound + low_bound)
    half_width = 0.5 * (high_bound - low_bound)
    ratio_value = centre_value / half_width
    damping = 1.0 / ratio_value
    first_list = [0.0]
    second_list = [1.0 / centre_value]
    for step_index in range(1, count):
        damping_next = 1.0 / (2.0 * ratio_value - damping)
        first_list.append(damping_next * damping)
        second_list.append(2.0 * damping_next / half_width)
        damping = damping_next
    return first_list, second_list


FIRST, SECOND = chebyshev_weights(SWEEPS)


def ring(axis):
    count = lax.axis_size(axis)
    me = lax.axis_index(axis)
    low = {axis: lax.rem(me + count - 1, count)}
    high = {axis: lax.rem(me + 1, count)}
    return low, high


def kernel(
    fields_hbm, coef_hbm, held_hbm, x_hbm, r_hbm,
    slots_f, slots_c, send_f, send_c, recv_f, recv_c,
    field, alpha, bx, by, bz, rhs, near, edge_y, edge_x, diag, scaled, total, resid,
    pack, face_y, halo_x, halo_y, rim_y, held_ref,
    part_x, part_y, part_z, part_p, inner_y, got_x, got_y, got_z, got_p,
    load_sem, held_sem, pair_send, pair_recv, halo_send, halo_recv, part_send, got_sem, out_sem,
):
    group = lax.axis_index("gy")
    half = lax.rem(group, 2)
    first_slab = 3 * (group // 2)
    partner = {"gy": group + 1 - 2 * half}
    x_low, x_high = ring("gx")
    y_low, y_high = ring("gy")
    z_low, z_high = ring("gz")

    barrier = pltpu.get_barrier_semaphore()
    devices = lax.axis_size("gy")
    pair = [{"gy": group - half}, {"gy": group - half + 1}]
    outer_first = lax.rem(group - half + devices + 4 * half - 2, devices)
    fans = [{**side, **member} for side in (x_low, x_high, z_low, z_high) for member in pair]
    callers = fans + [{"gy": outer_first}, {"gy": outer_first + 1}, partner]
    for neighbour in callers:
        pl.semaphore_signal(barrier, inc=1, device_id=neighbour, device_id_type=MESH)

    load_held = pltpu.make_async_copy(held_hbm, held_ref, held_sem.at[0])
    loads_f = [pltpu.make_async_copy(fields_hbm.at[c], slots_f.at[c], load_sem.at[c]) for c in range(2)]
    loads_c = [pltpu.make_async_copy(coef_hbm.at[c], slots_c.at[c], load_sem.at[2 + c]) for c in range(4)]
    load_held.start()
    loads_f[0].start()
    for c in (1, 2, 3, 0):
        loads_c[c].start()
    loads_f[1].start()
    load_held.wait()

    id0 = held_ref[0, 0, 0]
    id1 = held_ref[0, 0, 1]
    mine = [first_slab + (3 * half + g) // 2 for g in range(GROUPS)]
    theirs = [first_slab + (3 * (1 - half) + g) // 2 for g in range(GROUPS)]
    my_part = [lax.rem(half + g, 2) for g in range(GROUPS)]
    their_part = [lax.rem(1 - half + g, 2) for g in range(GROUPS)]

    row8 = lax.broadcasted_iota(jnp.int32, (ROWS, LANES), 0)
    row = lax.broadcasted_iota(jnp.int32, (NY, LANES), 0)
    lane = lax.broadcasted_iota(jnp.int32, (NY, LANES), 1)
    lane8 = lax.broadcasted_iota(jnp.int32, (ROWS, LANES), 1)
    end_row = row == NY - 1
    first_lane = lane == 0
    last_lane = lane == LANES - 1
    spots = lane8 // 2

    def copy_to(source, target, send_sem, recv_sem, device):
        return pltpu.make_async_remote_copy(
            src_ref=source, dst_ref=target, send_sem=send_sem, recv_sem=recv_sem,
            device_id=device, device_id_type=MESH,
        )

    pair_f = [copy_to(send_f.at[c], recv_f.at[c], pair_send.at[c], pair_recv.at[c], partner) for c in range(2)]
    pair_c = [
        copy_to(send_c.at[c], recv_c.at[c], pair_send.at[2 + c], pair_recv.at[2 + c], partner) for c in range(4)
    ]

    def halo_copies(k):
        return [
            copy_to(pack.at[k], halo_x.at[k, 1], halo_send.at[k, 0], halo_recv.at[k, 0], x_low),
            copy_to(pack.at[k], halo_x.at[k, 0], halo_send.at[k, 1], halo_recv.at[k, 1], x_high),
            copy_to(face_y.at[k, 0], halo_y.at[k, 1], halo_send.at[k, 2], halo_recv.at[k, 2], y_low),
            copy_to(face_y.at[k, 1], halo_y.at[k, 0], halo_send.at[k, 3], halo_recv.at[k, 3], y_high),
            copy_to(field.at[k, 1], field.at[k, NZ + 1], halo_send.at[k, 4], halo_recv.at[k, 4], z_low),
            copy_to(field.at[k, NZ], field.at[k, 0], halo_send.at[k, 5], halo_recv.at[k, 5], z_high),
        ]

    halos = [None] + [halo_copies(k) for k in range(1, SWEEPS + 1)]
    def part_copy(i, slot, source, target, device):
        return copy_to(source, target, part_send.at[i], got_sem.at[slot, half], device)

    parts = []
    for h, member in enumerate(pair):
        parts.append(part_copy(h, 1, part_x.at[h], got_x.at[1, half], {**x_low, **member}))
    for h, member in enumerate(pair):
        parts.append(part_copy(2 + h, 0, part_x.at[h], got_x.at[0, half], {**x_high, **member}))
    parts.append(part_copy(4, 4, part_y.at[0], got_y.at[half], {"gy": lax.rem(group - half + devices - 1, devices)}))
    parts.append(part_copy(5, 4, part_y.at[1], got_y.at[half], {"gy": lax.rem(group - half + 2, devices)}))
    for h, member in enumerate(pair):
        parts.append(part_copy(6 + h, 3, part_z.at[0, h], got_z.at[1, half], {**z_low, **member}))
    for h, member in enumerate(pair):
        parts.append(
            part_copy(8 + h, 2, part_z.at[1, h, pl.ds(0, 1)], got_z.at[0, half, pl.ds(0, 1)], {**z_high, **member})
        )
    parts.append(copy_to(part_p, got_p, part_send.at[10], pair_recv.at[6], partner))

    def planes(body, carry=0, first=0, last=NZ):
        return lax.fori_loop(first, last, body, carry, unroll=True)

    def prepare(slots, out):
        def body(z, carry):
            for g in range(GROUPS):
                out[z, g] = lax.select(id0 == theirs[g], slots[0, z, their_part[g]], slots[1, z, their_part[g]])
            return carry

        planes(body)

    def assembled(slots, received, z, g):
        return lax.select(
            id0 == mine[g],
            slots[0, z, my_part[g]],
            lax.select(id1 == mine[g], slots[1, z, my_part[g]], received[z, g]),
        ).astype(F32)

    def packed(z, g, tile_low, tile_high, carry):
        return packed_at(g * NZ + z, tile_low, tile_high, carry)

    def packed_at(spot, tile_low, tile_high, carry):
        both = jnp.where(lane8 == 0, tile_low, tile_high)
        moved = pltpu.roll(both, (2 * spot + 1) % LANES, 1)
        return jnp.where(spots == spot, moved, carry)

    region = [first_slab + g // 2 for g in range(2 * GROUPS)]

    def chosen(slab, first, second):
        zero = jnp.zeros(first.shape, first.dtype)
        return lax.select(id0 == slab, first, lax.select(id1 == slab, second, zero)).astype(F32)

    def part_columns(slots, index):
        def body(z, carry):
            for slot in range(2):
                for p in range(2):
                    value = slots[slot, z, p].astype(F32)
                    carry = packed_at((2 * slot + p) * NZ + z, value[:, :LANES], value[:, LANES:], carry)
            return carry

        whole = planes(body, jnp.zeros((ROWS, LANES), F32))
        segment = LANES // 4
        for h in range(2):
            value = jnp.zeros((ROWS, LANES), F32)
            for g in range(GROUPS):
                p = (GROUPS * h + g) % 2
                moved = [pltpu.roll(whole, segment * (g - 2 * slot - p) % LANES, 1) for slot in range(2)]
                value = jnp.where(lane8 // segment == g, chosen(region[GROUPS * h + g], *moved), value)
            part_x[h, index] = value

    def part_planes(slots, side, index):
        z = side * (NZ - 1)
        for g in range(2 * GROUPS):
            rows = slice((g % GROUPS) * ROWS, (g % GROUPS + 1) * ROWS)
            part_z[side, g // GROUPS, index, rows, :] = chosen(region[g], slots[0, z, g % 2], slots[1, z, g % 2])

    def part_rows(slots, index):
        middle = first_slab + 1

        def body(z, carry):
            part_y[0, index, z] = chosen(region[0], slots[0, z, 0, 0:1], slots[1, z, 0, 0:1])
            part_y[1, index, z] = chosen(region[5], slots[0, z, 1, ROWS - 1 : ROWS], slots[1, z, 1, ROWS - 1 : ROWS])
            upper = chosen(middle, slots[0, z, 1, 0:1], slots[1, z, 1, 0:1])
            lower = chosen(middle, slots[0, z, 0, ROWS - 1 : ROWS], slots[1, z, 0, ROWS - 1 : ROWS])
            part_p[index, z] = lax.select(half == 0, lower, upper)
            inner_y[index, z] = lax.select(half == 0, upper, lower)
            return carry

        planes(body)

    def plain(slots, received, out, shift=0):
        def body(z, carry):
            for g in range(GROUPS):
                out[z + shift, g * ROWS : (g + 1) * ROWS, :] = assembled(slots, received, z, g)
            return carry

        planes(body)

    loads_f[0].wait()
    prepare(slots_f.at[0], send_f.at[0])
    part_columns(slots_f.at[0], 0)
    part_rows(slots_f.at[0], 0)
    part_planes(slots_f.at[0], 0, 0)
    part_planes(slots_f.at[0], 1, 0)
    loads_c[1].wait()
    part_columns(slots_c.at[1], 1)
    loads_c[2].wait()
    part_rows(slots_c.at[2], 1)
    loads_c[3].wait()
    part_planes(slots_c.at[3], 0, 1)
    pl.semaphore_wait(barrier, len(callers))
    for copy in parts[:10]:
        copy.start()
    pair_f[0].start()
    for c in (1, 2, 3, 0):
        if c == 0:
            parts[10].start()
            loads_c[c].wait()
        prepare(slots_c.at[c], send_c.at[c])
        pair_c[c].start()
    loads_f[1].wait()
    prepare(slots_f.at[1], send_f.at[1])
    pair_f[1].start()

    zero_pack = jnp.zeros((ROWS, LANES), F32)

    pair_f[0].wait_recv()
    plain(slots_f.at[0], recv_f.at[0], field.at[0], 1)

    def sum_body(z, carry):
        total[z] = field[0, z + 1]
        return carry

    planes(sum_body)
    pair_c[1].wait_recv()
    plain(slots_c.at[1], recv_c.at[1], bx)
    pair_c[2].wait_recv()
    plain(slots_c.at[2], recv_c.at[2], by)
    pair_c[3].wait_recv()
    plain(slots_c.at[3], recv_c.at[3], bz)
    pair_c[0].wait_recv()
    plain(slots_c.at[0], recv_c.at[0], alpha)
    pair_f[1].wait_recv()
    plain(slots_f.at[1], recv_f.at[1], rhs)
    parts[10].wait_recv()
    for member in range(2):
        for side in range(2):
            copy_to(part_x.at[0], got_x.at[side, member], part_send.at[0], got_sem.at[side, member], x_low).wait_recv()
            count = pl.ds(0, 1 + side)
            source, target = part_z.at[0, 0, count], got_z.at[side, member, count]
            copy_to(source, target, part_send.at[0], got_sem.at[2 + side, member], z_low).wait_recv()
        copy_to(part_y.at[0], got_y.at[member], part_send.at[0], got_sem.at[4, member], y_low).wait_recv()

    for side in range(2):
        halo_x[0, side] = got_x[side, 0, 0] + got_x[side, 1, 0]
        field[0, side * (NZ + 1)] = got_z[side, 0, 0] + got_z[side, 1, 0]
    bz[NZ] = got_z[1, 0, 1] + got_z[1, 1, 1]
    rim_values = got_x[1, 0, 1] + got_x[1, 1, 1]

    def row_body(z, carry):
        halo_y[0, half, z] = got_y[0, 0, z] + got_y[1, 0, z]
        halo_y[0, 1 - half, z] = inner_y[0, z] + got_p[0, z]
        rim_y[z] = lax.select(half == 0, inner_y[1, z] + got_p[1, z], got_y[0, 1, z] + got_y[1, 1, z])
        return carry

    planes(row_body)

    halves = (slice(0, LANES), slice(LANES, NX))
    group_rows = [slice(g * ROWS, (g + 1) * ROWS) for g in range(GROUPS)]

    def scale_body(z, carry):
        low_rolled = pltpu.roll(bx[z, :, :LANES], LANES - 1, 1)
        high_rolled = pltpu.roll(bx[z, :, LANES:], LANES - 1, 1)
        edge = jnp.concatenate(
            [pltpu.roll(rim_values, 126 - 2 * (g * NZ + z), 1) for g in range(GROUPS)], axis=0
        )
        upper_x = (jnp.where(last_lane, high_rolled, low_rolled), jnp.where(last_lane, edge, high_rolled))
        before = []
        after = []
        for j, part in enumerate(halves):
            here_y = by[z, :, part]
            upper_y = jnp.where(
                end_row, jnp.broadcast_to(rim_y[z, :, part], (NY, LANES)), pltpu.roll(here_y, NY - 1, 0)
            )
            faces = [bx[z, :, part], upper_x[j], here_y, upper_y, bz[z, :, part], bz[z + 1, :, part]]
            centre = alpha[z, :, part]
            for face in faces:
                centre = centre + face
            inverse = 1.0 / centre
            diag[z, :, part] = centre
            scaled[z, :, part] = inverse * rhs[z, :, part]
            weights = [inverse * face for face in faces]
            before.append(weights[0])
            after.append(weights[1])
            if j == 0:
                weights[0] = jnp.where(first_lane, 0.0, weights[0])
            else:
                weights[1] = jnp.where(last_lane, 0.0, weights[1])
            edge_y[0, z, :, part] = jnp.where(row8 == 0, weights[2][:ROWS], 0.0)
            edge_y[1, z, :, part] = jnp.where(row8 == ROWS - 1, weights[3][NY - ROWS :], 0.0)
            weights[2] = jnp.where(row == 0, 0.0, weights[2])
            weights[3] = jnp.where(end_row, 0.0, weights[3])
            for i, weight in enumerate(weights):
                near[i, z, :, part] = weight
        for g, rows in enumerate(group_rows):
            carry = packed(z, g, before[0][rows], after[1][rows], carry)
        return carry

    edge_x[...] = planes(scale_body, zero_pack)

    def inner(k, z, first, last):
        low, high = field[k, z + 1, :, :LANES], field[k, z + 1, :, LANES:]
        low_after, high_after = pltpu.roll(low, LANES - 1, 1), pltpu.roll(high, LANES - 1, 1)
        low_before, high_before = pltpu.roll(low, 1, 1), pltpu.roll(high, 1, 1)
        x_before = (low_before, jnp.where(first_lane, low_before, high_before))
        x_after = (jnp.where(last_lane, high_after, low_after), high_after)
        for j, part in enumerate(halves):
            here = (low, high)[j]
            value = scaled[z, :, part] - here
            value = value + near[0, z, :, part] * x_before[j] + near[1, z, :, part] * x_after[j]
            value = value + near[2, z, :, part] * pltpu.roll(here, 1, 0)
            value = value + near[3, z, :, part] * pltpu.roll(here, NY - 1, 0)
            if not first:
                value = value + near[4, z, :, part] * field[k, z, :, part]
            if not last:
                value = value + near[5, z, :, part] * field[k, z + 2, :, part]
            scaled[z, :, part] = value

    def outer(k, z, first, last, sides, carry):
        fresh = [[], []]
        for g, rows in enumerate(group_rows):
            moved = pltpu.roll(sides, LANES - 1 - 2 * (g * NZ + z), 1)
            for j, part in enumerate(halves):
                value = scaled[z, rows, part] + jnp.where(lane8 == (0, LANES - 1)[j], moved, 0.0)
                if g == 0:
                    value = value + edge_y[0, z, :, part] * jnp.broadcast_to(halo_y[k, 0, z, :, part], (ROWS, LANES))
                if g == GROUPS - 1:
                    value = value + edge_y[1, z, :, part] * jnp.broadcast_to(halo_y[k, 1, z, :, part], (ROWS, LANES))
                if first:
                    value = value + near[4, z, rows, part] * field[k, z, rows, part]
                if last:
                    value = value + near[5, z, rows, part] * field[k, z + 2, rows, part]
                if k == SWEEPS:
                    resid[z, rows, part] = diag[z, rows, part] * value
                    continue
                scaled[z, rows, part] = value
                step = SECOND[k] * value
                if k > 0:
                    step = step + FIRST[k] * field[k, z + 1, rows, part]
                field[k + 1, z + 1, rows, part] = step
                total[z, rows, part] = total[z, rows, part] + step
                if g == 0:
                    face_y[k + 1, 0, z, :, part] = step[0:1, :]
                if g == GROUPS - 1:
                    face_y[k + 1, 1, z, :, part] = step[ROWS - 1 : ROWS, :]
                fresh[j].append(step)
            if k < SWEEPS:
                carry = packed(z, g, fresh[0][g], fresh[1][g], carry)
        return carry

    def apply(k):
        inner(k, 0, True, False)

        def inner_body(z, carry):
            inner(k, z, False, False)
            return carry

        planes(inner_body, 0, 1, NZ - 1)
        inner(k, NZ - 1, False, True)
        if k > 0:
            for copy in halos[k]:
                copy.wait_recv()
        from_low = pltpu.roll(halo_x[k, 0], 1, 1)
        from_high = pltpu.roll(halo_x[k, 1], LANES - 1, 1)
        sides = edge_x[...] * jnp.where(lane8 - 2 * spots == 1, from_low, from_high)
        carry = outer(k, 0, True, False, sides, zero_pack)
        carry = planes(lambda z, carry: outer(k, z, False, False, sides, carry), carry, 1, NZ - 1)
        return outer(k, NZ - 1, False, True, sides, carry)

    for k in range(SWEEPS):
        pack[k + 1] = apply(k)
        for copy in halos[k + 1]:
            copy.start()
    x_out = pltpu.make_async_copy(total, x_hbm, out_sem.at[0])
    x_out.start()
    apply(SWEEPS)
    r_out = pltpu.make_async_copy(resid, r_hbm, out_sem.at[1])
    r_out.start()
    for copy in pair_f + pair_c + parts:
        copy.wait_send()
    for copies in halos[1:]:
        for copy in copies:
            copy.wait_send()
    x_out.wait()
    r_out.wait()


def emit(x_ref, r_ref, x_out, r_out, sem):
    first = pltpu.make_async_copy(x_ref, x_out, sem.at[0])
    second = pltpu.make_async_copy(r_ref, r_out, sem.at[1])
    first.start()
    second.start()
    first.wait()
    second.wait()


def local(old_fields, old_coef, held_slabs):
    slots = old_fields.shape[1]
    fields = old_fields.reshape(2, slots, NZ, 2, ROWS, NX)
    coef = old_coef.reshape(4, slots, NZ, 2, ROWS, NX)
    brick = (NZ, NY, NX)
    rounds = SWEEPS + 1
    dma = pltpu.SemaphoreType.DMA
    anywhere = pl.BlockSpec(memory_space=pl.ANY)
    hbm = pl.BlockSpec(memory_space=pltpu.HBM)
    held = pltpu.with_memory_space_constraint(jnp.transpose(held_slabs, (1, 2, 0)), pltpu.HBM)
    results = pl.pallas_call(
        kernel,
        out_shape=(jax.ShapeDtypeStruct(brick, F32), jax.ShapeDtypeStruct(brick, F32)),
        in_specs=[hbm, hbm, hbm],
        out_specs=(anywhere, anywhere),
        scratch_shapes=[
            pltpu.VMEM((2, slots, NZ, 2, ROWS, NX), F32),
            pltpu.VMEM((4, slots, NZ, 2, ROWS, NX), BF16),
            pltpu.VMEM((2, NZ, GROUPS, ROWS, NX), F32),
            pltpu.VMEM((4, NZ, GROUPS, ROWS, NX), BF16),
            pltpu.VMEM((2, NZ, GROUPS, ROWS, NX), F32),
            pltpu.VMEM((4, NZ, GROUPS, ROWS, NX), BF16),
            pltpu.VMEM((rounds, NZ + 2, NY, NX), F32),
            pltpu.VMEM(brick, F32),
            pltpu.VMEM(brick, F32),
            pltpu.VMEM(brick, F32),
            pltpu.VMEM((NZ + 1, NY, NX), F32),
            pltpu.VMEM(brick, F32),
            pltpu.VMEM((6, NZ, NY, NX), F32),
            pltpu.VMEM((2, NZ, ROWS, NX), F32),
            pltpu.VMEM((ROWS, LANES), F32),
            pltpu.VMEM(brick, F32),
            pltpu.VMEM(brick, F32),
            pltpu.VMEM(brick, F32),
            pltpu.VMEM(brick, F32),
            pltpu.VMEM((rounds, ROWS, LANES), F32),
            pltpu.VMEM((rounds, 2, NZ, 1, NX), F32),
            pltpu.VMEM((rounds, 2, ROWS, LANES), F32),
            pltpu.VMEM((rounds, 2, NZ, 1, NX), F32),
            pltpu.VMEM((NZ, 1, NX), F32),
            pltpu.SMEM((1, 1, slots), jnp.int32),
            pltpu.VMEM((2, 2, ROWS, LANES), F32),
            pltpu.VMEM((2, 2, NZ, 1, NX), F32),
            pltpu.VMEM((2, 2, 2, NY, NX), F32),
            pltpu.VMEM((2, NZ, 1, NX), F32),
            pltpu.VMEM((2, NZ, 1, NX), F32),
            pltpu.VMEM((2, 2, 2, ROWS, LANES), F32),
            pltpu.VMEM((2, 2, NZ, 1, NX), F32),
            pltpu.VMEM((2, 2, 2, NY, NX), F32),
            pltpu.VMEM((2, NZ, 1, NX), F32),
            dma((6,)),
            dma((1,)),
            dma((6,)),
            dma((7,)),
            dma((rounds, 6)),
            dma((rounds, 6)),
            dma((11,)),
            dma((5, 2)),
            dma((2,)),
        ],
        compiler_params=pltpu.CompilerParams(
            collective_id=0, has_side_effects=True, vmem_limit_bytes=55767040
        ),
        name="smooth",
    )(fields, coef, held)
    return pl.pallas_call(
        emit,
        out_shape=(jax.ShapeDtypeStruct(brick, F32), jax.ShapeDtypeStruct(brick, F32)),
        in_specs=[anywhere, anywhere],
        out_specs=(hbm, hbm),
        scratch_shapes=[dma((2,))],
        compiler_params=pltpu.CompilerParams(vmem_limit_bytes=1 << 20),
        name="emit",
    )(*results)


def solution(mesh):
    in_specs = (
        P(None, "gy", "gz", None, "gx"),
        P(None, "gy", "gz", None, "gx"),
        P("gy", "gz", "gx"),
    )
    out_specs = (P("gz", "gy", "gx"), P("gz", "gy", "gx"))
    return jax.shard_map(local, mesh=mesh, in_specs=in_specs, out_specs=out_specs, check_vma=False)
```

```python
import functools
import jax
import jax.numpy as jnp
from jax import lax
from jax.experimental import pallas as pl
from jax.experimental.pallas import tpu as pltpu
from jax.sharding import PartitionSpec as P

SWEEPS = 4
NZ = 16
NY = 24
NX = 256
ROWS = 8
LANES = 128
GROUPS = NY // ROWS
MESH = pl.DeviceIdType.MESH
F32 = jnp.float32
BF16 = jnp.bfloat16


def chebyshev_weights(count):
    low_bound = 0.25
    high_bound = 2.0
    centre_value = 0.5 * (high_bound + low_bound)
    half_width = 0.5 * (high_bound - low_bound)
    ratio_value = centre_value / half_width
    damping = 1.0 / ratio_value
    first_list = [0.0]
    second_list = [1.0 / centre_value]
    for step_index in range(1, count):
        damping_next = 1.0 / (2.0 * ratio_value - damping)
        first_list.append(damping_next * damping)
        second_list.append(2.0 * damping_next / half_width)
        damping = damping_next
    return first_list, second_list


FIRST, SECOND = chebyshev_weights(SWEEPS)


def ring(axis):
    count = lax.axis_size(axis)
    me = lax.axis_index(axis)
    low = {axis: lax.rem(me + count - 1, count)}
    high = {axis: lax.rem(me + 1, count)}
    return low, high


def kernel(
    fields_hbm, coef_hbm, held_hbm, x_hbm, r_hbm,
    slots_f, slots_c, send_f, send_c, recv_f, recv_c,
    field, alpha, bx, by, bz, rhs, near, edge_y, edge_x, diag, inverse_ref, scaled, total, resid,
    pack, face_y, halo_x, halo_y, rim_pack, rim_face, rim_x, rim_y, beta_pack,
    sent_z, got_z, sent_y, got_y, sent_x, got_x, sent_yz, got_yz, sent_q, got_xz, got_xy, line_weight, line_fix, pack_weight, held_ref,
    load_sem, held_sem, pair_send, pair_recv, halo_send, halo_recv, rim_send, rim_recv, out_sem,
    both_send, both_recv,
):
    group = lax.axis_index("gy")
    half = lax.rem(group, 2)
    first_slab = 3 * (group // 2)
    partner = {"gy": group + 1 - 2 * half}
    x_low, x_high = ring("gx")
    y_low, y_high = ring("gy")
    z_low, z_high = ring("gz")

    barrier = pltpu.get_barrier_semaphore()
    x_sides, y_sides, z_sides = (x_low, x_high), (y_low, y_high), (z_low, z_high)
    faces = [x_low, x_high, y_low, y_high, z_low, z_high]
    edges = [{**a, **b} for a in z_sides for b in y_sides]
    edges += [{**a, **b} for a in x_sides for b in z_sides]
    edges += [{**a, **b} for a in x_sides for b in y_sides]
    for neighbour in faces + edges:
        pl.semaphore_signal(barrier, inc=1, device_id=neighbour, device_id_type=MESH)

    load_held = pltpu.make_async_copy(held_hbm, held_ref, held_sem.at[0])
    loads_f = [pltpu.make_async_copy(fields_hbm.at[c], slots_f.at[c], load_sem.at[c]) for c in range(2)]
    loads_c = [pltpu.make_async_copy(coef_hbm.at[c], slots_c.at[c], load_sem.at[2 + c]) for c in range(4)]
    load_held.start()
    loads_f[0].start()
    for c in (1, 2, 3, 0):
        loads_c[c].start()
    loads_f[1].start()
    load_held.wait()

    id0 = held_ref[0, 0, 0]
    id1 = held_ref[0, 0, 1]
    mine = [first_slab + (3 * half + g) // 2 for g in range(GROUPS)]
    theirs = [first_slab + (3 * (1 - half) + g) // 2 for g in range(GROUPS)]
    my_part = [lax.rem(half + g, 2) for g in range(GROUPS)]
    their_part = [lax.rem(1 - half + g, 2) for g in range(GROUPS)]

    row8 = lax.broadcasted_iota(jnp.int32, (ROWS, LANES), 0)
    row = lax.broadcasted_iota(jnp.int32, (NY, LANES), 0)
    lane = lax.broadcasted_iota(jnp.int32, (NY, LANES), 1)
    lane8 = lax.broadcasted_iota(jnp.int32, (ROWS, LANES), 1)
    end_row = row == NY - 1
    first_lane = lane == 0
    last_lane = lane == LANES - 1
    spots = lane8 // 2

    def copy_to(source, target, send_sem, recv_sem, device):
        return pltpu.make_async_remote_copy(
            src_ref=source, dst_ref=target, send_sem=send_sem, recv_sem=recv_sem,
            device_id=device, device_id_type=MESH,
        )

    pair_f = [copy_to(send_f.at[c], recv_f.at[c], pair_send.at[c], pair_recv.at[c], partner) for c in range(2)]
    pair_c = [
        copy_to(send_c.at[c], recv_c.at[c], pair_send.at[2 + c], pair_recv.at[2 + c], partner) for c in range(4)
    ]

    def halo_copies(k):
        return [
            copy_to(pack.at[k], halo_x.at[k, 1], halo_send.at[k, 0], halo_recv.at[k, 0], x_low),
            copy_to(pack.at[k], halo_x.at[k, 0], halo_send.at[k, 1], halo_recv.at[k, 1], x_high),
            copy_to(face_y.at[k, 0], halo_y.at[k, 1], halo_send.at[k, 2], halo_recv.at[k, 2], y_low),
            copy_to(face_y.at[k, 1], halo_y.at[k, 0], halo_send.at[k, 3], halo_recv.at[k, 3], y_high),
            copy_to(field.at[k, 1], field.at[k, NZ + 1], halo_send.at[k, 4], halo_recv.at[k, 4], z_low),
            copy_to(field.at[k, NZ], field.at[k, 0], halo_send.at[k, 5], halo_recv.at[k, 5], z_high),
        ]

    first_halos = halo_copies(0)

    def numbered(r, first, moves):
        return [
            copy_to(source, target, both_send.at[r, first + i], both_recv.at[r, first + i], device)
            for i, (source, target, device) in enumerate(moves)
        ]

    def edge_copies(r):
        moves = []
        for a in range(2):
            for b in range(2):
                device = {**x_sides[a], **y_sides[b]}
                line = pl.ds(b * (ROWS - 1), 1)
                moves.append((sent_q.at[r, pl.ds(0, 2), line], got_xy.at[r, 1 - a, 1 - b, pl.ds(0, 2), line], device))
        for a in range(2):
            for b in range(2):
                device = {**x_sides[a], **z_sides[b]}
                moves.append((sent_q.at[r, 2], got_xz.at[r, 1 - a, 1 - b], device))
        for a in range(2):
            for b in range(2):
                moves.append((sent_yz.at[r, a, b], got_yz.at[r, 1 - a, 1 - b], {**z_sides[a], **y_sides[b]}))
        return numbered(r, 12, moves)

    def face_copies(r, first, part):
        moves = [(sent_x.at[r, part], got_x.at[r, 1 - a, part], x_sides[a]) for a in range(2)]
        moves += [(sent_y.at[r, a, part], got_y.at[r, 1 - a, part], y_sides[a]) for a in range(2)]
        moves += [(sent_z.at[r, a, part], got_z.at[r, 1 - a, part], z_sides[a]) for a in range(2)]
        return numbered(r, first, moves)

    rims = [
        copy_to(rim_pack, rim_x, rim_send.at[0], rim_recv.at[0], x_low),
        copy_to(rim_face, rim_y, rim_send.at[1], rim_recv.at[1], y_low),
        copy_to(bz.at[0], bz.at[NZ], rim_send.at[2], rim_recv.at[2], z_low),
    ]

    def planes(body, carry=0, first=0, last=NZ):
        return lax.fori_loop(first, last, body, carry, unroll=True)

    def prepare(slots, out):
        def body(z, carry):
            for g in range(GROUPS):
                out[z, g] = lax.select(id0 == theirs[g], slots[0, z, their_part[g]], slots[1, z, their_part[g]])
            return carry

        planes(body)

    def assembled(slots, received, z, g):
        return lax.select(
            id0 == mine[g],
            slots[0, z, my_part[g]],
            lax.select(id1 == mine[g], slots[1, z, my_part[g]], received[z, g]),
        ).astype(F32)

    def packed(z, g, tile_low, tile_high, carry):
        spot = z * GROUPS + g
        both = jnp.where(lane8 == 0, tile_low, tile_high)
        moved = pltpu.roll(both, 2 * spot + 1, 1)
        return jnp.where(spots == spot, moved, carry)

    loads_f[0].wait()
    prepare(slots_f.at[0], send_f.at[0])
    pl.semaphore_wait(barrier, len(faces) + len(edges))
    pair_f[0].start()
    for c in (1, 2, 3, 0):
        loads_c[c].wait()
        prepare(slots_c.at[c], send_c.at[c])
        pair_c[c].start()
    loads_f[1].wait()
    prepare(slots_f.at[1], send_f.at[1])
    pair_f[1].start()

    zero_pack = jnp.zeros((ROWS, LANES), F32)

    pair_f[0].wait_recv()

    def start_body(z, carry):
        for g in range(GROUPS):
            value = assembled(slots_f.at[0], recv_f.at[0], z, g)
            field[0, z + 1, g * ROWS : (g + 1) * ROWS, :] = value
            if g == 0:
                face_y[0, 0, z] = value[0:1, :]
            if g == GROUPS - 1:
                face_y[0, 1, z] = value[ROWS - 1 : ROWS, :]
            carry = packed(z, g, value[:, :LANES], value[:, LANES:], carry)
        return carry

    pack[0] = planes(start_body, zero_pack)
    for copy in first_halos:
        copy.start()

    pair_c[1].wait_recv()

    def bx_body(z, carry):
        for g in range(GROUPS):
            value = assembled(slots_c.at[1], recv_c.at[1], z, g)
            bx[z, g * ROWS : (g + 1) * ROWS, :] = value
            carry = packed(z, g, value[:, :LANES], value[:, LANES:], carry)
        return carry

    rim_pack[...] = planes(bx_body, zero_pack)
    rims[0].start()
    pair_c[2].wait_recv()

    def by_body(z, carry):
        for g in range(GROUPS):
            value = assembled(slots_c.at[2], recv_c.at[2], z, g)
            by[z, g * ROWS : (g + 1) * ROWS, :] = value
            if g == 0:
                rim_face[z] = value[0:1, :]
        return carry

    planes(by_body)
    rims[1].start()

    def plain(slots, received, out):
        def body(z, carry):
            for g in range(GROUPS):
                out[z, g * ROWS : (g + 1) * ROWS, :] = assembled(slots, received, z, g)
            return carry

        planes(body)

    pair_c[3].wait_recv()
    plain(slots_c.at[3], recv_c.at[3], bz)
    rims[2].start()
    pair_c[0].wait_recv()
    plain(slots_c.at[0], recv_c.at[0], alpha)
    pair_f[1].wait_recv()
    plain(slots_f.at[1], recv_f.at[1], rhs)
    for copy in rims:
        copy.wait_recv()

    halves = (slice(0, LANES), slice(LANES, NX))
    group_rows = [slice(g * ROWS, (g + 1) * ROWS) for g in range(GROUPS)]
    rim_values = rim_x[...]

    def scale_body(z, carry):
        low_rolled = pltpu.roll(bx[z, :, :LANES], LANES - 1, 1)
        high_rolled = pltpu.roll(bx[z, :, LANES:], LANES - 1, 1)
        edge = jnp.concatenate(
            [pltpu.roll(rim_values, 126 - 2 * (z * GROUPS + g), 1) for g in range(GROUPS)], axis=0
        )
        upper_x = (jnp.where(last_lane, high_rolled, low_rolled), jnp.where(last_lane, edge, high_rolled))
        before = []
        after = []
        inverses = []
        uppers = []
        for j, part in enumerate(halves):
            here_y = by[z, :, part]
            upper_y = jnp.where(
                end_row, jnp.broadcast_to(rim_y[z, :, part], (NY, LANES)), pltpu.roll(here_y, NY - 1, 0)
            )
            faces = [bx[z, :, part], upper_x[j], here_y, upper_y, bz[z, :, part], bz[z + 1, :, part]]
            centre = alpha[z, :, part]
            for face in faces:
                centre = centre + face
            inverse = 1.0 / centre
            inverses.append(inverse)
            inverse_ref[z, :, part] = inverse
            sent_y[0, 0, 2, z, :, part] = inverse[:1]
            sent_y[0, 1, 2, z, :, part] = inverse[NY - 1 :]
            uppers.append(upper_y[NY - ROWS :])
            diag[z, :, part] = centre
            scaled[z, :, part] = inverse * rhs[z, :, part]
            weights = [inverse * face for face in faces]
            before.append(weights[0])
            after.append(weights[1])
            if j == 0:
                weights[0] = jnp.where(first_lane, 0.0, weights[0])
            else:
                weights[1] = jnp.where(last_lane, 0.0, weights[1])
            edge_y[0, z, :, part] = jnp.where(row8 == 0, weights[2][:ROWS], 0.0)
            edge_y[1, z, :, part] = jnp.where(row8 == ROWS - 1, weights[3][NY - ROWS :], 0.0)
            weights[2] = jnp.where(row == 0, 0.0, weights[2])
            weights[3] = jnp.where(end_row, 0.0, weights[3])
            for i, weight in enumerate(weights):
                near[i, z, :, part] = weight
        edge_pack, inverse_pack, y_pack = carry
        for g, rows in enumerate(group_rows):
            edge_pack = packed(z, g, before[0][rows], after[1][rows], edge_pack)
            inverse_pack = packed(z, g, inverses[0][rows], inverses[1][rows], inverse_pack)
        y_pack = packed(z, 0, by[z, :ROWS, :LANES], by[z, :ROWS, LANES:], y_pack)
        y_pack = packed(z, GROUPS - 1, uppers[0], uppers[1], y_pack)
        return edge_pack, inverse_pack, y_pack

    edge_x[...], sent_x[0, 2], y_pack = planes(scale_body, (zero_pack, zero_pack, zero_pack))
    odd = lane8 - 2 * spots == 1
    spot_group = spots - GROUPS * (spots // GROUPS)
    low_rim = (spot_group == 0) & (row8 == 0)
    high_rim = (spot_group == GROUPS - 1) & (row8 == ROWS - 1)
    low_spots = spots < GROUPS
    high_spots = (spots >= GROUPS * (NZ - 1)) & (spots < GROUPS * NZ)
    z_pack = zero_pack
    for g, rows in enumerate(group_rows):
        z_pack = packed(0, g, bz[0, rows, :LANES], bz[0, rows, LANES:], z_pack)
        z_pack = packed(NZ - 1, g, bz[NZ, rows, :LANES], bz[NZ, rows, LANES:], z_pack)
    beta_pack[0] = jnp.where(low_rim | high_rim, y_pack, 0.0)
    beta_pack[1] = jnp.where(odd, rim_pack[...], pltpu.roll(rim_values, LANES - 1, 1))
    beta_pack[2] = z_pack
    sent_z[0, 0, 2] = inverse_ref[0]
    sent_z[0, 1, 2] = inverse_ref[NZ - 1]

    def swapped(value):
        return jnp.where(odd, pltpu.roll(value, 1, 1), pltpu.roll(value, LANES - 1, 1))

    def halo_z_of(k, side):
        return got_z.at[k // 2, side, 0] if k % 2 else field.at[k, side * (NZ + 1)]

    def halo_y_of(k, side):
        return got_y.at[k // 2, side, 0] if k % 2 else halo_y.at[k, side]

    def inner(k, z, first, last, carry):
        low, high = field[k, z + 1, :, :LANES], field[k, z + 1, :, LANES:]
        low_after, high_after = pltpu.roll(low, LANES - 1, 1), pltpu.roll(high, LANES - 1, 1)
        low_before, high_before = pltpu.roll(low, 1, 1), pltpu.roll(high, 1, 1)
        x_before = (low_before, jnp.where(first_lane, low_before, high_before))
        x_after = (jnp.where(last_lane, high_after, low_after), high_after)
        values = []
        for j, part in enumerate(halves):
            here = (low, high)[j]
            value = scaled[z, :, part] - here
            value = value + near[0, z, :, part] * x_before[j] + near[1, z, :, part] * x_after[j]
            value = value + near[2, z, :, part] * pltpu.roll(here, 1, 0)
            value = value + near[3, z, :, part] * pltpu.roll(here, NY - 1, 0)
            if not first:
                value = value + near[4, z, :, part] * field[k, z, :, part]
            if not last:
                value = value + near[5, z, :, part] * field[k, z + 2, :, part]
            scaled[z, :, part] = value
            values.append(value)
            if k % 2:
                ahead = SECOND[k] * value + FIRST[k] * here
                sent_y[k // 2, 0, 1, z, :, part] = ahead[:1]
                sent_y[k // 2, 1, 1, z, :, part] = ahead[NY - 1 :]
                if first:
                    sent_z[k // 2, 0, 1, :, part] = ahead
                if last:
                    sent_z[k // 2, 1, 1, :, part] = ahead
        if k % 2:
            for g, rows in enumerate(group_rows):
                carry = packed(z, g, values[0][rows], values[1][rows], carry)
        return carry

    def outer(k, z, first, last, sides, carry):
        fresh = [[], []]
        sending = k % 2 == 0 and k < SWEEPS
        for g, rows in enumerate(group_rows):
            moved = pltpu.roll(sides, LANES - 1 - 2 * (z * GROUPS + g), 1)
            for j, part in enumerate(halves):
                value = scaled[z, rows, part] + jnp.where(lane8 == (0, LANES - 1)[j], moved, 0.0)
                if g == 0:
                    value = value + edge_y[0, z, :, part] * jnp.broadcast_to(
                        halo_y_of(k, 0)[z, :, part], (ROWS, LANES)
                    )
                if g == GROUPS - 1:
                    value = value + edge_y[1, z, :, part] * jnp.broadcast_to(
                        halo_y_of(k, 1)[z, :, part], (ROWS, LANES)
                    )
                if first:
                    value = value + near[4, z, rows, part] * halo_z_of(k, 0)[rows, part]
                if last:
                    value = value + near[5, z, rows, part] * halo_z_of(k, 1)[rows, part]
                for b in range(2):
                    if k and k % 2 == 0 and (first or last) and g == b * (GROUPS - 1):
                        line = jnp.broadcast_to(line_fix[0 if first else 1, b, :, part], (ROWS, LANES))
                        value = value + jnp.where(row8 == b * (ROWS - 1), line, 0.0)
                if k == SWEEPS:
                    resid[z, rows, part] = diag[z, rows, part] * value
                    continue
                scaled[z, rows, part] = value
                step = SECOND[k] * value
                if k > 0:
                    step = step + FIRST[k] * field[k, z + 1, rows, part]
                field[k + 1, z + 1, rows, part] = step
                if k == SWEEPS - 1:
                    total[z, rows, part] = total[z, rows, part] + step
                if not sending:
                    continue
                if first:
                    sent_z[k // 2, 0, 0, rows, part] = step
                if last:
                    sent_z[k // 2, 1, 0, rows, part] = step
                if g == 0:
                    sent_y[k // 2, 0, 0, z, :, part] = step[:1]
                if g == GROUPS - 1:
                    sent_y[k // 2, 1, 0, z, :, part] = step[ROWS - 1 :]
                fresh[j].append(step)
            if sending:
                carry = packed(z, g, fresh[0][g], fresh[1][g], carry)
        return carry

    def run_inner(k):
        carry = inner(k, 0, True, False, zero_pack)
        carry = planes(lambda z, carry: inner(k, z, False, False, carry), carry, 1, NZ - 1)
        return inner(k, NZ - 1, False, True, carry)

    def run_outer(k, x_halo, extra=0.0):
        sides = edge_x[...] * swapped(x_halo) + extra
        carry = outer(k, 0, True, False, sides, zero_pack)
        carry = planes(lambda z, carry: outer(k, z, False, False, sides, carry), carry, 1, NZ - 1)
        return outer(k, NZ - 1, False, True, sides, carry)

    def either(ref_low, ref_high):
        return jnp.where(odd, ref_high, ref_low)

    def ahead(r, k):
        for side in range(2):
            own = side * (NZ - 1)
            for part in halves:
                value = got_z[0, side, 2, :, part] * (bz[side * NZ, :, part] * field[k, own + 1, :, part])
                field[k + 1, side * (NZ + 1), :, part] = got_z[r, side, 1, :, part] + SECOND[k] * value
            face = (rim_face, rim_y)[side]
            value = got_y[0, side, 2] * (face[...] * sent_y[r, side, 0])
            halo_y[k + 1, side] = got_y[r, side, 1] + SECOND[k] * value
        value = either(got_x[0, 0, 2], got_x[0, 1, 2]) * swapped(sent_q[r, 1])
        return either(got_x[r, 0, 1], got_x[r, 1, 1]) + SECOND[k] * value

    def weigh_edges():
        y_pack = zero_pack
        z_pack = zero_pack
        for a in range(2):
            z = a * (NZ - 1)
            tiles = [near[4 + a, z, :, part] * got_z[0, a, 2, :, part] for part in halves]
            for g, rows in enumerate(group_rows):
                z_pack = packed(z, g, tiles[0][rows], tiles[1][rows], z_pack)
            for b in range(2):
                at = b * (NY - 1)
                low = b * (ROWS - 1)
                line_weight[a, b, 0] = near[4 + a, z, at : at + 1, :] * got_z[0, a, 2, at : at + 1, :]
                line_weight[a, b, 1] = edge_y[b, z, low : low + 1, :] * got_y[0, b, 2, z]

        def body(z, y_pack):
            for b in range(2):
                tiles = [
                    edge_y[b, z, :, part] * jnp.broadcast_to(got_y[0, b, 2, z, :, part], (ROWS, LANES))
                    for part in halves
                ]
                y_pack = packed(z, b * (GROUPS - 1), tiles[0], tiles[1], y_pack)
            return y_pack

        pack_weight[0] = edge_x[...] * swapped(either(got_x[0, 0, 2], got_x[0, 1, 2]))
        pack_weight[1] = planes(body, y_pack)
        pack_weight[2] = z_pack

    def edge_fix(r, k):
        for a in range(2):
            for b in range(2):
                value = line_weight[a, b, 0] * got_yz[r, a, b, 0] + line_weight[a, b, 1] * got_yz[r, a, b, 1]
                line_fix[a, b] = SECOND[k] * value

        def from_y(i):
            below = swapped(either(got_xy[r, 0, 0, i], got_xy[r, 1, 0, i]))
            above = swapped(either(got_xy[r, 0, 1, i], got_xy[r, 1, 1, i]))
            shift = 2 * (GROUPS - 1)
            below = jnp.where(low_rim, pltpu.roll(pltpu.roll(below, 1, 0), LANES - shift, 1), 0.0)
            return below + jnp.where(high_rim, pltpu.roll(pltpu.roll(above, ROWS - 1, 0), shift, 1), 0.0)

        def from_z(i):
            below = swapped(either(got_xz[r, 0, 0], got_xz[r, 1, 0]))
            above = swapped(either(got_xz[r, 0, 1], got_xz[r, 1, 1]))
            shift = 2 * GROUPS * (NZ - 1)
            back = (1 - i) * ROWS
            below = jnp.where(low_spots, pltpu.roll(below, LANES - shift - back, 1), 0.0)
            return below + jnp.where(high_spots, pltpu.roll(above, shift - back, 1), 0.0)

        value = pack_weight[0] * (from_y(0) + from_z(1))
        return SECOND[k] * (value + pack_weight[1] * from_y(1) + pack_weight[2] * from_z(0))

    def apply_two(r):
        k = 2 * r + 1
        own = sent_x[r, 0]
        sent_q[r, 0] = beta_pack[0] * own
        across = beta_pack[1] * own
        sent_q[r, 1] = across
        ends = pltpu.roll(jnp.where(low_spots | high_spots, across, 0.0), ROWS, 1)
        sent_q[r, 2] = beta_pack[2] * own + ends
        for a in range(2):
            z = a * (NZ - 1)
            for b in range(2):
                line = sent_y[r, b, 0, z]
                at = b * (NY - 1)
                sent_yz[r, a, b, 0] = (rim_face, rim_y)[b][z] * line
                sent_yz[r, a, b, 1] = bz[a * NZ, at : at + 1, :] * line
        far_copies = edge_copies(r)
        for copy in far_copies:
            copy.start()

        sent_x[r, 1] = SECOND[k] * run_inner(k) + FIRST[k] * own
        near_copies = face_copies(r, 0, pl.ds(0, 2))
        for copy in near_copies:
            copy.start()
        if r == 0:
            near_copies += face_copies(r, 6, pl.ds(2, 1))
            for copy in near_copies[6:]:
                copy.start()
        def sum_body(z, carry):
            for part in halves:
                if r == 0:
                    total[z, :, part] = field[0, z + 1, :, part] + field[1, z + 1, :, part]
                else:
                    total[z, :, part] = (
                        total[z, :, part] + field[2, z + 1, :, part] + field[3, z + 1, :, part]
                    )
            return carry

        planes(sum_body)
        for copy in near_copies[:6]:
            copy.wait_recv()
        run_outer(k, either(got_x[r, 0, 0], got_x[r, 1, 0]))
        if k == SWEEPS - 1:
            x_out.start()
        for copy in near_copies[6:]:
            copy.wait_recv()
        x_halo = ahead(r, k)
        if r == 0:
            weigh_edges()
        run_inner(k + 1)
        for copy in far_copies:
            copy.wait_recv()
        return near_copies + far_copies, run_outer(k + 1, x_halo, edge_fix(r, k))

    x_out = pltpu.make_async_copy(total, x_hbm, out_sem.at[0])
    run_inner(0)
    for copy in first_halos:
        copy.wait_recv()
    sent_x[0, 0] = run_outer(0, either(halo_x[0, 0], halo_x[0, 1]))
    first_copies, sent_x[1, 0] = apply_two(0)
    second_copies, unused = apply_two(1)
    r_out = pltpu.make_async_copy(resid, r_hbm, out_sem.at[1])
    r_out.start()
    for copy in pair_f + pair_c + rims + first_halos + first_copies + second_copies:
        copy.wait_send()
    x_out.wait()
    r_out.wait()


def emit(x_ref, r_ref, x_out, r_out, sem):
    first = pltpu.make_async_copy(x_ref, x_out, sem.at[0])
    second = pltpu.make_async_copy(r_ref, r_out, sem.at[1])
    first.start()
    second.start()
    first.wait()
    second.wait()


def local(old_fields, old_coef, held_slabs):
    slots = old_fields.shape[1]
    fields = old_fields.reshape(2, slots, NZ, 2, ROWS, NX)
    coef = old_coef.reshape(4, slots, NZ, 2, ROWS, NX)
    brick = (NZ, NY, NX)
    rounds = SWEEPS + 1
    dma = pltpu.SemaphoreType.DMA
    anywhere = pl.BlockSpec(memory_space=pl.ANY)
    hbm = pl.BlockSpec(memory_space=pltpu.HBM)
    held = pltpu.with_memory_space_constraint(jnp.transpose(held_slabs, (1, 2, 0)), pltpu.HBM)
    results = pl.pallas_call(
        kernel,
        out_shape=(jax.ShapeDtypeStruct(brick, F32), jax.ShapeDtypeStruct(brick, F32)),
        in_specs=[hbm, hbm, hbm],
        out_specs=(anywhere, anywhere),
        scratch_shapes=[
            pltpu.VMEM((2, slots, NZ, 2, ROWS, NX), F32),
            pltpu.VMEM((4, slots, NZ, 2, ROWS, NX), BF16),
            pltpu.VMEM((2, NZ, GROUPS, ROWS, NX), F32),
            pltpu.VMEM((4, NZ, GROUPS, ROWS, NX), BF16),
            pltpu.VMEM((2, NZ, GROUPS, ROWS, NX), F32),
            pltpu.VMEM((4, NZ, GROUPS, ROWS, NX), BF16),
            pltpu.VMEM((rounds, NZ + 2, NY, NX), F32),
            pltpu.VMEM(brick, F32),
            pltpu.VMEM(brick, F32),
            pltpu.VMEM(brick, F32),
            pltpu.VMEM((NZ + 1, NY, NX), F32),
            pltpu.VMEM(brick, F32),
            pltpu.VMEM((6, NZ, NY, NX), F32),
            pltpu.VMEM((2, NZ, ROWS, NX), F32),
            pltpu.VMEM((ROWS, LANES), F32),
            pltpu.VMEM(brick, F32),
            pltpu.VMEM(brick, F32),
            pltpu.VMEM(brick, F32),
            pltpu.VMEM(brick, F32),
            pltpu.VMEM(brick, F32),
            pltpu.VMEM((rounds, ROWS, LANES), F32),
            pltpu.VMEM((rounds, 2, NZ, 1, NX), F32),
            pltpu.VMEM((rounds, 2, ROWS, LANES), F32),
            pltpu.VMEM((rounds, 2, NZ, 1, NX), F32),
            pltpu.VMEM((ROWS, LANES), F32),
            pltpu.VMEM((NZ, 1, NX), F32),
            pltpu.VMEM((ROWS, LANES), F32),
            pltpu.VMEM((NZ, 1, NX), F32),
            pltpu.VMEM((3, ROWS, LANES), F32),
            pltpu.VMEM((2, 2, 3, NY, NX), F32),
            pltpu.VMEM((2, 2, 3, NY, NX), F32),
            pltpu.VMEM((2, 2, 3, NZ, 1, NX), F32),
            pltpu.VMEM((2, 2, 3, NZ, 1, NX), F32),
            pltpu.VMEM((2, 3, ROWS, LANES), F32),
            pltpu.VMEM((2, 2, 3, ROWS, LANES), F32),
            pltpu.VMEM((2, 2, 2, 2, 1, NX), F32),
            pltpu.VMEM((2, 2, 2, 2, 1, NX), F32),
            pltpu.VMEM((2, 3, ROWS, LANES), F32),
            pltpu.VMEM((2, 2, 2, ROWS, LANES), F32),
            pltpu.VMEM((2, 2, 2, 2, ROWS, LANES), F32),
            pltpu.VMEM((2, 2, 2, 1, NX), F32),
            pltpu.VMEM((2, 2, 1, NX), F32),
            pltpu.VMEM((3, ROWS, LANES), F32),
            pltpu.SMEM((1, 1, slots), jnp.int32),
            dma((6,)),
            dma((1,)),
            dma((6,)),
            dma((6,)),
            dma((rounds, 6)),
            dma((rounds, 6)),
            dma((3,)),
            dma((3,)),
            dma((2,)),
            dma((2, 24)),
            dma((2, 24)),
        ],
        compiler_params=pltpu.CompilerParams(
            collective_id=0, has_side_effects=True, vmem_limit_bytes=55767040
        ),
        name="smooth",
    )(fields, coef, held)
    return pl.pallas_call(
        emit,
        out_shape=(jax.ShapeDtypeStruct(brick, F32), jax.ShapeDtypeStruct(brick, F32)),
        in_specs=[anywhere, anywhere],
        out_specs=(hbm, hbm),
        scratch_shapes=[dma((2,))],
        compiler_params=pltpu.CompilerParams(vmem_limit_bytes=1 << 20),
        name="emit",
    )(*results)


def solution(mesh):
    in_specs = (
        P(None, "gy", "gz", None, "gx"),
        P(None, "gy", "gz", None, "gx"),
        P("gy", "gz", "gx"),
    )
    out_specs = (P("gz", "gy", "gx"), P("gz", "gy", "gx"))
    return jax.shard_map(local, mesh=mesh, in_specs=in_specs, out_specs=out_specs, check_vma=False)
```

```python
import functools
import jax
import jax.numpy as jnp
from jax import lax
from jax.experimental import pallas as pl
from jax.experimental.pallas import tpu as pltpu
from jax.sharding import PartitionSpec as P

SWEEPS = 4
NZ = 16
NY = 24
NX = 256
ROWS = 8
LANES = 128
GROUPS = NY // ROWS
MESH = pl.DeviceIdType.MESH
F32 = jnp.float32
BF16 = jnp.bfloat16


def chebyshev_weights(count):
    low_bound = 0.25
    high_bound = 2.0
    centre_value = 0.5 * (high_bound + low_bound)
    half_width = 0.5 * (high_bound - low_bound)
    ratio_value = centre_value / half_width
    damping = 1.0 / ratio_value
    first_list = [0.0]
    second_list = [1.0 / centre_value]
    for step_index in range(1, count):
        damping_next = 1.0 / (2.0 * ratio_value - damping)
        first_list.append(damping_next * damping)
        second_list.append(2.0 * damping_next / half_width)
        damping = damping_next
    return first_list, second_list


FIRST, SECOND = chebyshev_weights(SWEEPS)


def ring(axis):
    count = lax.axis_size(axis)
    me = lax.axis_index(axis)
    low = {axis: lax.rem(me + count - 1, count)}
    high = {axis: lax.rem(me + 1, count)}
    return low, high


def kernel(
    fields_hbm, coef_hbm, held_hbm, x_hbm, r_hbm,
    slots_f, slots_c, send_f, send_c, recv_f, recv_c,
    field, alpha, bx, by, bz, rhs, near, edge_y, edge_x, diag, inverse_ref, scaled, total, resid,
    pack, face_y, halo_x, halo_y, rim_pack, rim_face, rim_x, rim_y, beta_pack,
    sent_z, got_z, sent_y, got_y, sent_x, got_x, sent_yz, got_yz, sent_q, got_xz, got_xy, line_weight, line_fix, pack_weight, held_ref,
    load_sem, held_sem, pair_send, pair_recv, halo_send, halo_recv, rim_send, rim_recv, out_sem,
    both_send, both_recv,
):
    group = lax.axis_index("gy")
    half = lax.rem(group, 2)
    first_slab = 3 * (group // 2)
    partner = {"gy": group + 1 - 2 * half}
    x_low, x_high = ring("gx")
    y_low, y_high = ring("gy")
    z_low, z_high = ring("gz")

    barrier = pltpu.get_barrier_semaphore()
    x_sides, y_sides, z_sides = (x_low, x_high), (y_low, y_high), (z_low, z_high)
    faces = [x_low, x_high, y_low, y_high, z_low, z_high]
    for neighbour in faces:
        pl.semaphore_signal(barrier, inc=1, device_id=neighbour, device_id_type=MESH)

    load_held = pltpu.make_async_copy(held_hbm, held_ref, held_sem.at[0])
    loads_f = [pltpu.make_async_copy(fields_hbm.at[c], slots_f.at[c], load_sem.at[c]) for c in range(2)]
    loads_c = [pltpu.make_async_copy(coef_hbm.at[c], slots_c.at[c], load_sem.at[2 + c]) for c in range(4)]
    load_held.start()
    loads_f[0].start()
    for c in (1, 2, 3, 0):
        loads_c[c].start()
    loads_f[1].start()
    load_held.wait()

    id0 = held_ref[0, 0, 0]
    id1 = held_ref[0, 0, 1]
    mine = [first_slab + (3 * half + g) // 2 for g in range(GROUPS)]
    theirs = [first_slab + (3 * (1 - half) + g) // 2 for g in range(GROUPS)]
    my_part = [lax.rem(half + g, 2) for g in range(GROUPS)]
    their_part = [lax.rem(1 - half + g, 2) for g in range(GROUPS)]

    row8 = lax.broadcasted_iota(jnp.int32, (ROWS, LANES), 0)
    row = lax.broadcasted_iota(jnp.int32, (NY, LANES), 0)
    lane = lax.broadcasted_iota(jnp.int32, (NY, LANES), 1)
    lane8 = lax.broadcasted_iota(jnp.int32, (ROWS, LANES), 1)
    end_row = row == NY - 1
    first_lane = lane == 0
    last_lane = lane == LANES - 1
    spots = lane8 // 2

    def copy_to(source, target, send_sem, recv_sem, device):
        return pltpu.make_async_remote_copy(
            src_ref=source, dst_ref=target, send_sem=send_sem, recv_sem=recv_sem,
            device_id=device, device_id_type=MESH,
        )

    pair_f = [copy_to(send_f.at[c], recv_f.at[c], pair_send.at[c], pair_recv.at[c], partner) for c in range(2)]
    pair_c = [
        copy_to(send_c.at[c], recv_c.at[c], pair_send.at[2 + c], pair_recv.at[2 + c], partner) for c in range(4)
    ]

    def halo_copies(k):
        return [
            copy_to(pack.at[k], halo_x.at[k, 1], halo_send.at[k, 0], halo_recv.at[k, 0], x_low),
            copy_to(pack.at[k], halo_x.at[k, 0], halo_send.at[k, 1], halo_recv.at[k, 1], x_high),
            copy_to(face_y.at[k, 0], halo_y.at[k, 1], halo_send.at[k, 2], halo_recv.at[k, 2], y_low),
            copy_to(face_y.at[k, 1], halo_y.at[k, 0], halo_send.at[k, 3], halo_recv.at[k, 3], y_high),
            copy_to(field.at[k, 1], field.at[k, NZ + 1], halo_send.at[k, 4], halo_recv.at[k, 4], z_low),
            copy_to(field.at[k, NZ], field.at[k, 0], halo_send.at[k, 5], halo_recv.at[k, 5], z_high),
        ]

    first_halos = halo_copies(0)

    def numbered(r, first, moves):
        return [
            copy_to(source, target, both_send.at[r, first + i], both_recv.at[r, first + i], device)
            for i, (source, target, device) in enumerate(moves)
        ]

    def edge_copies(r):
        moves = []
        for a in range(2):
            for b in range(2):
                device = {**x_sides[a], **y_sides[b]}
                line = pl.ds(b * (ROWS - 1), 1)
                moves.append((sent_q.at[r, pl.ds(0, 2), line], got_xy.at[r, 1 - a, 1 - b, pl.ds(0, 2), line], device))
        for a in range(2):
            for b in range(2):
                device = {**x_sides[a], **z_sides[b]}
                moves.append((sent_q.at[r, 2], got_xz.at[r, 1 - a, 1 - b], device))
        for a in range(2):
            for b in range(2):
                moves.append((sent_yz.at[r, a, b], got_yz.at[r, 1 - a, 1 - b], {**z_sides[a], **y_sides[b]}))
        return numbered(r, 12, moves)

    def face_copies(r, first, part):
        moves = [(sent_x.at[r, part], got_x.at[r, 1 - a, part], x_sides[a]) for a in range(2)]
        moves += [(sent_y.at[r, a, part], got_y.at[r, 1 - a, part], y_sides[a]) for a in range(2)]
        moves += [(sent_z.at[r, a, part], got_z.at[r, 1 - a, part], z_sides[a]) for a in range(2)]
        return numbered(r, first, moves)

    rims = [
        copy_to(rim_pack, rim_x, rim_send.at[0], rim_recv.at[0], x_low),
        copy_to(rim_face, rim_y, rim_send.at[1], rim_recv.at[1], y_low),
        copy_to(bz.at[0], bz.at[NZ], rim_send.at[2], rim_recv.at[2], z_low),
    ]

    def planes(body, carry=0, first=0, last=NZ):
        return lax.fori_loop(first, last, body, carry, unroll=True)

    def prepare(slots, out):
        def body(z, carry):
            for g in range(GROUPS):
                out[z, g] = lax.select(id0 == theirs[g], slots[0, z, their_part[g]], slots[1, z, their_part[g]])
            return carry

        planes(body)

    def assembled(slots, received, z, g):
        return lax.select(
            id0 == mine[g],
            slots[0, z, my_part[g]],
            lax.select(id1 == mine[g], slots[1, z, my_part[g]], received[z, g]),
        ).astype(F32)

    def packed(z, g, tile_low, tile_high, carry):
        spot = z * GROUPS + g
        both = jnp.where(lane8 == 0, tile_low, tile_high)
        moved = pltpu.roll(both, 2 * spot + 1, 1)
        return jnp.where(spots == spot, moved, carry)

    loads_f[0].wait()
    prepare(slots_f.at[0], send_f.at[0])
    pl.semaphore_wait(barrier, len(faces))
    pair_f[0].start()
    for c in (1, 2, 3, 0):
        loads_c[c].wait()
        prepare(slots_c.at[c], send_c.at[c])
        pair_c[c].start()
    loads_f[1].wait()
    prepare(slots_f.at[1], send_f.at[1])
    pair_f[1].start()

    zero_pack = jnp.zeros((ROWS, LANES), F32)

    pair_f[0].wait_recv()

    def start_body(z, carry):
        for g in range(GROUPS):
            value = assembled(slots_f.at[0], recv_f.at[0], z, g)
            field[0, z + 1, g * ROWS : (g + 1) * ROWS, :] = value
            if g == 0:
                face_y[0, 0, z] = value[0:1, :]
            if g == GROUPS - 1:
                face_y[0, 1, z] = value[ROWS - 1 : ROWS, :]
            carry = packed(z, g, value[:, :LANES], value[:, LANES:], carry)
        return carry

    pack[0] = planes(start_body, zero_pack)
    for copy in first_halos:
        copy.start()

    pair_c[1].wait_recv()

    def bx_body(z, carry):
        for g in range(GROUPS):
            value = assembled(slots_c.at[1], recv_c.at[1], z, g)
            bx[z, g * ROWS : (g + 1) * ROWS, :] = value
            carry = packed(z, g, value[:, :LANES], value[:, LANES:], carry)
        return carry

    rim_pack[...] = planes(bx_body, zero_pack)
    rims[0].start()
    pair_c[2].wait_recv()

    def by_body(z, carry):
        for g in range(GROUPS):
            value = assembled(slots_c.at[2], recv_c.at[2], z, g)
            by[z, g * ROWS : (g + 1) * ROWS, :] = value
            if g == 0:
                rim_face[z] = value[0:1, :]
        return carry

    planes(by_body)
    rims[1].start()

    def plain(slots, received, out):
        def body(z, carry):
            for g in range(GROUPS):
                out[z, g * ROWS : (g + 1) * ROWS, :] = assembled(slots, received, z, g)
            return carry

        planes(body)

    pair_c[3].wait_recv()
    plain(slots_c.at[3], recv_c.at[3], bz)
    rims[2].start()
    pair_c[0].wait_recv()
    plain(slots_c.at[0], recv_c.at[0], alpha)
    pair_f[1].wait_recv()
    plain(slots_f.at[1], recv_f.at[1], rhs)
    for copy in rims:
        copy.wait_recv()

    halves = (slice(0, LANES), slice(LANES, NX))
    group_rows = [slice(g * ROWS, (g + 1) * ROWS) for g in range(GROUPS)]
    rim_values = rim_x[...]

    def scale_body(z, carry):
        low_rolled = pltpu.roll(bx[z, :, :LANES], LANES - 1, 1)
        high_rolled = pltpu.roll(bx[z, :, LANES:], LANES - 1, 1)
        edge = jnp.concatenate(
            [pltpu.roll(rim_values, 126 - 2 * (z * GROUPS + g), 1) for g in range(GROUPS)], axis=0
        )
        upper_x = (jnp.where(last_lane, high_rolled, low_rolled), jnp.where(last_lane, edge, high_rolled))
        before = []
        after = []
        inverses = []
        uppers = []
        for j, part in enumerate(halves):
            here_y = by[z, :, part]
            upper_y = jnp.where(
                end_row, jnp.broadcast_to(rim_y[z, :, part], (NY, LANES)), pltpu.roll(here_y, NY - 1, 0)
            )
            faces = [bx[z, :, part], upper_x[j], here_y, upper_y, bz[z, :, part], bz[z + 1, :, part]]
            centre = alpha[z, :, part]
            for face in faces:
                centre = centre + face
            inverse = 1.0 / centre
            inverses.append(inverse)
            inverse_ref[z, :, part] = inverse
            sent_y[0, 0, 2, z, :, part] = inverse[:1]
            sent_y[0, 1, 2, z, :, part] = inverse[NY - 1 :]
            uppers.append(upper_y[NY - ROWS :])
            diag[z, :, part] = centre
            scaled[z, :, part] = inverse * rhs[z, :, part]
            weights = [inverse * face for face in faces]
            before.append(weights[0])
            after.append(weights[1])
            if j == 0:
                weights[0] = jnp.where(first_lane, 0.0, weights[0])
            else:
                weights[1] = jnp.where(last_lane, 0.0, weights[1])
            edge_y[0, z, :, part] = jnp.where(row8 == 0, weights[2][:ROWS], 0.0)
            edge_y[1, z, :, part] = jnp.where(row8 == ROWS - 1, weights[3][NY - ROWS :], 0.0)
            weights[2] = jnp.where(row == 0, 0.0, weights[2])
            weights[3] = jnp.where(end_row, 0.0, weights[3])
            for i, weight in enumerate(weights):
                near[i, z, :, part] = weight
        edge_pack, inverse_pack, y_pack = carry
        for g, rows in enumerate(group_rows):
            edge_pack = packed(z, g, before[0][rows], after[1][rows], edge_pack)
            inverse_pack = packed(z, g, inverses[0][rows], inverses[1][rows], inverse_pack)
        y_pack = packed(z, 0, by[z, :ROWS, :LANES], by[z, :ROWS, LANES:], y_pack)
        y_pack = packed(z, GROUPS - 1, uppers[0], uppers[1], y_pack)
        return edge_pack, inverse_pack, y_pack

    edge_x[...], sent_x[0, 2], y_pack = planes(scale_body, (zero_pack, zero_pack, zero_pack))
    odd = lane8 - 2 * spots == 1
    spot_group = spots - GROUPS * (spots // GROUPS)
    low_rim = (spot_group == 0) & (row8 == 0)
    high_rim = (spot_group == GROUPS - 1) & (row8 == ROWS - 1)
    low_spots = spots < GROUPS
    high_spots = (spots >= GROUPS * (NZ - 1)) & (spots < GROUPS * NZ)
    z_pack = zero_pack
    for g, rows in enumerate(group_rows):
        z_pack = packed(0, g, bz[0, rows, :LANES], bz[0, rows, LANES:], z_pack)
        z_pack = packed(NZ - 1, g, bz[NZ, rows, :LANES], bz[NZ, rows, LANES:], z_pack)
    beta_pack[0] = jnp.where(low_rim | high_rim, y_pack, 0.0)
    beta_pack[1] = jnp.where(odd, rim_pack[...], pltpu.roll(rim_values, LANES - 1, 1))
    beta_pack[2] = z_pack
    sent_z[0, 0, 2] = inverse_ref[0]
    sent_z[0, 1, 2] = inverse_ref[NZ - 1]

    def swapped(value):
        return jnp.where(odd, pltpu.roll(value, 1, 1), pltpu.roll(value, LANES - 1, 1))

    def halo_z_of(k, side):
        return got_z.at[k // 2, side, 0] if k % 2 else field.at[k, side * (NZ + 1)]

    def halo_y_of(k, side):
        return got_y.at[k // 2, side, 0] if k % 2 else halo_y.at[k, side]

    def inner(k, z, first, last, carry):
        low, high = field[k, z + 1, :, :LANES], field[k, z + 1, :, LANES:]
        low_after, high_after = pltpu.roll(low, LANES - 1, 1), pltpu.roll(high, LANES - 1, 1)
        low_before, high_before = pltpu.roll(low, 1, 1), pltpu.roll(high, 1, 1)
        x_before = (low_before, jnp.where(first_lane, low_before, high_before))
        x_after = (jnp.where(last_lane, high_after, low_after), high_after)
        values = []
        for j, part in enumerate(halves):
            here = (low, high)[j]
            value = scaled[z, :, part] - here
            value = value + near[0, z, :, part] * x_before[j] + near[1, z, :, part] * x_after[j]
            value = value + near[2, z, :, part] * pltpu.roll(here, 1, 0)
            value = value + near[3, z, :, part] * pltpu.roll(here, NY - 1, 0)
            if not first:
                value = value + near[4, z, :, part] * field[k, z, :, part]
            if not last:
                value = value + near[5, z, :, part] * field[k, z + 2, :, part]
            scaled[z, :, part] = value
            values.append(value)
            if k % 2:
                ahead = SECOND[k] * value + FIRST[k] * here
                sent_y[k // 2, 0, 1, z, :, part] = ahead[:1]
                sent_y[k // 2, 1, 1, z, :, part] = ahead[NY - 1 :]
                if first:
                    sent_z[k // 2, 0, 1, :, part] = ahead
                if last:
                    sent_z[k // 2, 1, 1, :, part] = ahead
        if k % 2:
            for g, rows in enumerate(group_rows):
                carry = packed(z, g, values[0][rows], values[1][rows], carry)
        return carry

    def outer(k, z, first, last, sides, carry):
        fresh = [[], []]
        sending = k % 2 == 0 and k < SWEEPS
        for g, rows in enumerate(group_rows):
            moved = pltpu.roll(sides, LANES - 1 - 2 * (z * GROUPS + g), 1)
            for j, part in enumerate(halves):
                value = scaled[z, rows, part] + jnp.where(lane8 == (0, LANES - 1)[j], moved, 0.0)
                if g == 0:
                    value = value + edge_y[0, z, :, part] * jnp.broadcast_to(
                        halo_y_of(k, 0)[z, :, part], (ROWS, LANES)
                    )
                if g == GROUPS - 1:
                    value = value + edge_y[1, z, :, part] * jnp.broadcast_to(
                        halo_y_of(k, 1)[z, :, part], (ROWS, LANES)
                    )
                if first:
                    value = value + near[4, z, rows, part] * halo_z_of(k, 0)[rows, part]
                if last:
                    value = value + near[5, z, rows, part] * halo_z_of(k, 1)[rows, part]
                for b in range(2):
                    if k and k % 2 == 0 and (first or last) and g == b * (GROUPS - 1):
                        line = jnp.broadcast_to(line_fix[0 if first else 1, b, :, part], (ROWS, LANES))
                        value = value + jnp.where(row8 == b * (ROWS - 1), line, 0.0)
                if k == SWEEPS:
                    resid[z, rows, part] = diag[z, rows, part] * value
                    continue
                scaled[z, rows, part] = value
                step = SECOND[k] * value
                if k > 0:
                    step = step + FIRST[k] * field[k, z + 1, rows, part]
                field[k + 1, z + 1, rows, part] = step
                if k == SWEEPS - 1:
                    total[z, rows, part] = total[z, rows, part] + step
                if not sending:
                    continue
                if first:
                    sent_z[k // 2, 0, 0, rows, part] = step
                if last:
                    sent_z[k // 2, 1, 0, rows, part] = step
                if g == 0:
                    sent_y[k // 2, 0, 0, z, :, part] = step[:1]
                if g == GROUPS - 1:
                    sent_y[k // 2, 1, 0, z, :, part] = step[ROWS - 1 :]
                fresh[j].append(step)
            if sending:
                carry = packed(z, g, fresh[0][g], fresh[1][g], carry)
        return carry

    def run_inner(k):
        carry = inner(k, 0, True, False, zero_pack)
        carry = planes(lambda z, carry: inner(k, z, False, False, carry), carry, 1, NZ - 1)
        return inner(k, NZ - 1, False, True, carry)

    def run_outer(k, x_halo, extra=0.0):
        sides = edge_x[...] * swapped(x_halo) + extra
        carry = outer(k, 0, True, False, sides, zero_pack)
        carry = planes(lambda z, carry: outer(k, z, False, False, sides, carry), carry, 1, NZ - 1)
        return outer(k, NZ - 1, False, True, sides, carry)

    def either(ref_low, ref_high):
        return jnp.where(odd, ref_high, ref_low)

    def ahead(r, k):
        for side in range(2):
            own = side * (NZ - 1)
            for part in halves:
                value = got_z[0, side, 2, :, part] * (bz[side * NZ, :, part] * field[k, own + 1, :, part])
                field[k + 1, side * (NZ + 1), :, part] = got_z[r, side, 1, :, part] + SECOND[k] * value
            face = (rim_face, rim_y)[side]
            value = got_y[0, side, 2] * (face[...] * sent_y[r, side, 0])
            halo_y[k + 1, side] = got_y[r, side, 1] + SECOND[k] * value
        value = either(got_x[0, 0, 2], got_x[0, 1, 2]) * swapped(sent_q[r, 1])
        return either(got_x[r, 0, 1], got_x[r, 1, 1]) + SECOND[k] * value

    def weigh_edges():
        y_pack = zero_pack
        z_pack = zero_pack
        for a in range(2):
            z = a * (NZ - 1)
            tiles = [near[4 + a, z, :, part] * got_z[0, a, 2, :, part] for part in halves]
            for g, rows in enumerate(group_rows):
                z_pack = packed(z, g, tiles[0][rows], tiles[1][rows], z_pack)
            for b in range(2):
                at = b * (NY - 1)
                low = b * (ROWS - 1)
                line_weight[a, b, 0] = near[4 + a, z, at : at + 1, :] * got_z[0, a, 2, at : at + 1, :]
                line_weight[a, b, 1] = edge_y[b, z, low : low + 1, :] * got_y[0, b, 2, z]

        def body(z, y_pack):
            for b in range(2):
                tiles = [
                    edge_y[b, z, :, part] * jnp.broadcast_to(got_y[0, b, 2, z, :, part], (ROWS, LANES))
                    for part in halves
                ]
                y_pack = packed(z, b * (GROUPS - 1), tiles[0], tiles[1], y_pack)
            return y_pack

        pack_weight[0] = edge_x[...] * swapped(either(got_x[0, 0, 2], got_x[0, 1, 2]))
        pack_weight[1] = planes(body, y_pack)
        pack_weight[2] = z_pack

    def edge_fix(r, k):
        for a in range(2):
            for b in range(2):
                value = line_weight[a, b, 0] * got_yz[r, a, b, 0] + line_weight[a, b, 1] * got_yz[r, a, b, 1]
                line_fix[a, b] = SECOND[k] * value

        def from_y(i):
            below = swapped(either(got_xy[r, 0, 0, i], got_xy[r, 1, 0, i]))
            above = swapped(either(got_xy[r, 0, 1, i], got_xy[r, 1, 1, i]))
            shift = 2 * (GROUPS - 1)
            below = jnp.where(low_rim, pltpu.roll(pltpu.roll(below, 1, 0), LANES - shift, 1), 0.0)
            return below + jnp.where(high_rim, pltpu.roll(pltpu.roll(above, ROWS - 1, 0), shift, 1), 0.0)

        def from_z(i):
            below = swapped(either(got_xz[r, 0, 0], got_xz[r, 1, 0]))
            above = swapped(either(got_xz[r, 0, 1], got_xz[r, 1, 1]))
            shift = 2 * GROUPS * (NZ - 1)
            back = (1 - i) * ROWS
            below = jnp.where(low_spots, pltpu.roll(below, LANES - shift - back, 1), 0.0)
            return below + jnp.where(high_spots, pltpu.roll(above, shift - back, 1), 0.0)

        value = pack_weight[0] * (from_y(0) + from_z(1))
        return SECOND[k] * (value + pack_weight[1] * from_y(1) + pack_weight[2] * from_z(0))

    def apply_two(r):
        k = 2 * r + 1
        own = sent_x[r, 0]
        sent_q[r, 0] = beta_pack[0] * own
        across = beta_pack[1] * own
        sent_q[r, 1] = across
        ends = pltpu.roll(jnp.where(low_spots | high_spots, across, 0.0), ROWS, 1)
        sent_q[r, 2] = beta_pack[2] * own + ends
        for a in range(2):
            z = a * (NZ - 1)
            for b in range(2):
                line = sent_y[r, b, 0, z]
                at = b * (NY - 1)
                sent_yz[r, a, b, 0] = (rim_face, rim_y)[b][z] * line
                sent_yz[r, a, b, 1] = bz[a * NZ, at : at + 1, :] * line
        far_copies = edge_copies(r)
        for copy in far_copies:
            copy.start()

        sent_x[r, 1] = SECOND[k] * run_inner(k) + FIRST[k] * own
        near_copies = face_copies(r, 0, pl.ds(0, 2))
        for copy in near_copies:
            copy.start()
        if r == 0:
            near_copies += face_copies(r, 6, pl.ds(2, 1))
            for copy in near_copies[6:]:
                copy.start()
        def sum_body(z, carry):
            for part in halves:
                if r == 0:
                    total[z, :, part] = field[0, z + 1, :, part] + field[1, z + 1, :, part]
                else:
                    total[z, :, part] = (
                        total[z, :, part] + field[2, z + 1, :, part] + field[3, z + 1, :, part]
                    )
            return carry

        planes(sum_body)
        for copy in near_copies[:6]:
            copy.wait_recv()
        run_outer(k, either(got_x[r, 0, 0], got_x[r, 1, 0]))
        if k == SWEEPS - 1:
            x_out.start()
        for copy in near_copies[6:]:
            copy.wait_recv()
        x_halo = ahead(r, k)
        if r == 0:
            weigh_edges()
        run_inner(k + 1)
        for copy in far_copies:
            copy.wait_recv()
        return near_copies + far_copies, run_outer(k + 1, x_halo, edge_fix(r, k))

    x_out = pltpu.make_async_copy(total, x_hbm, out_sem.at[0])
    run_inner(0)
    for copy in first_halos:
        copy.wait_recv()
    sent_x[0, 0] = run_outer(0, either(halo_x[0, 0], halo_x[0, 1]))
    first_copies, sent_x[1, 0] = apply_two(0)
    second_copies, unused = apply_two(1)
    r_out = pltpu.make_async_copy(resid, r_hbm, out_sem.at[1])
    r_out.start()
    for copy in pair_f + pair_c + rims + first_halos + first_copies + second_copies:
        copy.wait_send()
    x_out.wait()
    r_out.wait()


def emit(x_ref, r_ref, x_out, r_out, sem):
    first = pltpu.make_async_copy(x_ref, x_out, sem.at[0])
    second = pltpu.make_async_copy(r_ref, r_out, sem.at[1])
    first.start()
    second.start()
    first.wait()
    second.wait()


def local(old_fields, old_coef, held_slabs):
    slots = old_fields.shape[1]
    fields = old_fields.reshape(2, slots, NZ, 2, ROWS, NX)
    coef = old_coef.reshape(4, slots, NZ, 2, ROWS, NX)
    brick = (NZ, NY, NX)
    rounds = SWEEPS + 1
    dma = pltpu.SemaphoreType.DMA
    anywhere = pl.BlockSpec(memory_space=pl.ANY)
    hbm = pl.BlockSpec(memory_space=pltpu.HBM)
    held = pltpu.with_memory_space_constraint(jnp.transpose(held_slabs, (1, 2, 0)), pltpu.HBM)
    results = pl.pallas_call(
        kernel,
        out_shape=(jax.ShapeDtypeStruct(brick, F32), jax.ShapeDtypeStruct(brick, F32)),
        in_specs=[hbm, hbm, hbm],
        out_specs=(anywhere, anywhere),
        scratch_shapes=[
            pltpu.VMEM((2, slots, NZ, 2, ROWS, NX), F32),
            pltpu.VMEM((4, slots, NZ, 2, ROWS, NX), BF16),
            pltpu.VMEM((2, NZ, GROUPS, ROWS, NX), F32),
            pltpu.VMEM((4, NZ, GROUPS, ROWS, NX), BF16),
            pltpu.VMEM((2, NZ, GROUPS, ROWS, NX), F32),
            pltpu.VMEM((4, NZ, GROUPS, ROWS, NX), BF16),
            pltpu.VMEM((rounds, NZ + 2, NY, NX), F32),
            pltpu.VMEM(brick, F32),
            pltpu.VMEM(brick, F32),
            pltpu.VMEM(brick, F32),
            pltpu.VMEM((NZ + 1, NY, NX), F32),
            pltpu.VMEM(brick, F32),
            pltpu.VMEM((6, NZ, NY, NX), F32),
            pltpu.VMEM((2, NZ, ROWS, NX), F32),
            pltpu.VMEM((ROWS, LANES), F32),
            pltpu.VMEM(brick, F32),
            pltpu.VMEM(brick, F32),
            pltpu.VMEM(brick, F32),
            pltpu.VMEM(brick, F32),
            pltpu.VMEM(brick, F32),
            pltpu.VMEM((rounds, ROWS, LANES), F32),
            pltpu.VMEM((rounds, 2, NZ, 1, NX), F32),
            pltpu.VMEM((rounds, 2, ROWS, LANES), F32),
            pltpu.VMEM((rounds, 2, NZ, 1, NX), F32),
            pltpu.VMEM((ROWS, LANES), F32),
            pltpu.VMEM((NZ, 1, NX), F32),
            pltpu.VMEM((ROWS, LANES), F32),
            pltpu.VMEM((NZ, 1, NX), F32),
            pltpu.VMEM((3, ROWS, LANES), F32),
            pltpu.VMEM((2, 2, 3, NY, NX), F32),
            pltpu.VMEM((2, 2, 3, NY, NX), F32),
            pltpu.VMEM((2, 2, 3, NZ, 1, NX), F32),
            pltpu.VMEM((2, 2, 3, NZ, 1, NX), F32),
            pltpu.VMEM((2, 3, ROWS, LANES), F32),
            pltpu.VMEM((2, 2, 3, ROWS, LANES), F32),
            pltpu.VMEM((2, 2, 2, 2, 1, NX), F32),
            pltpu.VMEM((2, 2, 2, 2, 1, NX), F32),
            pltpu.VMEM((2, 3, ROWS, LANES), F32),
            pltpu.VMEM((2, 2, 2, ROWS, LANES), F32),
            pltpu.VMEM((2, 2, 2, 2, ROWS, LANES), F32),
            pltpu.VMEM((2, 2, 2, 1, NX), F32),
            pltpu.VMEM((2, 2, 1, NX), F32),
            pltpu.VMEM((3, ROWS, LANES), F32),
            pltpu.SMEM((1, 1, slots), jnp.int32),
            dma((6,)),
            dma((1,)),
            dma((6,)),
            dma((6,)),
            dma((rounds, 6)),
            dma((rounds, 6)),
            dma((3,)),
            dma((3,)),
            dma((2,)),
            dma((2, 24)),
            dma((2, 24)),
        ],
        compiler_params=pltpu.CompilerParams(
            collective_id=0, has_side_effects=True, vmem_limit_bytes=55767040
        ),
        name="smooth",
    )(fields, coef, held)
    return pl.pallas_call(
        emit,
        out_shape=(jax.ShapeDtypeStruct(brick, F32), jax.ShapeDtypeStruct(brick, F32)),
        in_specs=[anywhere, anywhere],
        out_specs=(hbm, hbm),
        scratch_shapes=[dma((2,))],
        compiler_params=pltpu.CompilerParams(vmem_limit_bytes=1 << 20),
        name="emit",
    )(*results)


def solution(mesh):
    in_specs = (
        P(None, "gy", "gz", None, "gx"),
        P(None, "gy", "gz", None, "gx"),
        P("gy", "gz", "gx"),
    )
    out_specs = (P("gz", "gy", "gx"), P("gz", "gy", "gx"))
    return jax.shard_map(local, mesh=mesh, in_specs=in_specs, out_specs=out_specs, check_vma=False)
```

```python
import functools
import jax
import jax.numpy as jnp
from jax import lax
from jax.experimental import pallas as pl
from jax.experimental.pallas import tpu as pltpu
from jax.sharding import PartitionSpec as P

SWEEPS = 4
NZ = 16
NY = 24
NX = 256
ROWS = 8
LANES = 128
GROUPS = NY // ROWS
MESH = pl.DeviceIdType.MESH
F32 = jnp.float32
BF16 = jnp.bfloat16


def chebyshev_weights(count):
    low_bound = 0.25
    high_bound = 2.0
    centre_value = 0.5 * (high_bound + low_bound)
    half_width = 0.5 * (high_bound - low_bound)
    ratio_value = centre_value / half_width
    damping = 1.0 / ratio_value
    first_list = [0.0]
    second_list = [1.0 / centre_value]
    for step_index in range(1, count):
        damping_next = 1.0 / (2.0 * ratio_value - damping)
        first_list.append(damping_next * damping)
        second_list.append(2.0 * damping_next / half_width)
        damping = damping_next
    return first_list, second_list


FIRST, SECOND = chebyshev_weights(SWEEPS)


def ring(axis):
    count = lax.axis_size(axis)
    me = lax.axis_index(axis)
    low = {axis: lax.rem(me + count - 1, count)}
    high = {axis: lax.rem(me + 1, count)}
    return low, high


def kernel(
    fields_hbm, coef_hbm, held_hbm, x_hbm, r_hbm,
    slots_f, slots_c, send_f, send_c, recv_f, recv_c,
    field, alpha, bx, by, bz, rhs, near, edge_y, edge_x, diag, inverse_ref, scaled, total, resid,
    pack, face_y, halo_x, halo_y, rim_pack, rim_face, rim_x, rim_y, beta_pack,
    sent_z, got_z, sent_y, got_y, sent_x, got_x, sent_yz, got_yz, sent_q, got_xz, got_xy, line_weight, line_fix, pack_weight,
    part_x, part_y, part_z, give_x, give_y, give_z, face_z, held_ref,
    load_sem, held_sem, pair_send, pair_recv, halo_send, halo_recv, rim_send, rim_recv, out_sem,
    both_send, both_recv, part_send, part_recv,
):
    group = lax.axis_index("gy")
    half = lax.rem(group, 2)
    first_slab = 3 * (group // 2)
    partner = {"gy": group + 1 - 2 * half}
    x_low, x_high = ring("gx")
    y_low, y_high = ring("gy")
    z_low, z_high = ring("gz")

    barrier = pltpu.get_barrier_semaphore()
    x_sides, y_sides, z_sides = (x_low, x_high), (y_low, y_high), (z_low, z_high)
    faces = [x_low, x_high, y_low, y_high, z_low, z_high]
    for neighbour in faces:
        pl.semaphore_signal(barrier, inc=1, device_id=neighbour, device_id_type=MESH)

    load_held = pltpu.make_async_copy(held_hbm, held_ref, held_sem.at[0])
    loads_f = [pltpu.make_async_copy(fields_hbm.at[c], slots_f.at[c], load_sem.at[c]) for c in range(2)]
    loads_c = [pltpu.make_async_copy(coef_hbm.at[c], slots_c.at[c], load_sem.at[2 + c]) for c in range(4)]
    load_held.start()
    loads_f[0].start()
    for c in (1, 2, 3, 0):
        loads_c[c].start()
    loads_f[1].start()
    load_held.wait()

    id0 = held_ref[0, 0, 0]
    id1 = held_ref[0, 0, 1]
    mine = [first_slab + (3 * half + g) // 2 for g in range(GROUPS)]
    theirs = [first_slab + (3 * (1 - half) + g) // 2 for g in range(GROUPS)]
    my_part = [lax.rem(half + g, 2) for g in range(GROUPS)]
    their_part = [lax.rem(1 - half + g, 2) for g in range(GROUPS)]

    row8 = lax.broadcasted_iota(jnp.int32, (ROWS, LANES), 0)
    row = lax.broadcasted_iota(jnp.int32, (NY, LANES), 0)
    lane = lax.broadcasted_iota(jnp.int32, (NY, LANES), 1)
    lane8 = lax.broadcasted_iota(jnp.int32, (ROWS, LANES), 1)
    end_row = row == NY - 1
    first_lane = lane == 0
    last_lane = lane == LANES - 1
    spots = lane8 // 2

    def copy_to(source, target, send_sem, recv_sem, device):
        return pltpu.make_async_remote_copy(
            src_ref=source, dst_ref=target, send_sem=send_sem, recv_sem=recv_sem,
            device_id=device, device_id_type=MESH,
        )

    pair_f = [copy_to(send_f.at[c], recv_f.at[c], pair_send.at[c], pair_recv.at[c], partner) for c in range(2)]
    pair_c = [
        copy_to(send_c.at[c], recv_c.at[c], pair_send.at[2 + c], pair_recv.at[2 + c], partner) for c in range(4)
    ]

    def halo_copies(k):
        return [
            copy_to(pack.at[k], halo_x.at[k, 1], halo_send.at[k, 0], halo_recv.at[k, 0], x_low),
            copy_to(pack.at[k], halo_x.at[k, 0], halo_send.at[k, 1], halo_recv.at[k, 1], x_high),
            copy_to(face_y.at[k, 0], halo_y.at[k, 1], halo_send.at[k, 2], halo_recv.at[k, 2], y_low),
            copy_to(face_y.at[k, 1], halo_y.at[k, 0], halo_send.at[k, 3], halo_recv.at[k, 3], y_high),
            copy_to(face_z.at[0], field.at[k, NZ + 1], halo_send.at[k, 4], halo_recv.at[k, 4], z_low),
            copy_to(face_z.at[1], field.at[k, 0], halo_send.at[k, 5], halo_recv.at[k, 5], z_high),
        ]

    first_halos = halo_copies(0)

    def numbered(r, first, moves):
        return [
            copy_to(source, target, both_send.at[r, first + i], both_recv.at[r, first + i], device)
            for i, (source, target, device) in enumerate(moves)
        ]

    def edge_copies(r):
        moves = []
        for a in range(2):
            for b in range(2):
                device = {**x_sides[a], **y_sides[b]}
                line = pl.ds(b * (ROWS - 1), 1)
                moves.append((sent_q.at[r, pl.ds(0, 2), line], got_xy.at[r, 1 - a, 1 - b, pl.ds(0, 2), line], device))
        for a in range(2):
            for b in range(2):
                device = {**x_sides[a], **z_sides[b]}
                moves.append((sent_q.at[r, 2], got_xz.at[r, 1 - a, 1 - b], device))
        for a in range(2):
            for b in range(2):
                moves.append((sent_yz.at[r, a, b], got_yz.at[r, 1 - a, 1 - b], {**z_sides[a], **y_sides[b]}))
        return numbered(r, 12, moves)

    def face_copies(r, first, part):
        moves = [(sent_x.at[r, part], got_x.at[r, 1 - a, part], x_sides[a]) for a in range(2)]
        moves += [(sent_y.at[r, a, part], got_y.at[r, 1 - a, part], y_sides[a]) for a in range(2)]
        moves += [(sent_z.at[r, a, part], got_z.at[r, 1 - a, part], z_sides[a]) for a in range(2)]
        return numbered(r, first, moves)

    rims = [
        copy_to(rim_pack, rim_x, rim_send.at[0], rim_recv.at[0], x_low),
        copy_to(rim_face, rim_y, rim_send.at[1], rim_recv.at[1], y_low),
        copy_to(face_z.at[2], bz.at[NZ], rim_send.at[2], rim_recv.at[2], z_low),
    ]

    def planes(body, carry=0, first=0, last=NZ):
        return lax.fori_loop(first, last, body, carry, unroll=True)

    def prepare(slots, out):
        def body(z, carry):
            for g in range(GROUPS):
                out[z, g] = lax.select(id0 == theirs[g], slots[0, z, their_part[g]], slots[1, z, their_part[g]])
            return carry

        planes(body)

    def assembled(slots, received, z, g):
        return lax.select(
            id0 == mine[g],
            slots[0, z, my_part[g]],
            lax.select(id1 == mine[g], slots[1, z, my_part[g]], received[z, g]),
        ).astype(F32)

    def packed(z, g, tile_low, tile_high, carry):
        return packed_at(z * GROUPS + g, tile_low, tile_high, carry)

    def packed_at(spot, tile_low, tile_high, carry):
        both = jnp.where(lane8 == 0, tile_low, tile_high)
        moved = pltpu.roll(both, 2 * spot + 1, 1)
        return jnp.where(spots == spot, moved, carry)

    region = [first_slab + g // 2 for g in range(2 * GROUPS)]

    def chosen(slab, first, second):
        zero = jnp.zeros(first.shape, first.dtype)
        return lax.select(id0 == slab, first, lax.select(id1 == slab, second, zero)).astype(F32)

    def part_columns(slots, index):
        def body(z, carry):
            for h in range(2):
                value = carry[h]
                for g in range(GROUPS):
                    at = GROUPS * h + g
                    tile = chosen(region[at], slots[0, z, at % 2], slots[1, z, at % 2])
                    value = packed(z, g, tile[:, :LANES], tile[:, LANES:], value)
                carry = (value, carry[1]) if h == 0 else (carry[0], value)
            return carry

        part_x[0, index], part_x[1, index] = planes(body, (zero_pack, zero_pack))

    def part_planes(slots, z, index):
        for at in range(2 * GROUPS):
            rows = slice((at % GROUPS) * ROWS, (at % GROUPS + 1) * ROWS)
            part_z[at // GROUPS, index, rows, :] = chosen(region[at], slots[0, z, at % 2], slots[1, z, at % 2])

    def part_rows(slots, side, index):
        def body(z, carry):
            for h in range(2):
                at = GROUPS * h + side * (GROUPS - 1)
                line = slice(side * (ROWS - 1), side * (ROWS - 1) + 1)
                part_y[h, index, z] = chosen(region[at], slots[0, z, at % 2, line], slots[1, z, at % 2, line])
            return carry

        planes(body)

    gives = [
        copy_to(part_x.at[1 - half], give_x, part_send.at[0], part_recv.at[0], partner),
        copy_to(part_y.at[1 - half], give_y, part_send.at[1], part_recv.at[1], partner),
        copy_to(part_z.at[1 - half], give_z, part_send.at[2], part_recv.at[2], partner),
    ]
    zero_pack = jnp.zeros((ROWS, LANES), F32)

    def plain(slots, received, out, shift=0):
        def body(z, carry):
            for g in range(GROUPS):
                out[z + shift, g * ROWS : (g + 1) * ROWS, :] = assembled(slots, received, z, g)
            return carry

        planes(body)

    loads_f[0].wait()
    part_columns(slots_f.at[0], 0)
    part_planes(slots_f.at[0], 0, 0)
    part_planes(slots_f.at[0], NZ - 1, 1)
    part_rows(slots_f.at[0], 0, 0)
    part_rows(slots_f.at[0], 1, 1)
    loads_c[1].wait()
    part_columns(slots_c.at[1], 1)
    loads_c[2].wait()
    part_rows(slots_c.at[2], 0, 2)
    loads_c[3].wait()
    part_planes(slots_c.at[3], 0, 2)
    pl.semaphore_wait(barrier, len(faces))
    for copy in gives:
        copy.start()
    gives[0].wait_recv()
    pack[0] = part_x[half, 0] + give_x[0]
    rim_pack[...] = part_x[half, 1] + give_x[1]
    first_halos[0].start()
    first_halos[1].start()
    rims[0].start()
    gives[1].wait_recv()
    for b in range(2):
        face_y[0, b] = part_y[half, b] + give_y[b]
    rim_face[...] = part_y[half, 2] + give_y[2]
    first_halos[2].start()
    first_halos[3].start()
    rims[1].start()
    gives[2].wait_recv()
    for i in range(3):
        face_z[i] = part_z[half, i] + give_z[i]
    rims[2].start()
    first_halos[4].start()
    first_halos[5].start()
    prepare(slots_f.at[0], send_f.at[0])
    pair_f[0].start()
    for c in (1, 2, 3, 0):
        if c == 0:
            loads_c[c].wait()
        prepare(slots_c.at[c], send_c.at[c])
        pair_c[c].start()
    loads_f[1].wait()
    prepare(slots_f.at[1], send_f.at[1])
    pair_f[1].start()
    pair_f[0].wait_recv()
    plain(slots_f.at[0], recv_f.at[0], field.at[0], 1)
    for c, out in ((1, bx), (2, by), (3, bz), (0, alpha)):
        pair_c[c].wait_recv()
        plain(slots_c.at[c], recv_c.at[c], out)
    pair_f[1].wait_recv()
    plain(slots_f.at[1], recv_f.at[1], rhs)
    for copy in rims:
        copy.wait_recv()

    halves = (slice(0, LANES), slice(LANES, NX))
    group_rows = [slice(g * ROWS, (g + 1) * ROWS) for g in range(GROUPS)]
    rim_values = rim_x[...]

    def scale_body(z, carry):
        low_rolled = pltpu.roll(bx[z, :, :LANES], LANES - 1, 1)
        high_rolled = pltpu.roll(bx[z, :, LANES:], LANES - 1, 1)
        edge = jnp.concatenate(
            [pltpu.roll(rim_values, 126 - 2 * (z * GROUPS + g), 1) for g in range(GROUPS)], axis=0
        )
        upper_x = (jnp.where(last_lane, high_rolled, low_rolled), jnp.where(last_lane, edge, high_rolled))
        before = []
        after = []
        inverses = []
        uppers = []
        for j, part in enumerate(halves):
            here_y = by[z, :, part]
            upper_y = jnp.where(
                end_row, jnp.broadcast_to(rim_y[z, :, part], (NY, LANES)), pltpu.roll(here_y, NY - 1, 0)
            )
            faces = [bx[z, :, part], upper_x[j], here_y, upper_y, bz[z, :, part], bz[z + 1, :, part]]
            centre = alpha[z, :, part]
            for face in faces:
                centre = centre + face
            inverse = 1.0 / centre
            inverses.append(inverse)
            inverse_ref[z, :, part] = inverse
            sent_y[0, 0, 2, z, :, part] = inverse[:1]
            sent_y[0, 1, 2, z, :, part] = inverse[NY - 1 :]
            uppers.append(upper_y[NY - ROWS :])
            diag[z, :, part] = centre
            scaled[z, :, part] = inverse * rhs[z, :, part]
            weights = [inverse * face for face in faces]
            before.append(weights[0])
            after.append(weights[1])
            if j == 0:
                weights[0] = jnp.where(first_lane, 0.0, weights[0])
            else:
                weights[1] = jnp.where(last_lane, 0.0, weights[1])
            edge_y[0, z, :, part] = jnp.where(row8 == 0, weights[2][:ROWS], 0.0)
            edge_y[1, z, :, part] = jnp.where(row8 == ROWS - 1, weights[3][NY - ROWS :], 0.0)
            weights[2] = jnp.where(row == 0, 0.0, weights[2])
            weights[3] = jnp.where(end_row, 0.0, weights[3])
            for i, weight in enumerate(weights):
                near[i, z, :, part] = weight
        edge_pack, inverse_pack, y_pack = carry
        for g, rows in enumerate(group_rows):
            edge_pack = packed(z, g, before[0][rows], after[1][rows], edge_pack)
            inverse_pack = packed(z, g, inverses[0][rows], inverses[1][rows], inverse_pack)
        y_pack = packed(z, 0, by[z, :ROWS, :LANES], by[z, :ROWS, LANES:], y_pack)
        y_pack = packed(z, GROUPS - 1, uppers[0], uppers[1], y_pack)
        return edge_pack, inverse_pack, y_pack

    edge_x[...], sent_x[0, 2], y_pack = planes(scale_body, (zero_pack, zero_pack, zero_pack))
    odd = lane8 - 2 * spots == 1
    spot_group = spots - GROUPS * (spots // GROUPS)
    low_rim = (spot_group == 0) & (row8 == 0)
    high_rim = (spot_group == GROUPS - 1) & (row8 == ROWS - 1)
    low_spots = spots < GROUPS
    high_spots = (spots >= GROUPS * (NZ - 1)) & (spots < GROUPS * NZ)
    z_pack = zero_pack
    for g, rows in enumerate(group_rows):
        z_pack = packed(0, g, bz[0, rows, :LANES], bz[0, rows, LANES:], z_pack)
        z_pack = packed(NZ - 1, g, bz[NZ, rows, :LANES], bz[NZ, rows, LANES:], z_pack)
    beta_pack[0] = jnp.where(low_rim | high_rim, y_pack, 0.0)
    beta_pack[1] = jnp.where(odd, rim_pack[...], pltpu.roll(rim_values, LANES - 1, 1))
    beta_pack[2] = z_pack
    sent_z[0, 0, 2] = inverse_ref[0]
    sent_z[0, 1, 2] = inverse_ref[NZ - 1]

    def swapped(value):
        return jnp.where(odd, pltpu.roll(value, 1, 1), pltpu.roll(value, LANES - 1, 1))

    def halo_z_of(k, side):
        return got_z.at[k // 2, side, 0] if k % 2 else field.at[k, side * (NZ + 1)]

    def halo_y_of(k, side):
        return got_y.at[k // 2, side, 0] if k % 2 else halo_y.at[k, side]

    def inner(k, z, first, last, carry):
        low, high = field[k, z + 1, :, :LANES], field[k, z + 1, :, LANES:]
        low_after, high_after = pltpu.roll(low, LANES - 1, 1), pltpu.roll(high, LANES - 1, 1)
        low_before, high_before = pltpu.roll(low, 1, 1), pltpu.roll(high, 1, 1)
        x_before = (low_before, jnp.where(first_lane, low_before, high_before))
        x_after = (jnp.where(last_lane, high_after, low_after), high_after)
        values = []
        for j, part in enumerate(halves):
            here = (low, high)[j]
            value = scaled[z, :, part] - here
            value = value + near[0, z, :, part] * x_before[j] + near[1, z, :, part] * x_after[j]
            value = value + near[2, z, :, part] * pltpu.roll(here, 1, 0)
            value = value + near[3, z, :, part] * pltpu.roll(here, NY - 1, 0)
            if not first:
                value = value + near[4, z, :, part] * field[k, z, :, part]
            if not last:
                value = value + near[5, z, :, part] * field[k, z + 2, :, part]
            scaled[z, :, part] = value
            values.append(value)
            if k % 2:
                ahead = SECOND[k] * value + FIRST[k] * here
                sent_y[k // 2, 0, 1, z, :, part] = ahead[:1]
                sent_y[k // 2, 1, 1, z, :, part] = ahead[NY - 1 :]
                if first:
                    sent_z[k // 2, 0, 1, :, part] = ahead
                if last:
                    sent_z[k // 2, 1, 1, :, part] = ahead
        if k % 2:
            for g, rows in enumerate(group_rows):
                carry = packed(z, g, values[0][rows], values[1][rows], carry)
        return carry

    def outer(k, z, first, last, sides, carry):
        fresh = [[], []]
        sending = k % 2 == 0 and k < SWEEPS
        for g, rows in enumerate(group_rows):
            moved = pltpu.roll(sides, LANES - 1 - 2 * (z * GROUPS + g), 1)
            for j, part in enumerate(halves):
                value = scaled[z, rows, part] + jnp.where(lane8 == (0, LANES - 1)[j], moved, 0.0)
                if g == 0:
                    value = value + edge_y[0, z, :, part] * jnp.broadcast_to(
                        halo_y_of(k, 0)[z, :, part], (ROWS, LANES)
                    )
                if g == GROUPS - 1:
                    value = value + edge_y[1, z, :, part] * jnp.broadcast_to(
                        halo_y_of(k, 1)[z, :, part], (ROWS, LANES)
                    )
                if first:
                    value = value + near[4, z, rows, part] * halo_z_of(k, 0)[rows, part]
                if last:
                    value = value + near[5, z, rows, part] * halo_z_of(k, 1)[rows, part]
                for b in range(2):
                    if k and k % 2 == 0 and (first or last) and g == b * (GROUPS - 1):
                        line = jnp.broadcast_to(line_fix[0 if first else 1, b, :, part], (ROWS, LANES))
                        value = value + jnp.where(row8 == b * (ROWS - 1), line, 0.0)
                if k == SWEEPS:
                    resid[z, rows, part] = diag[z, rows, part] * value
                    continue
                scaled[z, rows, part] = value
                step = SECOND[k] * value
                if k > 0:
                    step = step + FIRST[k] * field[k, z + 1, rows, part]
                field[k + 1, z + 1, rows, part] = step
                if k == SWEEPS - 1:
                    total[z, rows, part] = total[z, rows, part] + step
                if not sending:
                    continue
                if first:
                    sent_z[k // 2, 0, 0, rows, part] = step
                if last:
                    sent_z[k // 2, 1, 0, rows, part] = step
                if g == 0:
                    sent_y[k // 2, 0, 0, z, :, part] = step[:1]
                if g == GROUPS - 1:
                    sent_y[k // 2, 1, 0, z, :, part] = step[ROWS - 1 :]
                fresh[j].append(step)
            if sending:
                carry = packed(z, g, fresh[0][g], fresh[1][g], carry)
        return carry

    def run_inner(k):
        carry = inner(k, 0, True, False, zero_pack)
        carry = planes(lambda z, carry: inner(k, z, False, False, carry), carry, 1, NZ - 1)
        return inner(k, NZ - 1, False, True, carry)

    def run_outer(k, x_halo, extra=0.0):
        sides = edge_x[...] * swapped(x_halo) + extra
        carry = outer(k, 0, True, False, sides, zero_pack)
        carry = planes(lambda z, carry: outer(k, z, False, False, sides, carry), carry, 1, NZ - 1)
        return outer(k, NZ - 1, False, True, sides, carry)

    def either(ref_low, ref_high):
        return jnp.where(odd, ref_high, ref_low)

    def ahead(r, k):
        for side in range(2):
            own = side * (NZ - 1)
            for part in halves:
                value = got_z[0, side, 2, :, part] * (bz[side * NZ, :, part] * field[k, own + 1, :, part])
                field[k + 1, side * (NZ + 1), :, part] = got_z[r, side, 1, :, part] + SECOND[k] * value
            face = (rim_face, rim_y)[side]
            value = got_y[0, side, 2] * (face[...] * sent_y[r, side, 0])
            halo_y[k + 1, side] = got_y[r, side, 1] + SECOND[k] * value
        value = either(got_x[0, 0, 2], got_x[0, 1, 2]) * swapped(sent_q[r, 1])
        return either(got_x[r, 0, 1], got_x[r, 1, 1]) + SECOND[k] * value

    def weigh_edges():
        y_pack = zero_pack
        z_pack = zero_pack
        for a in range(2):
            z = a * (NZ - 1)
            tiles = [near[4 + a, z, :, part] * got_z[0, a, 2, :, part] for part in halves]
            for g, rows in enumerate(group_rows):
                z_pack = packed(z, g, tiles[0][rows], tiles[1][rows], z_pack)
            for b in range(2):
                at = b * (NY - 1)
                low = b * (ROWS - 1)
                line_weight[a, b, 0] = near[4 + a, z, at : at + 1, :] * got_z[0, a, 2, at : at + 1, :]
                line_weight[a, b, 1] = edge_y[b, z, low : low + 1, :] * got_y[0, b, 2, z]

        def body(z, y_pack):
            for b in range(2):
                tiles = [
                    edge_y[b, z, :, part] * jnp.broadcast_to(got_y[0, b, 2, z, :, part], (ROWS, LANES))
                    for part in halves
                ]
                y_pack = packed(z, b * (GROUPS - 1), tiles[0], tiles[1], y_pack)
            return y_pack

        pack_weight[0] = edge_x[...] * swapped(either(got_x[0, 0, 2], got_x[0, 1, 2]))
        pack_weight[1] = planes(body, y_pack)
        pack_weight[2] = z_pack

    def edge_fix(r, k):
        for a in range(2):
            for b in range(2):
                value = line_weight[a, b, 0] * got_yz[r, a, b, 0] + line_weight[a, b, 1] * got_yz[r, a, b, 1]
                line_fix[a, b] = SECOND[k] * value

        def from_y(i):
            below = swapped(either(got_xy[r, 0, 0, i], got_xy[r, 1, 0, i]))
            above = swapped(either(got_xy[r, 0, 1, i], got_xy[r, 1, 1, i]))
            shift = 2 * (GROUPS - 1)
            below = jnp.where(low_rim, pltpu.roll(pltpu.roll(below, 1, 0), LANES - shift, 1), 0.0)
            return below + jnp.where(high_rim, pltpu.roll(pltpu.roll(above, ROWS - 1, 0), shift, 1), 0.0)

        def from_z(i):
            below = swapped(either(got_xz[r, 0, 0], got_xz[r, 1, 0]))
            above = swapped(either(got_xz[r, 0, 1], got_xz[r, 1, 1]))
            shift = 2 * GROUPS * (NZ - 1)
            back = (1 - i) * ROWS
            below = jnp.where(low_spots, pltpu.roll(below, LANES - shift - back, 1), 0.0)
            return below + jnp.where(high_spots, pltpu.roll(above, shift - back, 1), 0.0)

        value = pack_weight[0] * (from_y(0) + from_z(1))
        return SECOND[k] * (value + pack_weight[1] * from_y(1) + pack_weight[2] * from_z(0))

    def apply_two(r):
        k = 2 * r + 1
        own = sent_x[r, 0]
        sent_q[r, 0] = beta_pack[0] * own
        across = beta_pack[1] * own
        sent_q[r, 1] = across
        ends = pltpu.roll(jnp.where(low_spots | high_spots, across, 0.0), ROWS, 1)
        sent_q[r, 2] = beta_pack[2] * own + ends
        for a in range(2):
            z = a * (NZ - 1)
            for b in range(2):
                line = sent_y[r, b, 0, z]
                at = b * (NY - 1)
                sent_yz[r, a, b, 0] = (rim_face, rim_y)[b][z] * line
                sent_yz[r, a, b, 1] = bz[a * NZ, at : at + 1, :] * line
        near_copies = face_copies(r, 0, pl.ds(0, 1))
        far_copies = edge_copies(r)
        for copy in far_copies[:8] + near_copies + far_copies[8:]:
            copy.start()

        sent_x[r, 1] = SECOND[k] * run_inner(k) + FIRST[k] * own
        ahead_copies = face_copies(r, 24, pl.ds(1, 1))
        if r == 0:
            ahead_copies += face_copies(r, 6, pl.ds(2, 1))
        for copy in ahead_copies:
            copy.start()

        def sum_body(z, carry):
            for part in halves:
                if r == 0:
                    total[z, :, part] = field[0, z + 1, :, part] + field[1, z + 1, :, part]
                else:
                    total[z, :, part] = (
                        total[z, :, part] + field[2, z + 1, :, part] + field[3, z + 1, :, part]
                    )
            return carry

        planes(sum_body)
        for copy in near_copies:
            copy.wait_recv()
        run_outer(k, either(got_x[r, 0, 0], got_x[r, 1, 0]))
        if k == SWEEPS - 1:
            x_out.start()
        for copy in ahead_copies:
            copy.wait_recv()
        x_halo = ahead(r, k)
        if r == 0:
            weigh_edges()
        run_inner(k + 1)
        for copy in far_copies:
            copy.wait_recv()
        return near_copies + far_copies + ahead_copies, run_outer(k + 1, x_halo, edge_fix(r, k))

    x_out = pltpu.make_async_copy(total, x_hbm, out_sem.at[0])
    run_inner(0)
    for copy in first_halos:
        copy.wait_recv()
    sent_x[0, 0] = run_outer(0, either(halo_x[0, 0], halo_x[0, 1]))
    first_copies, sent_x[1, 0] = apply_two(0)
    second_copies, unused = apply_two(1)
    r_out = pltpu.make_async_copy(resid, r_hbm, out_sem.at[1])
    r_out.start()
    for copy in gives + pair_f + pair_c + rims + first_halos + first_copies + second_copies:
        copy.wait_send()
    x_out.wait()
    r_out.wait()


def emit(x_ref, r_ref, x_out, r_out, sem):
    first = pltpu.make_async_copy(x_ref, x_out, sem.at[0])
    second = pltpu.make_async_copy(r_ref, r_out, sem.at[1])
    first.start()
    second.start()
    first.wait()
    second.wait()


def local(old_fields, old_coef, held_slabs):
    slots = old_fields.shape[1]
    fields = old_fields.reshape(2, slots, NZ, 2, ROWS, NX)
    coef = old_coef.reshape(4, slots, NZ, 2, ROWS, NX)
    brick = (NZ, NY, NX)
    rounds = SWEEPS + 1
    dma = pltpu.SemaphoreType.DMA
    anywhere = pl.BlockSpec(memory_space=pl.ANY)
    hbm = pl.BlockSpec(memory_space=pltpu.HBM)
    held = pltpu.with_memory_space_constraint(jnp.transpose(held_slabs, (1, 2, 0)), pltpu.HBM)
    results = pl.pallas_call(
        kernel,
        out_shape=(jax.ShapeDtypeStruct(brick, F32), jax.ShapeDtypeStruct(brick, F32)),
        in_specs=[hbm, hbm, hbm],
        out_specs=(anywhere, anywhere),
        scratch_shapes=[
            pltpu.VMEM((2, slots, NZ, 2, ROWS, NX), F32),
            pltpu.VMEM((4, slots, NZ, 2, ROWS, NX), BF16),
            pltpu.VMEM((2, NZ, GROUPS, ROWS, NX), F32),
            pltpu.VMEM((4, NZ, GROUPS, ROWS, NX), BF16),
            pltpu.VMEM((2, NZ, GROUPS, ROWS, NX), F32),
            pltpu.VMEM((4, NZ, GROUPS, ROWS, NX), BF16),
            pltpu.VMEM((rounds, NZ + 2, NY, NX), F32),
            pltpu.VMEM(brick, F32),
            pltpu.VMEM(brick, F32),
            pltpu.VMEM(brick, F32),
            pltpu.VMEM((NZ + 1, NY, NX), F32),
            pltpu.VMEM(brick, F32),
            pltpu.VMEM((6, NZ, NY, NX), F32),
            pltpu.VMEM((2, NZ, ROWS, NX), F32),
            pltpu.VMEM((ROWS, LANES), F32),
            pltpu.VMEM(brick, F32),
            pltpu.VMEM(brick, F32),
            pltpu.VMEM(brick, F32),
            pltpu.VMEM(brick, F32),
            pltpu.VMEM(brick, F32),
            pltpu.VMEM((rounds, ROWS, LANES), F32),
            pltpu.VMEM((rounds, 2, NZ, 1, NX), F32),
            pltpu.VMEM((rounds, 2, ROWS, LANES), F32),
            pltpu.VMEM((rounds, 2, NZ, 1, NX), F32),
            pltpu.VMEM((ROWS, LANES), F32),
            pltpu.VMEM((NZ, 1, NX), F32),
            pltpu.VMEM((ROWS, LANES), F32),
            pltpu.VMEM((NZ, 1, NX), F32),
            pltpu.VMEM((3, ROWS, LANES), F32),
            pltpu.VMEM((2, 2, 3, NY, NX), F32),
            pltpu.VMEM((2, 2, 3, NY, NX), F32),
            pltpu.VMEM((2, 2, 3, NZ, 1, NX), F32),
            pltpu.VMEM((2, 2, 3, NZ, 1, NX), F32),
            pltpu.VMEM((2, 3, ROWS, LANES), F32),
            pltpu.VMEM((2, 2, 3, ROWS, LANES), F32),
            pltpu.VMEM((2, 2, 2, 2, 1, NX), F32),
            pltpu.VMEM((2, 2, 2, 2, 1, NX), F32),
            pltpu.VMEM((2, 3, ROWS, LANES), F32),
            pltpu.VMEM((2, 2, 2, ROWS, LANES), F32),
            pltpu.VMEM((2, 2, 2, 2, ROWS, LANES), F32),
            pltpu.VMEM((2, 2, 2, 1, NX), F32),
            pltpu.VMEM((2, 2, 1, NX), F32),
            pltpu.VMEM((3, ROWS, LANES), F32),
            pltpu.VMEM((2, 2, ROWS, LANES), F32),
            pltpu.VMEM((2, 3, NZ, 1, NX), F32),
            pltpu.VMEM((2, 3, NY, NX), F32),
            pltpu.VMEM((2, ROWS, LANES), F32),
            pltpu.VMEM((3, NZ, 1, NX), F32),
            pltpu.VMEM((3, NY, NX), F32),
            pltpu.VMEM((3, NY, NX), F32),
            pltpu.SMEM((1, 1, slots), jnp.int32),
            dma((6,)),
            dma((1,)),
            dma((6,)),
            dma((6,)),
            dma((rounds, 6)),
            dma((rounds, 6)),
            dma((3,)),
            dma((3,)),
            dma((2,)),
            dma((2, 30)),
            dma((2, 30)),
            dma((3,)),
            dma((3,)),
        ],
        compiler_params=pltpu.CompilerParams(
            collective_id=0, has_side_effects=True, vmem_limit_bytes=55767040
        ),
        name="smooth",
    )(fields, coef, held)
    return pl.pallas_call(
        emit,
        out_shape=(jax.ShapeDtypeStruct(brick, F32), jax.ShapeDtypeStruct(brick, F32)),
        in_specs=[anywhere, anywhere],
        out_specs=(hbm, hbm),
        scratch_shapes=[dma((2,))],
        compiler_params=pltpu.CompilerParams(vmem_limit_bytes=1 << 20),
        name="emit",
    )(*results)


def solution(mesh):
    in_specs = (
        P(None, "gy", "gz", None, "gx"),
        P(None, "gy", "gz", None, "gx"),
        P("gy", "gz", "gx"),
    )
    out_specs = (P("gz", "gy", "gx"), P("gz", "gy", "gx"))
    return jax.shard_map(local, mesh=mesh, in_specs=in_specs, out_specs=out_specs, check_vma=False)
```

```python
import functools
import jax
import jax.numpy as jnp
from jax import lax
from jax.experimental import pallas as pl
from jax.experimental.pallas import tpu as pltpu
from jax.sharding import PartitionSpec as P

SWEEPS = 4
NZ = 16
NY = 24
NX = 256
ROWS = 8
LANES = 128
GROUPS = NY // ROWS
MESH = pl.DeviceIdType.MESH
F32 = jnp.float32
BF16 = jnp.bfloat16


def chebyshev_weights(count):
    low_bound = 0.25
    high_bound = 2.0
    centre_value = 0.5 * (high_bound + low_bound)
    half_width = 0.5 * (high_bound - low_bound)
    ratio_value = centre_value / half_width
    damping = 1.0 / ratio_value
    first_list = [0.0]
    second_list = [1.0 / centre_value]
    for step_index in range(1, count):
        damping_next = 1.0 / (2.0 * ratio_value - damping)
        first_list.append(damping_next * damping)
        second_list.append(2.0 * damping_next / half_width)
        damping = damping_next
    return first_list, second_list


FIRST, SECOND = chebyshev_weights(SWEEPS)


def ring(axis):
    count = lax.axis_size(axis)
    me = lax.axis_index(axis)
    low = {axis: lax.rem(me + count - 1, count)}
    high = {axis: lax.rem(me + 1, count)}
    return low, high


def kernel(
    fields_hbm, coef_hbm, held_hbm, x_hbm, r_hbm,
    slots_f, slots_c, send_f, send_c, recv_f, recv_c,
    field, alpha, bx, by, bz, rhs, near, edge_y, edge_x, diag, inverse_ref, scaled, total, resid,
    pack, face_y, halo_x, halo_y, rim_pack, rim_face, rim_x, rim_y, beta_pack,
    sent_z, got_z, sent_y, got_y, sent_x, got_x, sent_yz, got_yz, sent_q, got_xz, got_xy, line_weight, line_fix, pack_weight,
    part_x, part_y, part_z, give_x, give_y, give_z, face_z, held_ref,
    load_sem, held_sem, pair_send, pair_recv, halo_send, halo_recv, rim_send, rim_recv, out_sem,
    both_send, both_recv, part_send, part_recv,
):
    group = lax.axis_index("gy")
    half = lax.rem(group, 2)
    first_slab = 3 * (group // 2)
    partner = {"gy": group + 1 - 2 * half}
    x_low, x_high = ring("gx")
    y_low, y_high = ring("gy")
    z_low, z_high = ring("gz")

    barrier = pltpu.get_barrier_semaphore()
    x_sides, y_sides, z_sides = (x_low, x_high), (y_low, y_high), (z_low, z_high)
    faces = [x_low, x_high, y_low, y_high, z_low, z_high]
    for neighbour in faces:
        pl.semaphore_signal(barrier, inc=1, device_id=neighbour, device_id_type=MESH)

    load_held = pltpu.make_async_copy(held_hbm, held_ref, held_sem.at[0])
    loads_f = [pltpu.make_async_copy(fields_hbm.at[c], slots_f.at[c], load_sem.at[c]) for c in range(2)]
    loads_c = [pltpu.make_async_copy(coef_hbm.at[c], slots_c.at[c], load_sem.at[2 + c]) for c in range(4)]
    load_held.start()
    loads_f[0].start()
    for c in (1, 2, 3, 0):
        loads_c[c].start()
    loads_f[1].start()
    load_held.wait()

    id0 = held_ref[0, 0, 0]
    id1 = held_ref[0, 0, 1]
    mine = [first_slab + (3 * half + g) // 2 for g in range(GROUPS)]
    theirs = [first_slab + (3 * (1 - half) + g) // 2 for g in range(GROUPS)]
    my_part = [lax.rem(half + g, 2) for g in range(GROUPS)]
    their_part = [lax.rem(1 - half + g, 2) for g in range(GROUPS)]

    row8 = lax.broadcasted_iota(jnp.int32, (ROWS, LANES), 0)
    row = lax.broadcasted_iota(jnp.int32, (NY, LANES), 0)
    lane = lax.broadcasted_iota(jnp.int32, (NY, LANES), 1)
    lane8 = lax.broadcasted_iota(jnp.int32, (ROWS, LANES), 1)
    end_row = row == NY - 1
    first_lane = lane == 0
    last_lane = lane == LANES - 1
    spots = lane8 // 2

    def copy_to(source, target, send_sem, recv_sem, device):
        return pltpu.make_async_remote_copy(
            src_ref=source, dst_ref=target, send_sem=send_sem, recv_sem=recv_sem,
            device_id=device, device_id_type=MESH,
        )

    pair_f = [copy_to(send_f.at[c], recv_f.at[c], pair_send.at[c], pair_recv.at[c], partner) for c in range(2)]
    pair_c = [
        copy_to(send_c.at[c], recv_c.at[c], pair_send.at[2 + c], pair_recv.at[2 + c], partner) for c in range(4)
    ]

    def halo_copies(k):
        return [
            copy_to(pack.at[k], halo_x.at[k, 1], halo_send.at[k, 0], halo_recv.at[k, 0], x_low),
            copy_to(pack.at[k], halo_x.at[k, 0], halo_send.at[k, 1], halo_recv.at[k, 1], x_high),
            copy_to(face_y.at[k, 0], halo_y.at[k, 1], halo_send.at[k, 2], halo_recv.at[k, 2], y_low),
            copy_to(face_y.at[k, 1], halo_y.at[k, 0], halo_send.at[k, 3], halo_recv.at[k, 3], y_high),
            copy_to(face_z.at[0], field.at[k, NZ + 1], halo_send.at[k, 4], halo_recv.at[k, 4], z_low),
            copy_to(face_z.at[1], field.at[k, 0], halo_send.at[k, 5], halo_recv.at[k, 5], z_high),
        ]

    first_halos = halo_copies(0)

    def numbered(r, first, moves):
        return [
            copy_to(source, target, both_send.at[r, first + i], both_recv.at[r, first + i], device)
            for i, (source, target, device) in enumerate(moves)
        ]

    def edge_copies(r):
        moves = []
        for a in range(2):
            for b in range(2):
                device = {**x_sides[a], **y_sides[b]}
                line = pl.ds(b * (ROWS - 1), 1)
                moves.append((sent_q.at[r, pl.ds(0, 2), line], got_xy.at[r, 1 - a, 1 - b, pl.ds(0, 2), line], device))
        for a in range(2):
            for b in range(2):
                device = {**x_sides[a], **z_sides[b]}
                moves.append((sent_q.at[r, 2], got_xz.at[r, 1 - a, 1 - b], device))
        for a in range(2):
            for b in range(2):
                moves.append((sent_yz.at[r, a, b], got_yz.at[r, 1 - a, 1 - b], {**z_sides[a], **y_sides[b]}))
        return numbered(r, 12, moves)

    def face_copies(r, first, part):
        moves = [(sent_x.at[r, part], got_x.at[r, 1 - a, part], x_sides[a]) for a in range(2)]
        moves += [(sent_y.at[r, a, part], got_y.at[r, 1 - a, part], y_sides[a]) for a in range(2)]
        moves += [(sent_z.at[r, a, part], got_z.at[r, 1 - a, part], z_sides[a]) for a in range(2)]
        return numbered(r, first, moves)

    rims = [
        copy_to(rim_pack, rim_x, rim_send.at[0], rim_recv.at[0], x_low),
        copy_to(rim_face, rim_y, rim_send.at[1], rim_recv.at[1], y_low),
        copy_to(face_z.at[2], bz.at[NZ], rim_send.at[2], rim_recv.at[2], z_low),
    ]

    def planes(body, carry=0, first=0, last=NZ):
        return lax.fori_loop(first, last, body, carry, unroll=True)

    def prepare(slots, out):
        def body(z, carry):
            for g in range(GROUPS):
                out[z, g] = lax.select(id0 == theirs[g], slots[0, z, their_part[g]], slots[1, z, their_part[g]])
            return carry

        planes(body)

    def assembled(slots, received, z, g):
        return lax.select(
            id0 == mine[g],
            slots[0, z, my_part[g]],
            lax.select(id1 == mine[g], slots[1, z, my_part[g]], received[z, g]),
        ).astype(F32)

    def packed(z, g, tile_low, tile_high, carry):
        return packed_at(z * GROUPS + g, tile_low, tile_high, carry)

    def packed_at(spot, tile_low, tile_high, carry):
        both = jnp.where(lane8 == 0, tile_low, tile_high)
        moved = pltpu.roll(both, 2 * spot + 1, 1)
        return jnp.where(spots == spot, moved, carry)

    region = [first_slab + g // 2 for g in range(2 * GROUPS)]

    def chosen(slab, first, second):
        zero = jnp.zeros(first.shape, first.dtype)
        return lax.select(id0 == slab, first, lax.select(id1 == slab, second, zero)).astype(F32)

    def part_columns(slots, index):
        def body(z, carry):
            for h in range(2):
                value = carry[h]
                for g in range(GROUPS):
                    at = GROUPS * h + g
                    tile = chosen(region[at], slots[0, z, at % 2], slots[1, z, at % 2])
                    value = packed(z, g, tile[:, :LANES], tile[:, LANES:], value)
                carry = (value, carry[1]) if h == 0 else (carry[0], value)
            return carry

        part_x[0, index], part_x[1, index] = planes(body, (zero_pack, zero_pack))

    def part_planes(slots, z, index):
        for at in range(2 * GROUPS):
            rows = slice((at % GROUPS) * ROWS, (at % GROUPS + 1) * ROWS)
            part_z[at // GROUPS, index, rows, :] = chosen(region[at], slots[0, z, at % 2], slots[1, z, at % 2])

    def part_rows(slots, side, index):
        def body(z, carry):
            for h in range(2):
                at = GROUPS * h + side * (GROUPS - 1)
                line = slice(side * (ROWS - 1), side * (ROWS - 1) + 1)
                part_y[h, index, z] = chosen(region[at], slots[0, z, at % 2, line], slots[1, z, at % 2, line])
            return carry

        planes(body)

    gives = [
        copy_to(part_x.at[1 - half], give_x, part_send.at[0], part_recv.at[0], partner),
        copy_to(part_y.at[1 - half], give_y, part_send.at[1], part_recv.at[1], partner),
        copy_to(part_z.at[1 - half], give_z, part_send.at[2], part_recv.at[2], partner),
    ]
    zero_pack = jnp.zeros((ROWS, LANES), F32)

    def plain(slots, received, out, shift=0):
        def body(z, carry):
            for g in range(GROUPS):
                out[z + shift, g * ROWS : (g + 1) * ROWS, :] = assembled(slots, received, z, g)
            return carry

        planes(body)

    loads_f[0].wait()
    part_columns(slots_f.at[0], 0)
    part_planes(slots_f.at[0], 0, 0)
    part_planes(slots_f.at[0], NZ - 1, 1)
    part_rows(slots_f.at[0], 0, 0)
    part_rows(slots_f.at[0], 1, 1)
    loads_c[1].wait()
    part_columns(slots_c.at[1], 1)
    loads_c[2].wait()
    part_rows(slots_c.at[2], 0, 2)
    loads_c[3].wait()
    part_planes(slots_c.at[3], 0, 2)
    pl.semaphore_wait(barrier, len(faces))
    for copy in gives:
        copy.start()
    gives[0].wait_recv()
    pack[0] = part_x[half, 0] + give_x[0]
    rim_pack[...] = part_x[half, 1] + give_x[1]
    first_halos[0].start()
    first_halos[1].start()
    rims[0].start()
    gives[1].wait_recv()
    for b in range(2):
        face_y[0, b] = part_y[half, b] + give_y[b]
    rim_face[...] = part_y[half, 2] + give_y[2]
    first_halos[2].start()
    first_halos[3].start()
    rims[1].start()
    gives[2].wait_recv()
    for i in range(3):
        face_z[i] = part_z[half, i] + give_z[i]
    rims[2].start()
    first_halos[4].start()
    first_halos[5].start()
    prepare(slots_f.at[0], send_f.at[0])
    pair_f[0].start()
    for c in (1, 2, 3, 0):
        if c == 0:
            loads_c[c].wait()
        prepare(slots_c.at[c], send_c.at[c])
        pair_c[c].start()
    loads_f[1].wait()
    prepare(slots_f.at[1], send_f.at[1])
    pair_f[1].start()
    pair_f[0].wait_recv()
    plain(slots_f.at[0], recv_f.at[0], field.at[0], 1)
    for c, out in ((1, bx), (2, by), (3, bz), (0, alpha)):
        pair_c[c].wait_recv()
        plain(slots_c.at[c], recv_c.at[c], out)
    pair_f[1].wait_recv()
    plain(slots_f.at[1], recv_f.at[1], rhs)
    halves = (slice(0, LANES), slice(LANES, NX))
    group_rows = [slice(g * ROWS, (g + 1) * ROWS) for g in range(GROUPS)]
    def gather(z, last):
        low_rolled = pltpu.roll(bx[z, :, :LANES], LANES - 1, 1)
        high_rolled = pltpu.roll(bx[z, :, LANES:], LANES - 1, 1)
        upper_x = (jnp.where(last_lane, high_rolled, low_rolled), jnp.where(last_lane, 0.0, high_rolled))
        low, high = field[0, z + 1, :, :LANES], field[0, z + 1, :, LANES:]
        low_after, high_after = pltpu.roll(low, LANES - 1, 1), pltpu.roll(high, LANES - 1, 1)
        low_before, high_before = pltpu.roll(low, 1, 1), pltpu.roll(high, 1, 1)
        x_before = (low_before, jnp.where(first_lane, low_before, high_before))
        x_after = (jnp.where(last_lane, high_after, low_after), high_after)
        for j, part in enumerate(halves):
            here = (low, high)[j]
            lower_x = bx[z, :, part]
            here_y = by[z, :, part]
            upper_y = jnp.where(end_row, 0.0, pltpu.roll(here_y, NY - 1, 0))
            centre = alpha[z, :, part] + lower_x + upper_x[j] + here_y + upper_y + bz[z, :, part]
            lower_x = jnp.where(first_lane, 0.0, lower_x) if j == 0 else lower_x
            lower_y = jnp.where(row == 0, 0.0, here_y)
            value = rhs[z, :, part] + lower_x * x_before[j] + upper_x[j] * x_after[j]
            value = value + lower_y * pltpu.roll(here, 1, 0) + upper_y * pltpu.roll(here, NY - 1, 0)
            if not isinstance(z, int) or z > 0:
                value = value + bz[z, :, part] * field[0, z, :, part]
            if not last:
                centre = centre + bz[z + 1, :, part]
                value = value + bz[z + 1, :, part] * field[0, z + 2, :, part]
            near[0, z, :, part] = lower_x
            near[1, z, :, part] = upper_x[j]
            near[2, z, :, part] = lower_y
            near[3, z, :, part] = upper_y
            scaled[z, :, part] = value
            diag[z, :, part] = centre

    def gather_body(z, carry):
        gather(z, False)
        return carry

    gather(0, False)
    planes(gather_body, 0, 1, NZ - 1)
    gather(NZ - 1, True)
    for copy in rims:
        copy.wait_recv()
    rim_values = rim_x[...]

    def scale(z, last, carry):
        edge = jnp.concatenate(
            [pltpu.roll(rim_values, 126 - 2 * (z * GROUPS + g), 1) for g in range(GROUPS)], axis=0
        )
        edge = jnp.where(last_lane, edge, 0.0)
        sides = []
        inverses = []
        uppers = []
        for j, part in enumerate(halves):
            rim_row = jnp.where(end_row, jnp.broadcast_to(rim_y[z, :, part], (NY, LANES)), 0.0)
            centre = diag[z, :, part] + rim_row
            if j == 1:
                centre = centre + edge
            if last:
                centre = centre + bz[z + 1, :, part]
            inverse = 1.0 / centre
            inverses.append(inverse)
            diag[z, :, part] = centre
            inverse_ref[z, :, part] = inverse
            scaled[z, :, part] = inverse * scaled[z, :, part] - field[0, z + 1, :, part]
            sent_y[0, 0, 2, z, :, part] = inverse[:1]
            sent_y[0, 1, 2, z, :, part] = inverse[NY - 1 :]
            uppers.append(rim_row[NY - ROWS :])
            sides.append(inverse * (bx[z, :, part] if j == 0 else edge))
            edge_y[0, z, :, part] = jnp.where(row8 == 0, inverse[:ROWS] * by[z, :ROWS, part], 0.0)
            edge_y[1, z, :, part] = inverse[NY - ROWS :] * rim_row[NY - ROWS :]
            if isinstance(z, int) and z == 0:
                near[4, z, :, part] = inverse * bz[z, :, part]
            if last:
                near[5, z, :, part] = inverse * bz[z + 1, :, part]
        edge_pack, inverse_pack, y_pack = carry
        for g, rows in enumerate(group_rows):
            edge_pack = packed(z, g, sides[0][rows], sides[1][rows], edge_pack)
            inverse_pack = packed(z, g, inverses[0][rows], inverses[1][rows], inverse_pack)
        y_pack = packed(z, 0, by[z, :ROWS, :LANES], by[z, :ROWS, LANES:], y_pack)
        y_pack = packed(z, GROUPS - 1, uppers[0], uppers[1], y_pack)
        return edge_pack, inverse_pack, y_pack

    def weigh(z, first, last):
        inverse = inverse_ref[z]
        for i in range(4):
            near[i, z] = inverse * near[i, z]
        if not first:
            near[4, z] = inverse * bz[z]
        if not last:
            near[5, z] = inverse * bz[z + 1]

    def weigh_body(z, carry):
        weigh(z, False, False)
        return carry

    carry = scale(0, False, (zero_pack, zero_pack, zero_pack))
    carry = planes(lambda z, carry: scale(z, False, carry), carry, 1, NZ - 1)
    edge_x[...], sent_x[0, 2], y_pack = scale(NZ - 1, True, carry)
    odd = lane8 - 2 * spots == 1
    spot_group = spots - GROUPS * (spots // GROUPS)
    low_rim = (spot_group == 0) & (row8 == 0)
    high_rim = (spot_group == GROUPS - 1) & (row8 == ROWS - 1)
    low_spots = spots < GROUPS
    high_spots = (spots >= GROUPS * (NZ - 1)) & (spots < GROUPS * NZ)
    z_pack = zero_pack
    for g, rows in enumerate(group_rows):
        z_pack = packed(0, g, bz[0, rows, :LANES], bz[0, rows, LANES:], z_pack)
        z_pack = packed(NZ - 1, g, bz[NZ, rows, :LANES], bz[NZ, rows, LANES:], z_pack)
    beta_pack[0] = jnp.where(low_rim | high_rim, y_pack, 0.0)
    beta_pack[1] = jnp.where(odd, rim_pack[...], pltpu.roll(rim_values, LANES - 1, 1))
    beta_pack[2] = z_pack
    sent_z[0, 0, 2] = inverse_ref[0]
    sent_z[0, 1, 2] = inverse_ref[NZ - 1]

    def swapped(value):
        return jnp.where(odd, pltpu.roll(value, 1, 1), pltpu.roll(value, LANES - 1, 1))

    def halo_z_of(k, side):
        return got_z.at[k // 2, side, 0] if k % 2 else field.at[k, side * (NZ + 1)]

    def halo_y_of(k, side):
        return got_y.at[k // 2, side, 0] if k % 2 else halo_y.at[k, side]

    def inner(k, z, first, last, carry):
        low, high = field[k, z + 1, :, :LANES], field[k, z + 1, :, LANES:]
        low_after, high_after = pltpu.roll(low, LANES - 1, 1), pltpu.roll(high, LANES - 1, 1)
        low_before, high_before = pltpu.roll(low, 1, 1), pltpu.roll(high, 1, 1)
        x_before = (low_before, jnp.where(first_lane, low_before, high_before))
        x_after = (jnp.where(last_lane, high_after, low_after), high_after)
        values = []
        for j, part in enumerate(halves):
            here = (low, high)[j]
            value = scaled[z, :, part] - here
            value = value + near[0, z, :, part] * x_before[j] + near[1, z, :, part] * x_after[j]
            value = value + near[2, z, :, part] * pltpu.roll(here, 1, 0)
            value = value + near[3, z, :, part] * pltpu.roll(here, NY - 1, 0)
            if not first:
                value = value + near[4, z, :, part] * field[k, z, :, part]
            if not last:
                value = value + near[5, z, :, part] * field[k, z + 2, :, part]
            scaled[z, :, part] = value
            values.append(value)
            if k % 2:
                ahead = SECOND[k] * value + FIRST[k] * here
                sent_y[k // 2, 0, 1, z, :, part] = ahead[:1]
                sent_y[k // 2, 1, 1, z, :, part] = ahead[NY - 1 :]
                if first:
                    sent_z[k // 2, 0, 1, :, part] = ahead
                if last:
                    sent_z[k // 2, 1, 1, :, part] = ahead
        if k % 2:
            for g, rows in enumerate(group_rows):
                carry = packed(z, g, values[0][rows], values[1][rows], carry)
        return carry

    def outer(k, z, first, last, sides, carry):
        fresh = [[], []]
        sending = k % 2 == 0 and k < SWEEPS
        for g, rows in enumerate(group_rows):
            moved = pltpu.roll(sides, LANES - 1 - 2 * (z * GROUPS + g), 1)
            for j, part in enumerate(halves):
                value = scaled[z, rows, part] + jnp.where(lane8 == (0, LANES - 1)[j], moved, 0.0)
                if g == 0:
                    value = value + edge_y[0, z, :, part] * jnp.broadcast_to(
                        halo_y_of(k, 0)[z, :, part], (ROWS, LANES)
                    )
                if g == GROUPS - 1:
                    value = value + edge_y[1, z, :, part] * jnp.broadcast_to(
                        halo_y_of(k, 1)[z, :, part], (ROWS, LANES)
                    )
                if first:
                    value = value + near[4, z, rows, part] * halo_z_of(k, 0)[rows, part]
                if last:
                    value = value + near[5, z, rows, part] * halo_z_of(k, 1)[rows, part]
                for b in range(2):
                    if k and k % 2 == 0 and (first or last) and g == b * (GROUPS - 1):
                        line = jnp.broadcast_to(line_fix[0 if first else 1, b, :, part], (ROWS, LANES))
                        value = value + jnp.where(row8 == b * (ROWS - 1), line, 0.0)
                if k == SWEEPS:
                    resid[z, rows, part] = diag[z, rows, part] * value
                    continue
                scaled[z, rows, part] = value
                step = SECOND[k] * value
                if k > 0:
                    step = step + FIRST[k] * field[k, z + 1, rows, part]
                field[k + 1, z + 1, rows, part] = step
                if k == SWEEPS - 1:
                    total[z, rows, part] = total[z, rows, part] + step
                if not sending:
                    continue
                if first:
                    sent_z[k // 2, 0, 0, rows, part] = step
                if last:
                    sent_z[k // 2, 1, 0, rows, part] = step
                if g == 0:
                    sent_y[k // 2, 0, 0, z, :, part] = step[:1]
                if g == GROUPS - 1:
                    sent_y[k // 2, 1, 0, z, :, part] = step[ROWS - 1 :]
                fresh[j].append(step)
            if sending:
                carry = packed(z, g, fresh[0][g], fresh[1][g], carry)
        return carry

    def run_inner(k):
        carry = inner(k, 0, True, False, zero_pack)
        carry = planes(lambda z, carry: inner(k, z, False, False, carry), carry, 1, NZ - 1)
        return inner(k, NZ - 1, False, True, carry)

    def run_outer(k, x_halo, extra=0.0):
        sides = edge_x[...] * swapped(x_halo) + extra
        carry = outer(k, 0, True, False, sides, zero_pack)
        carry = planes(lambda z, carry: outer(k, z, False, False, sides, carry), carry, 1, NZ - 1)
        return outer(k, NZ - 1, False, True, sides, carry)

    def either(ref_low, ref_high):
        return jnp.where(odd, ref_high, ref_low)

    def ahead(r, k):
        for side in range(2):
            own = side * (NZ - 1)
            for part in halves:
                value = got_z[0, side, 2, :, part] * (bz[side * NZ, :, part] * field[k, own + 1, :, part])
                field[k + 1, side * (NZ + 1), :, part] = got_z[r, side, 1, :, part] + SECOND[k] * value
            face = (rim_face, rim_y)[side]
            value = got_y[0, side, 2] * (face[...] * sent_y[r, side, 0])
            halo_y[k + 1, side] = got_y[r, side, 1] + SECOND[k] * value
        value = either(got_x[0, 0, 2], got_x[0, 1, 2]) * swapped(sent_q[r, 1])
        return either(got_x[r, 0, 1], got_x[r, 1, 1]) + SECOND[k] * value

    def weigh_edges():
        y_pack = zero_pack
        z_pack = zero_pack
        for a in range(2):
            z = a * (NZ - 1)
            tiles = [near[4 + a, z, :, part] * got_z[0, a, 2, :, part] for part in halves]
            for g, rows in enumerate(group_rows):
                z_pack = packed(z, g, tiles[0][rows], tiles[1][rows], z_pack)
            for b in range(2):
                at = b * (NY - 1)
                low = b * (ROWS - 1)
                line_weight[a, b, 0] = near[4 + a, z, at : at + 1, :] * got_z[0, a, 2, at : at + 1, :]
                line_weight[a, b, 1] = edge_y[b, z, low : low + 1, :] * got_y[0, b, 2, z]

        def body(z, y_pack):
            for b in range(2):
                tiles = [
                    edge_y[b, z, :, part] * jnp.broadcast_to(got_y[0, b, 2, z, :, part], (ROWS, LANES))
                    for part in halves
                ]
                y_pack = packed(z, b * (GROUPS - 1), tiles[0], tiles[1], y_pack)
            return y_pack

        pack_weight[0] = edge_x[...] * swapped(either(got_x[0, 0, 2], got_x[0, 1, 2]))
        pack_weight[1] = planes(body, y_pack)
        pack_weight[2] = z_pack

    def edge_fix(r, k):
        for a in range(2):
            for b in range(2):
                value = line_weight[a, b, 0] * got_yz[r, a, b, 0] + line_weight[a, b, 1] * got_yz[r, a, b, 1]
                line_fix[a, b] = SECOND[k] * value

        def from_y(i):
            below = swapped(either(got_xy[r, 0, 0, i], got_xy[r, 1, 0, i]))
            above = swapped(either(got_xy[r, 0, 1, i], got_xy[r, 1, 1, i]))
            shift = 2 * (GROUPS - 1)
            below = jnp.where(low_rim, pltpu.roll(pltpu.roll(below, 1, 0), LANES - shift, 1), 0.0)
            return below + jnp.where(high_rim, pltpu.roll(pltpu.roll(above, ROWS - 1, 0), shift, 1), 0.0)

        def from_z(i):
            below = swapped(either(got_xz[r, 0, 0], got_xz[r, 1, 0]))
            above = swapped(either(got_xz[r, 0, 1], got_xz[r, 1, 1]))
            shift = 2 * GROUPS * (NZ - 1)
            back = (1 - i) * ROWS
            below = jnp.where(low_spots, pltpu.roll(below, LANES - shift - back, 1), 0.0)
            return below + jnp.where(high_spots, pltpu.roll(above, shift - back, 1), 0.0)

        value = pack_weight[0] * (from_y(0) + from_z(1))
        return SECOND[k] * (value + pack_weight[1] * from_y(1) + pack_weight[2] * from_z(0))

    def apply_two(r):
        k = 2 * r + 1
        own = sent_x[r, 0]
        sent_q[r, 0] = beta_pack[0] * own
        across = beta_pack[1] * own
        sent_q[r, 1] = across
        ends = pltpu.roll(jnp.where(low_spots | high_spots, across, 0.0), ROWS, 1)
        sent_q[r, 2] = beta_pack[2] * own + ends
        for a in range(2):
            z = a * (NZ - 1)
            for b in range(2):
                line = sent_y[r, b, 0, z]
                at = b * (NY - 1)
                sent_yz[r, a, b, 0] = (rim_face, rim_y)[b][z] * line
                sent_yz[r, a, b, 1] = bz[a * NZ, at : at + 1, :] * line
        near_copies = face_copies(r, 0, pl.ds(0, 1))
        far_copies = edge_copies(r)
        for copy in far_copies[:8] + near_copies + far_copies[8:]:
            copy.start()

        if r == 0:
            weigh(0, True, False)
            planes(weigh_body, 0, 1, NZ - 1)
            weigh(NZ - 1, False, True)
        sent_x[r, 1] = SECOND[k] * run_inner(k) + FIRST[k] * own
        ahead_copies = face_copies(r, 24, pl.ds(1, 1))
        if r == 0:
            ahead_copies += face_copies(r, 6, pl.ds(2, 1))
        for copy in ahead_copies:
            copy.start()

        def sum_body(z, carry):
            for part in halves:
                if r == 0:
                    total[z, :, part] = field[0, z + 1, :, part] + field[1, z + 1, :, part]
                else:
                    total[z, :, part] = (
                        total[z, :, part] + field[2, z + 1, :, part] + field[3, z + 1, :, part]
                    )
            return carry

        planes(sum_body)
        for copy in near_copies:
            copy.wait_recv()
        run_outer(k, either(got_x[r, 0, 0], got_x[r, 1, 0]))
        if k == SWEEPS - 1:
            x_out.start()
        for copy in ahead_copies:
            copy.wait_recv()
        x_halo = ahead(r, k)
        if r == 0:
            weigh_edges()
        run_inner(k + 1)
        for copy in far_copies:
            copy.wait_recv()
        return near_copies + far_copies + ahead_copies, run_outer(k + 1, x_halo, edge_fix(r, k))

    x_out = pltpu.make_async_copy(total, x_hbm, out_sem.at[0])
    for copy in first_halos:
        copy.wait_recv()
    sent_x[0, 0] = run_outer(0, either(halo_x[0, 0], halo_x[0, 1]))
    first_copies, sent_x[1, 0] = apply_two(0)
    second_copies, unused = apply_two(1)
    r_out = pltpu.make_async_copy(resid, r_hbm, out_sem.at[1])
    r_out.start()
    for copy in gives + pair_f + pair_c + rims + first_halos + first_copies + second_copies:
        copy.wait_send()
    x_out.wait()
    r_out.wait()


def emit(x_ref, r_ref, x_out, r_out, sem):
    first = pltpu.make_async_copy(x_ref, x_out, sem.at[0])
    second = pltpu.make_async_copy(r_ref, r_out, sem.at[1])
    first.start()
    second.start()
    first.wait()
    second.wait()


def local(old_fields, old_coef, held_slabs):
    slots = old_fields.shape[1]
    fields = old_fields.reshape(2, slots, NZ, 2, ROWS, NX)
    coef = old_coef.reshape(4, slots, NZ, 2, ROWS, NX)
    brick = (NZ, NY, NX)
    rounds = SWEEPS + 1
    dma = pltpu.SemaphoreType.DMA
    anywhere = pl.BlockSpec(memory_space=pl.ANY)
    hbm = pl.BlockSpec(memory_space=pltpu.HBM)
    held = pltpu.with_memory_space_constraint(jnp.transpose(held_slabs, (1, 2, 0)), pltpu.HBM)
    results = pl.pallas_call(
        kernel,
        out_shape=(jax.ShapeDtypeStruct(brick, F32), jax.ShapeDtypeStruct(brick, F32)),
        in_specs=[hbm, hbm, hbm],
        out_specs=(anywhere, anywhere),
        scratch_shapes=[
            pltpu.VMEM((2, slots, NZ, 2, ROWS, NX), F32),
            pltpu.VMEM((4, slots, NZ, 2, ROWS, NX), BF16),
            pltpu.VMEM((2, NZ, GROUPS, ROWS, NX), F32),
            pltpu.VMEM((4, NZ, GROUPS, ROWS, NX), BF16),
            pltpu.VMEM((2, NZ, GROUPS, ROWS, NX), F32),
            pltpu.VMEM((4, NZ, GROUPS, ROWS, NX), BF16),
            pltpu.VMEM((rounds, NZ + 2, NY, NX), F32),
            pltpu.VMEM(brick, F32),
            pltpu.VMEM(brick, F32),
            pltpu.VMEM(brick, F32),
            pltpu.VMEM((NZ + 1, NY, NX), F32),
            pltpu.VMEM(brick, F32),
            pltpu.VMEM((6, NZ, NY, NX), F32),
            pltpu.VMEM((2, NZ, ROWS, NX), F32),
            pltpu.VMEM((ROWS, LANES), F32),
            pltpu.VMEM(brick, F32),
            pltpu.VMEM(brick, F32),
            pltpu.VMEM(brick, F32),
            pltpu.VMEM(brick, F32),
            pltpu.VMEM(brick, F32),
            pltpu.VMEM((rounds, ROWS, LANES), F32),
            pltpu.VMEM((rounds, 2, NZ, 1, NX), F32),
            pltpu.VMEM((rounds, 2, ROWS, LANES), F32),
            pltpu.VMEM((rounds, 2, NZ, 1, NX), F32),
            pltpu.VMEM((ROWS, LANES), F32),
            pltpu.VMEM((NZ, 1, NX), F32),
            pltpu.VMEM((ROWS, LANES), F32),
            pltpu.VMEM((NZ, 1, NX), F32),
            pltpu.VMEM((3, ROWS, LANES), F32),
            pltpu.VMEM((2, 2, 3, NY, NX), F32),
            pltpu.VMEM((2, 2, 3, NY, NX), F32),
            pltpu.VMEM((2, 2, 3, NZ, 1, NX), F32),
            pltpu.VMEM((2, 2, 3, NZ, 1, NX), F32),
            pltpu.VMEM((2, 3, ROWS, LANES), F32),
            pltpu.VMEM((2, 2, 3, ROWS, LANES), F32),
            pltpu.VMEM((2, 2, 2, 2, 1, NX), F32),
            pltpu.VMEM((2, 2, 2, 2, 1, NX), F32),
            pltpu.VMEM((2, 3, ROWS, LANES), F32),
            pltpu.VMEM((2, 2, 2, ROWS, LANES), F32),
            pltpu.VMEM((2, 2, 2, 2, ROWS, LANES), F32),
            pltpu.VMEM((2, 2, 2, 1, NX), F32),
            pltpu.VMEM((2, 2, 1, NX), F32),
            pltpu.VMEM((3, ROWS, LANES), F32),
            pltpu.VMEM((2, 2, ROWS, LANES), F32),
            pltpu.VMEM((2, 3, NZ, 1, NX), F32),
            pltpu.VMEM((2, 3, NY, NX), F32),
            pltpu.VMEM((2, ROWS, LANES), F32),
            pltpu.VMEM((3, NZ, 1, NX), F32),
            pltpu.VMEM((3, NY, NX), F32),
            pltpu.VMEM((3, NY, NX), F32),
            pltpu.SMEM((1, 1, slots), jnp.int32),
            dma((6,)),
            dma((1,)),
            dma((6,)),
            dma((6,)),
            dma((rounds, 6)),
            dma((rounds, 6)),
            dma((3,)),
            dma((3,)),
            dma((2,)),
            dma((2, 30)),
            dma((2, 30)),
            dma((3,)),
            dma((3,)),
        ],
        compiler_params=pltpu.CompilerParams(
            collective_id=0, has_side_effects=True, vmem_limit_bytes=55767040
        ),
        name="smooth",
    )(fields, coef, held)
    return pl.pallas_call(
        emit,
        out_shape=(jax.ShapeDtypeStruct(brick, F32), jax.ShapeDtypeStruct(brick, F32)),
        in_specs=[anywhere, anywhere],
        out_specs=(hbm, hbm),
        scratch_shapes=[dma((2,))],
        compiler_params=pltpu.CompilerParams(vmem_limit_bytes=1 << 20),
        name="emit",
    )(*results)


def solution(mesh):
    in_specs = (
        P(None, "gy", "gz", None, "gx"),
        P(None, "gy", "gz", None, "gx"),
        P("gy", "gz", "gx"),
    )
    out_specs = (P("gz", "gy", "gx"), P("gz", "gy", "gx"))
    return jax.shard_map(local, mesh=mesh, in_specs=in_specs, out_specs=out_specs, check_vma=False)
```

```python
import functools
import jax
import jax.numpy as jnp
from jax import lax
from jax.experimental import pallas as pl
from jax.experimental.pallas import tpu as pltpu
from jax.sharding import PartitionSpec as P

SWEEPS = 4
NZ = 16
NY = 24
NX = 256
ROWS = 8
LANES = 128
GROUPS = NY // ROWS
MESH = pl.DeviceIdType.MESH
F32 = jnp.float32
BF16 = jnp.bfloat16


def chebyshev_weights(count):
    low_bound = 0.25
    high_bound = 2.0
    centre_value = 0.5 * (high_bound + low_bound)
    half_width = 0.5 * (high_bound - low_bound)
    ratio_value = centre_value / half_width
    damping = 1.0 / ratio_value
    first_list = [0.0]
    second_list = [1.0 / centre_value]
    for step_index in range(1, count):
        damping_next = 1.0 / (2.0 * ratio_value - damping)
        first_list.append(damping_next * damping)
        second_list.append(2.0 * damping_next / half_width)
        damping = damping_next
    return first_list, second_list


FIRST, SECOND = chebyshev_weights(SWEEPS)


def ring(axis):
    count = lax.axis_size(axis)
    me = lax.axis_index(axis)
    low = {axis: lax.rem(me + count - 1, count)}
    high = {axis: lax.rem(me + 1, count)}
    return low, high


def kernel(
    fields_hbm, coef_hbm, held_hbm, x_hbm, r_hbm,
    slots_f, slots_c, send_f, send_c, recv_f, recv_c,
    field, alpha, bx, by, bz, rhs, near, edge_y, edge_x, diag, inverse_ref, scaled, total, resid,
    pack, face_y, halo_x, halo_y, rim_pack, rim_face, rim_x, rim_y, beta_pack,
    sent_z, got_z, sent_y, got_y, sent_x, got_x, sent_yz, got_yz, sent_q, got_xz, got_xy, line_weight, line_fix, pack_weight,
    part_x, part_y, part_z, give_x, give_y, give_z, face_z, held_ref,
    load_sem, held_sem, pair_send, pair_recv, halo_send, halo_recv, rim_send, rim_recv, out_sem,
    both_send, both_recv, part_send, part_recv,
):
    group = lax.axis_index("gy")
    half = lax.rem(group, 2)
    first_slab = 3 * (group // 2)
    partner = {"gy": group + 1 - 2 * half}
    x_low, x_high = ring("gx")
    y_low, y_high = ring("gy")
    z_low, z_high = ring("gz")

    barrier = pltpu.get_barrier_semaphore()
    x_sides, y_sides, z_sides = (x_low, x_high), (y_low, y_high), (z_low, z_high)
    faces = [x_low, x_high, y_low, y_high, z_low, z_high]
    for neighbour in faces:
        pl.semaphore_signal(barrier, inc=1, device_id=neighbour, device_id_type=MESH)

    load_held = pltpu.make_async_copy(held_hbm, held_ref, held_sem.at[0])
    loads_f = [pltpu.make_async_copy(fields_hbm.at[c], slots_f.at[c], load_sem.at[c]) for c in range(2)]
    loads_c = [pltpu.make_async_copy(coef_hbm.at[c], slots_c.at[c], load_sem.at[2 + c]) for c in range(4)]
    load_held.start()
    loads_f[0].start()
    for c in (1, 2, 3, 0):
        loads_c[c].start()
    loads_f[1].start()
    load_held.wait()

    id0 = held_ref[0, 0, 0]
    id1 = held_ref[0, 0, 1]
    mine = [first_slab + (3 * half + g) // 2 for g in range(GROUPS)]
    theirs = [first_slab + (3 * (1 - half) + g) // 2 for g in range(GROUPS)]
    my_part = [lax.rem(half + g, 2) for g in range(GROUPS)]
    their_part = [lax.rem(1 - half + g, 2) for g in range(GROUPS)]

    row8 = lax.broadcasted_iota(jnp.int32, (ROWS, LANES), 0)
    row = lax.broadcasted_iota(jnp.int32, (NY, LANES), 0)
    lane = lax.broadcasted_iota(jnp.int32, (NY, LANES), 1)
    lane8 = lax.broadcasted_iota(jnp.int32, (ROWS, LANES), 1)
    end_row = row == NY - 1
    first_lane = lane == 0
    last_lane = lane == LANES - 1
    spots = lane8 // 2

    def copy_to(source, target, send_sem, recv_sem, device):
        return pltpu.make_async_remote_copy(
            src_ref=source, dst_ref=target, send_sem=send_sem, recv_sem=recv_sem,
            device_id=device, device_id_type=MESH,
        )

    pair_f = [copy_to(send_f.at[c], recv_f.at[c], pair_send.at[c], pair_recv.at[c], partner) for c in range(2)]
    pair_c = [
        copy_to(send_c.at[c], recv_c.at[c], pair_send.at[2 + c], pair_recv.at[2 + c], partner) for c in range(4)
    ]

    def halo_copies(k):
        return [
            copy_to(pack.at[k], halo_x.at[k, 1], halo_send.at[k, 0], halo_recv.at[k, 0], x_low),
            copy_to(pack.at[k], halo_x.at[k, 0], halo_send.at[k, 1], halo_recv.at[k, 1], x_high),
            copy_to(face_y.at[k, 0], halo_y.at[k, 1], halo_send.at[k, 2], halo_recv.at[k, 2], y_low),
            copy_to(face_y.at[k, 1], halo_y.at[k, 0], halo_send.at[k, 3], halo_recv.at[k, 3], y_high),
            copy_to(face_z.at[0], field.at[k, NZ + 1], halo_send.at[k, 4], halo_recv.at[k, 4], z_low),
            copy_to(face_z.at[1], field.at[k, 0], halo_send.at[k, 5], halo_recv.at[k, 5], z_high),
        ]

    first_halos = halo_copies(0)

    def numbered(r, first, moves):
        return [
            copy_to(source, target, both_send.at[r, first + i], both_recv.at[r, first + i], device)
            for i, (source, target, device) in enumerate(moves)
        ]

    def edge_copies(r):
        moves = []
        for a in range(2):
            for b in range(2):
                device = {**x_sides[a], **y_sides[b]}
                line = pl.ds(b * (ROWS - 1), 1)
                moves.append((sent_q.at[r, pl.ds(0, 2), line], got_xy.at[r, 1 - a, 1 - b, pl.ds(0, 2), line], device))
        for a in range(2):
            for b in range(2):
                device = {**x_sides[a], **z_sides[b]}
                moves.append((sent_q.at[r, 2], got_xz.at[r, 1 - a, 1 - b], device))
        for a in range(2):
            for b in range(2):
                moves.append((sent_yz.at[r, a, b], got_yz.at[r, 1 - a, 1 - b], {**z_sides[a], **y_sides[b]}))
        return numbered(r, 12, moves)

    def face_copies(r, first, part):
        moves = [(sent_x.at[r, part], got_x.at[r, 1 - a, part], x_sides[a]) for a in range(2)]
        moves += [(sent_y.at[r, a, part], got_y.at[r, 1 - a, part], y_sides[a]) for a in range(2)]
        moves += [(sent_z.at[r, a, part], got_z.at[r, 1 - a, part], z_sides[a]) for a in range(2)]
        return numbered(r, first, moves)

    rims = [
        copy_to(rim_pack, rim_x, rim_send.at[0], rim_recv.at[0], x_low),
        copy_to(rim_face, rim_y, rim_send.at[1], rim_recv.at[1], y_low),
        copy_to(face_z.at[2], bz.at[NZ], rim_send.at[2], rim_recv.at[2], z_low),
    ]

    def planes(body, carry=0, first=0, last=NZ):
        return lax.fori_loop(first, last, body, carry, unroll=True)

    def prepare(slots, out):
        def body(z, carry):
            for g in range(GROUPS):
                out[z, g] = lax.select(id0 == theirs[g], slots[0, z, their_part[g]], slots[1, z, their_part[g]])
            return carry

        planes(body)

    def assembled(slots, received, z, g):
        return lax.select(
            id0 == mine[g],
            slots[0, z, my_part[g]],
            lax.select(id1 == mine[g], slots[1, z, my_part[g]], received[z, g]),
        ).astype(F32)

    def packed(z, g, tile_low, tile_high, carry):
        return packed_at(z * GROUPS + g, tile_low, tile_high, carry)

    def packed_at(spot, tile_low, tile_high, carry):
        both = jnp.where(lane8 == 0, tile_low, tile_high)
        moved = pltpu.roll(both, 2 * spot + 1, 1)
        return jnp.where(spots == spot, moved, carry)

    region = [first_slab + g // 2 for g in range(2 * GROUPS)]

    def chosen(slab, first, second):
        zero = jnp.zeros(first.shape, first.dtype)
        return lax.select(id0 == slab, first, lax.select(id1 == slab, second, zero)).astype(F32)

    def part_columns(slots, index):
        def body(z, carry):
            for h in range(2):
                value = carry[h]
                for g in range(GROUPS):
                    at = GROUPS * h + g
                    tile = chosen(region[at], slots[0, z, at % 2], slots[1, z, at % 2])
                    value = packed(z, g, tile[:, :LANES], tile[:, LANES:], value)
                carry = (value, carry[1]) if h == 0 else (carry[0], value)
            return carry

        part_x[0, index], part_x[1, index] = planes(body, (zero_pack, zero_pack))

    def part_planes(slots, z, index):
        for at in range(2 * GROUPS):
            rows = slice((at % GROUPS) * ROWS, (at % GROUPS + 1) * ROWS)
            part_z[at // GROUPS, index, rows, :] = chosen(region[at], slots[0, z, at % 2], slots[1, z, at % 2])

    def part_rows(slots, side, index):
        def body(z, carry):
            for h in range(2):
                at = GROUPS * h + side * (GROUPS - 1)
                line = slice(side * (ROWS - 1), side * (ROWS - 1) + 1)
                part_y[h, index, z] = chosen(region[at], slots[0, z, at % 2, line], slots[1, z, at % 2, line])
            return carry

        planes(body)

    gives = [
        copy_to(part_x.at[1 - half], give_x, part_send.at[0], part_recv.at[0], partner),
        copy_to(part_y.at[1 - half], give_y, part_send.at[1], part_recv.at[1], partner),
        copy_to(part_z.at[1 - half], give_z, part_send.at[2], part_recv.at[2], partner),
    ]
    zero_pack = jnp.zeros((ROWS, LANES), F32)

    def plain(slots, received, out, shift=0):
        def body(z, carry):
            for g in range(GROUPS):
                out[z + shift, g * ROWS : (g + 1) * ROWS, :] = assembled(slots, received, z, g)
            return carry

        planes(body)

    loads_f[0].wait()
    part_columns(slots_f.at[0], 0)
    part_planes(slots_f.at[0], 0, 0)
    part_planes(slots_f.at[0], NZ - 1, 1)
    part_rows(slots_f.at[0], 0, 0)
    part_rows(slots_f.at[0], 1, 1)
    loads_c[1].wait()
    part_columns(slots_c.at[1], 1)
    loads_c[2].wait()
    part_rows(slots_c.at[2], 0, 2)
    loads_c[3].wait()
    part_planes(slots_c.at[3], 0, 2)
    pl.semaphore_wait(barrier, len(faces))
    for copy in gives:
        copy.start()
    gives[0].wait_recv()
    pack[0] = part_x[half, 0] + give_x[0]
    rim_pack[...] = part_x[half, 1] + give_x[1]
    first_halos[0].start()
    first_halos[1].start()
    rims[0].start()
    gives[1].wait_recv()
    for b in range(2):
        face_y[0, b] = part_y[half, b] + give_y[b]
    rim_face[...] = part_y[half, 2] + give_y[2]
    first_halos[2].start()
    first_halos[3].start()
    rims[1].start()
    gives[2].wait_recv()
    for i in range(3):
        face_z[i] = part_z[half, i] + give_z[i]
    rims[2].start()
    first_halos[4].start()
    first_halos[5].start()
    prepare(slots_f.at[0], send_f.at[0])
    pair_f[0].start()
    for c in (1, 2, 3, 0):
        if c == 0:
            loads_c[c].wait()
        prepare(slots_c.at[c], send_c.at[c])
        pair_c[c].start()
    loads_f[1].wait()
    prepare(slots_f.at[1], send_f.at[1])
    pair_f[1].start()
    pair_f[0].wait_recv()
    plain(slots_f.at[0], recv_f.at[0], field.at[0], 1)
    for c, out in ((1, bx), (2, by), (3, bz), (0, alpha)):
        pair_c[c].wait_recv()
        plain(slots_c.at[c], recv_c.at[c], out)
    pair_f[1].wait_recv()
    plain(slots_f.at[1], recv_f.at[1], rhs)
    halves = (slice(0, LANES), slice(LANES, NX))
    group_rows = [slice(g * ROWS, (g + 1) * ROWS) for g in range(GROUPS)]
    def gather(z, last):
        low_rolled = pltpu.roll(bx[z, :, :LANES], LANES - 1, 1)
        high_rolled = pltpu.roll(bx[z, :, LANES:], LANES - 1, 1)
        upper_x = (jnp.where(last_lane, high_rolled, low_rolled), jnp.where(last_lane, 0.0, high_rolled))
        low, high = field[0, z + 1, :, :LANES], field[0, z + 1, :, LANES:]
        low_after, high_after = pltpu.roll(low, LANES - 1, 1), pltpu.roll(high, LANES - 1, 1)
        low_before, high_before = pltpu.roll(low, 1, 1), pltpu.roll(high, 1, 1)
        x_before = (low_before, jnp.where(first_lane, low_before, high_before))
        x_after = (jnp.where(last_lane, high_after, low_after), high_after)
        for j, part in enumerate(halves):
            here = (low, high)[j]
            lower_x = bx[z, :, part]
            here_y = by[z, :, part]
            upper_y = jnp.where(end_row, 0.0, pltpu.roll(here_y, NY - 1, 0))
            centre = alpha[z, :, part] + lower_x + upper_x[j] + here_y + upper_y + bz[z, :, part]
            lower_x = jnp.where(first_lane, 0.0, lower_x) if j == 0 else lower_x
            lower_y = jnp.where(row == 0, 0.0, here_y)
            value = rhs[z, :, part] + lower_x * x_before[j] + upper_x[j] * x_after[j]
            value = value + lower_y * pltpu.roll(here, 1, 0) + upper_y * pltpu.roll(here, NY - 1, 0)
            if not isinstance(z, int) or z > 0:
                value = value + bz[z, :, part] * field[0, z, :, part]
            if not last:
                centre = centre + bz[z + 1, :, part]
                value = value + bz[z + 1, :, part] * field[0, z + 2, :, part]
            near[0, z, :, part] = lower_x
            near[1, z, :, part] = upper_x[j]
            near[2, z, :, part] = lower_y
            near[3, z, :, part] = upper_y
            scaled[z, :, part] = value
            diag[z, :, part] = centre

    def gather_body(z, carry):
        gather(z, False)
        return carry

    gather(0, False)
    planes(gather_body, 0, 1, NZ - 1)
    gather(NZ - 1, True)
    low_pack = planes(lambda z, carry: packed(z, 0, by[z, :ROWS, :LANES], by[z, :ROWS, LANES:], carry), zero_pack)
    for copy in rims:
        copy.wait_recv()
    rim_values = rim_x[...]

    def scale(z, last, carry):
        edge = jnp.concatenate(
            [pltpu.roll(rim_values, 126 - 2 * (z * GROUPS + g), 1) for g in range(GROUPS)], axis=0
        )
        edge = jnp.where(last_lane, edge, 0.0)
        sides = []
        inverses = []
        uppers = []
        for j, part in enumerate(halves):
            rim_row = jnp.where(end_row, jnp.broadcast_to(rim_y[z, :, part], (NY, LANES)), 0.0)
            centre = diag[z, :, part] + rim_row
            if j == 1:
                centre = centre + edge
            if last:
                centre = centre + bz[z + 1, :, part]
            inverse = 1.0 / centre
            inverses.append(inverse)
            diag[z, :, part] = centre
            inverse_ref[z, :, part] = inverse
            scaled[z, :, part] = inverse * scaled[z, :, part] - field[0, z + 1, :, part]
            sent_y[0, 0, 2, z, :, part] = inverse[:1]
            sent_y[0, 1, 2, z, :, part] = inverse[NY - 1 :]
            uppers.append(rim_row[NY - ROWS :])
            sides.append(inverse * (bx[z, :, part] if j == 0 else edge))
            edge_y[0, z, :, part] = jnp.where(row8 == 0, inverse[:ROWS] * by[z, :ROWS, part], 0.0)
            edge_y[1, z, :, part] = inverse[NY - ROWS :] * rim_row[NY - ROWS :]
            if isinstance(z, int) and z == 0:
                near[4, z, :, part] = inverse * bz[z, :, part]
            if last:
                near[5, z, :, part] = inverse * bz[z + 1, :, part]
        edge_pack, y_pack = carry
        for g, rows in enumerate(group_rows):
            edge_pack = packed(z, g, sides[0][rows], sides[1][rows], edge_pack)
        y_pack = packed(z, GROUPS - 1, uppers[0], uppers[1], y_pack)
        return edge_pack, y_pack

    def weigh(z, first, last, carry):
        inverse = inverse_ref[z]
        for g, rows in enumerate(group_rows):
            carry = packed(z, g, inverse[rows, :LANES], inverse[rows, LANES:], carry)
        for i in range(4):
            near[i, z] = inverse * near[i, z]
        if not first:
            near[4, z] = inverse * bz[z]
        if not last:
            near[5, z] = inverse * bz[z + 1]
        return carry

    carry = scale(0, False, (zero_pack, low_pack))
    carry = planes(lambda z, carry: scale(z, False, carry), carry, 1, NZ - 1)
    edge_x[...], y_pack = scale(NZ - 1, True, carry)
    odd = lane8 - 2 * spots == 1
    spot_group = spots - GROUPS * (spots // GROUPS)
    low_rim = (spot_group == 0) & (row8 == 0)
    high_rim = (spot_group == GROUPS - 1) & (row8 == ROWS - 1)
    low_spots = spots < GROUPS
    high_spots = (spots >= GROUPS * (NZ - 1)) & (spots < GROUPS * NZ)
    z_pack = zero_pack
    for g, rows in enumerate(group_rows):
        z_pack = packed(0, g, bz[0, rows, :LANES], bz[0, rows, LANES:], z_pack)
        z_pack = packed(NZ - 1, g, bz[NZ, rows, :LANES], bz[NZ, rows, LANES:], z_pack)
    beta_pack[0] = jnp.where(low_rim | high_rim, y_pack, 0.0)
    beta_pack[1] = jnp.where(odd, rim_pack[...], pltpu.roll(rim_values, LANES - 1, 1))
    beta_pack[2] = z_pack
    sent_z[0, 0, 2] = inverse_ref[0]
    sent_z[0, 1, 2] = inverse_ref[NZ - 1]

    def swapped(value):
        return jnp.where(odd, pltpu.roll(value, 1, 1), pltpu.roll(value, LANES - 1, 1))

    def halo_z_of(k, side):
        return got_z.at[k // 2, side, 0] if k % 2 else field.at[k, side * (NZ + 1)]

    def halo_y_of(k, side):
        return got_y.at[k // 2, side, 0] if k % 2 else halo_y.at[k, side]

    def inner(k, z, first, last, carry):
        low, high = field[k, z + 1, :, :LANES], field[k, z + 1, :, LANES:]
        low_after, high_after = pltpu.roll(low, LANES - 1, 1), pltpu.roll(high, LANES - 1, 1)
        low_before, high_before = pltpu.roll(low, 1, 1), pltpu.roll(high, 1, 1)
        x_before = (low_before, jnp.where(first_lane, low_before, high_before))
        x_after = (jnp.where(last_lane, high_after, low_after), high_after)
        values = []
        for j, part in enumerate(halves):
            here = (low, high)[j]
            value = scaled[z, :, part] - here
            value = value + near[0, z, :, part] * x_before[j] + near[1, z, :, part] * x_after[j]
            value = value + near[2, z, :, part] * pltpu.roll(here, 1, 0)
            value = value + near[3, z, :, part] * pltpu.roll(here, NY - 1, 0)
            if not first:
                value = value + near[4, z, :, part] * field[k, z, :, part]
            if not last:
                value = value + near[5, z, :, part] * field[k, z + 2, :, part]
            scaled[z, :, part] = value
            values.append(value)
            if k % 2:
                ahead = SECOND[k] * value + FIRST[k] * here
                sent_y[k // 2, 0, 1, z, :, part] = ahead[:1]
                sent_y[k // 2, 1, 1, z, :, part] = ahead[NY - 1 :]
                if first:
                    sent_z[k // 2, 0, 1, :, part] = ahead
                if last:
                    sent_z[k // 2, 1, 1, :, part] = ahead
        if k % 2:
            for g, rows in enumerate(group_rows):
                carry = packed(z, g, values[0][rows], values[1][rows], carry)
        return carry

    def outer(k, z, first, last, sides, carry):
        fresh = [[], []]
        sending = k % 2 == 0 and k < SWEEPS
        for g, rows in enumerate(group_rows):
            moved = pltpu.roll(sides, LANES - 1 - 2 * (z * GROUPS + g), 1)
            for j, part in enumerate(halves):
                value = scaled[z, rows, part] + jnp.where(lane8 == (0, LANES - 1)[j], moved, 0.0)
                if g == 0:
                    value = value + edge_y[0, z, :, part] * jnp.broadcast_to(
                        halo_y_of(k, 0)[z, :, part], (ROWS, LANES)
                    )
                if g == GROUPS - 1:
                    value = value + edge_y[1, z, :, part] * jnp.broadcast_to(
                        halo_y_of(k, 1)[z, :, part], (ROWS, LANES)
                    )
                if first:
                    value = value + near[4, z, rows, part] * halo_z_of(k, 0)[rows, part]
                if last:
                    value = value + near[5, z, rows, part] * halo_z_of(k, 1)[rows, part]
                for b in range(2):
                    if k and k % 2 == 0 and (first or last) and g == b * (GROUPS - 1):
                        line = jnp.broadcast_to(line_fix[0 if first else 1, b, :, part], (ROWS, LANES))
                        value = value + jnp.where(row8 == b * (ROWS - 1), line, 0.0)
                if k == SWEEPS:
                    resid[z, rows, part] = diag[z, rows, part] * value
                    continue
                scaled[z, rows, part] = value
                step = SECOND[k] * value
                if k > 0:
                    step = step + FIRST[k] * field[k, z + 1, rows, part]
                field[k + 1, z + 1, rows, part] = step
                if k == SWEEPS - 1:
                    total[z, rows, part] = total[z, rows, part] + step
                if not sending:
                    continue
                if first:
                    sent_z[k // 2, 0, 0, rows, part] = step
                if last:
                    sent_z[k // 2, 1, 0, rows, part] = step
                if g == 0:
                    sent_y[k // 2, 0, 0, z, :, part] = step[:1]
                if g == GROUPS - 1:
                    sent_y[k // 2, 1, 0, z, :, part] = step[ROWS - 1 :]
                fresh[j].append(step)
            if sending:
                carry = packed(z, g, fresh[0][g], fresh[1][g], carry)
        return carry

    def run_inner(k):
        carry = inner(k, 0, True, False, zero_pack)
        carry = planes(lambda z, carry: inner(k, z, False, False, carry), carry, 1, NZ - 1)
        return inner(k, NZ - 1, False, True, carry)

    def run_outer(k, x_halo, extra=0.0):
        sides = edge_x[...] * swapped(x_halo) + extra
        carry = outer(k, 0, True, False, sides, zero_pack)
        carry = planes(lambda z, carry: outer(k, z, False, False, sides, carry), carry, 1, NZ - 1)
        return outer(k, NZ - 1, False, True, sides, carry)

    def either(ref_low, ref_high):
        return jnp.where(odd, ref_high, ref_low)

    def ahead(r, k):
        for side in range(2):
            own = side * (NZ - 1)
            for part in halves:
                value = got_z[0, side, 2, :, part] * (bz[side * NZ, :, part] * field[k, own + 1, :, part])
                field[k + 1, side * (NZ + 1), :, part] = got_z[r, side, 1, :, part] + SECOND[k] * value
            face = (rim_face, rim_y)[side]
            value = got_y[0, side, 2] * (face[...] * sent_y[r, side, 0])
            halo_y[k + 1, side] = got_y[r, side, 1] + SECOND[k] * value
        value = either(got_x[0, 0, 2], got_x[0, 1, 2]) * swapped(sent_q[r, 1])
        return either(got_x[r, 0, 1], got_x[r, 1, 1]) + SECOND[k] * value

    def weigh_edges():
        y_pack = zero_pack
        z_pack = zero_pack
        for a in range(2):
            z = a * (NZ - 1)
            tiles = [near[4 + a, z, :, part] * got_z[0, a, 2, :, part] for part in halves]
            for g, rows in enumerate(group_rows):
                z_pack = packed(z, g, tiles[0][rows], tiles[1][rows], z_pack)
            for b in range(2):
                at = b * (NY - 1)
                low = b * (ROWS - 1)
                line_weight[a, b, 0] = near[4 + a, z, at : at + 1, :] * got_z[0, a, 2, at : at + 1, :]
                line_weight[a, b, 1] = edge_y[b, z, low : low + 1, :] * got_y[0, b, 2, z]

        def body(z, y_pack):
            for b in range(2):
                tiles = [
                    edge_y[b, z, :, part] * jnp.broadcast_to(got_y[0, b, 2, z, :, part], (ROWS, LANES))
                    for part in halves
                ]
                y_pack = packed(z, b * (GROUPS - 1), tiles[0], tiles[1], y_pack)
            return y_pack

        pack_weight[0] = edge_x[...] * swapped(either(got_x[0, 0, 2], got_x[0, 1, 2]))
        pack_weight[1] = planes(body, y_pack)
        pack_weight[2] = z_pack

    def edge_fix(r, k):
        for a in range(2):
            for b in range(2):
                value = line_weight[a, b, 0] * got_yz[r, a, b, 0] + line_weight[a, b, 1] * got_yz[r, a, b, 1]
                line_fix[a, b] = SECOND[k] * value

        def from_y(i):
            below = swapped(either(got_xy[r, 0, 0, i], got_xy[r, 1, 0, i]))
            above = swapped(either(got_xy[r, 0, 1, i], got_xy[r, 1, 1, i]))
            shift = 2 * (GROUPS - 1)
            below = jnp.where(low_rim, pltpu.roll(pltpu.roll(below, 1, 0), LANES - shift, 1), 0.0)
            return below + jnp.where(high_rim, pltpu.roll(pltpu.roll(above, ROWS - 1, 0), shift, 1), 0.0)

        def from_z(i):
            below = swapped(either(got_xz[r, 0, 0], got_xz[r, 1, 0]))
            above = swapped(either(got_xz[r, 0, 1], got_xz[r, 1, 1]))
            shift = 2 * GROUPS * (NZ - 1)
            back = (1 - i) * ROWS
            below = jnp.where(low_spots, pltpu.roll(below, LANES - shift - back, 1), 0.0)
            return below + jnp.where(high_spots, pltpu.roll(above, shift - back, 1), 0.0)

        value = pack_weight[0] * (from_y(0) + from_z(1))
        return SECOND[k] * (value + pack_weight[1] * from_y(1) + pack_weight[2] * from_z(0))

    def apply_two(r):
        k = 2 * r + 1
        own = sent_x[r, 0]
        sent_q[r, 0] = beta_pack[0] * own
        across = beta_pack[1] * own
        sent_q[r, 1] = across
        ends = pltpu.roll(jnp.where(low_spots | high_spots, across, 0.0), ROWS, 1)
        sent_q[r, 2] = beta_pack[2] * own + ends
        for a in range(2):
            z = a * (NZ - 1)
            for b in range(2):
                line = sent_y[r, b, 0, z]
                at = b * (NY - 1)
                sent_yz[r, a, b, 0] = (rim_face, rim_y)[b][z] * line
                sent_yz[r, a, b, 1] = bz[a * NZ, at : at + 1, :] * line
        near_copies = face_copies(r, 0, pl.ds(0, 1))
        far_copies = edge_copies(r)
        for copy in far_copies[:8] + near_copies + far_copies[8:]:
            copy.start()

        if r == 0:
            carry = weigh(0, True, False, zero_pack)
            carry = planes(lambda z, carry: weigh(z, False, False, carry), carry, 1, NZ - 1)
            sent_x[0, 2] = weigh(NZ - 1, False, True, carry)
        sent_x[r, 1] = SECOND[k] * run_inner(k) + FIRST[k] * own
        ahead_copies = face_copies(r, 24, pl.ds(1, 1))
        if r == 0:
            ahead_copies += face_copies(r, 6, pl.ds(2, 1))
        for copy in ahead_copies:
            copy.start()

        def sum_body(z, carry):
            for part in halves:
                if r == 0:
                    total[z, :, part] = field[0, z + 1, :, part] + field[1, z + 1, :, part]
                else:
                    total[z, :, part] = (
                        total[z, :, part] + field[2, z + 1, :, part] + field[3, z + 1, :, part]
                    )
            return carry

        planes(sum_body)
        for copy in near_copies:
            copy.wait_recv()
        run_outer(k, either(got_x[r, 0, 0], got_x[r, 1, 0]))
        if k == SWEEPS - 1:
            x_out.start()
        for copy in ahead_copies:
            copy.wait_recv()
        x_halo = ahead(r, k)
        if r == 0:
            weigh_edges()
        run_inner(k + 1)
        for copy in far_copies:
            copy.wait_recv()
        return near_copies + far_copies + ahead_copies, run_outer(k + 1, x_halo, edge_fix(r, k))

    x_out = pltpu.make_async_copy(total, x_hbm, out_sem.at[0])
    for copy in first_halos:
        copy.wait_recv()
    sent_x[0, 0] = run_outer(0, either(halo_x[0, 0], halo_x[0, 1]))
    first_copies, sent_x[1, 0] = apply_two(0)
    second_copies, unused = apply_two(1)
    r_out = pltpu.make_async_copy(resid, r_hbm, out_sem.at[1])
    r_out.start()
    for copy in gives + pair_f + pair_c + rims + first_halos + first_copies + second_copies:
        copy.wait_send()
    x_out.wait()
    r_out.wait()


def emit(x_ref, r_ref, x_out, r_out, sem):
    first = pltpu.make_async_copy(x_ref, x_out, sem.at[0])
    second = pltpu.make_async_copy(r_ref, r_out, sem.at[1])
    first.start()
    second.start()
    first.wait()
    second.wait()


def local(old_fields, old_coef, held_slabs):
    slots = old_fields.shape[1]
    fields = old_fields.reshape(2, slots, NZ, 2, ROWS, NX)
    coef = old_coef.reshape(4, slots, NZ, 2, ROWS, NX)
    brick = (NZ, NY, NX)
    rounds = SWEEPS + 1
    dma = pltpu.SemaphoreType.DMA
    anywhere = pl.BlockSpec(memory_space=pl.ANY)
    hbm = pl.BlockSpec(memory_space=pltpu.HBM)
    held = pltpu.with_memory_space_constraint(jnp.transpose(held_slabs, (1, 2, 0)), pltpu.HBM)
    results = pl.pallas_call(
        kernel,
        out_shape=(jax.ShapeDtypeStruct(brick, F32), jax.ShapeDtypeStruct(brick, F32)),
        in_specs=[hbm, hbm, hbm],
        out_specs=(anywhere, anywhere),
        scratch_shapes=[
            pltpu.VMEM((2, slots, NZ, 2, ROWS, NX), F32),
            pltpu.VMEM((4, slots, NZ, 2, ROWS, NX), BF16),
            pltpu.VMEM((2, NZ, GROUPS, ROWS, NX), F32),
            pltpu.VMEM((4, NZ, GROUPS, ROWS, NX), BF16),
            pltpu.VMEM((2, NZ, GROUPS, ROWS, NX), F32),
            pltpu.VMEM((4, NZ, GROUPS, ROWS, NX), BF16),
            pltpu.VMEM((rounds, NZ + 2, NY, NX), F32),
            pltpu.VMEM(brick, F32),
            pltpu.VMEM(brick, F32),
            pltpu.VMEM(brick, F32),
            pltpu.VMEM((NZ + 1, NY, NX), F32),
            pltpu.VMEM(brick, F32),
            pltpu.VMEM((6, NZ, NY, NX), F32),
            pltpu.VMEM((2, NZ, ROWS, NX), F32),
            pltpu.VMEM((ROWS, LANES), F32),
            pltpu.VMEM(brick, F32),
            pltpu.VMEM(brick, F32),
            pltpu.VMEM(brick, F32),
            pltpu.VMEM(brick, F32),
            pltpu.VMEM(brick, F32),
            pltpu.VMEM((rounds, ROWS, LANES), F32),
            pltpu.VMEM((rounds, 2, NZ, 1, NX), F32),
            pltpu.VMEM((rounds, 2, ROWS, LANES), F32),
            pltpu.VMEM((rounds, 2, NZ, 1, NX), F32),
            pltpu.VMEM((ROWS, LANES), F32),
            pltpu.VMEM((NZ, 1, NX), F32),
            pltpu.VMEM((ROWS, LANES), F32),
            pltpu.VMEM((NZ, 1, NX), F32),
            pltpu.VMEM((3, ROWS, LANES), F32),
            pltpu.VMEM((2, 2, 3, NY, NX), F32),
            pltpu.VMEM((2, 2, 3, NY, NX), F32),
            pltpu.VMEM((2, 2, 3, NZ, 1, NX), F32),
            pltpu.VMEM((2, 2, 3, NZ, 1, NX), F32),
            pltpu.VMEM((2, 3, ROWS, LANES), F32),
            pltpu.VMEM((2, 2, 3, ROWS, LANES), F32),
            pltpu.VMEM((2, 2, 2, 2, 1, NX), F32),
            pltpu.VMEM((2, 2, 2, 2, 1, NX), F32),
            pltpu.VMEM((2, 3, ROWS, LANES), F32),
            pltpu.VMEM((2, 2, 2, ROWS, LANES), F32),
            pltpu.VMEM((2, 2, 2, 2, ROWS, LANES), F32),
            pltpu.VMEM((2, 2, 2, 1, NX), F32),
            pltpu.VMEM((2, 2, 1, NX), F32),
            pltpu.VMEM((3, ROWS, LANES), F32),
            pltpu.VMEM((2, 2, ROWS, LANES), F32),
            pltpu.VMEM((2, 3, NZ, 1, NX), F32),
            pltpu.VMEM((2, 3, NY, NX), F32),
            pltpu.VMEM((2, ROWS, LANES), F32),
            pltpu.VMEM((3, NZ, 1, NX), F32),
            pltpu.VMEM((3, NY, NX), F32),
            pltpu.VMEM((3, NY, NX), F32),
            pltpu.SMEM((1, 1, slots), jnp.int32),
            dma((6,)),
            dma((1,)),
            dma((6,)),
            dma((6,)),
            dma((rounds, 6)),
            dma((rounds, 6)),
            dma((3,)),
            dma((3,)),
            dma((2,)),
            dma((2, 30)),
            dma((2, 30)),
            dma((3,)),
            dma((3,)),
        ],
        compiler_params=pltpu.CompilerParams(
            collective_id=0, has_side_effects=True, vmem_limit_bytes=55767040
        ),
        name="smooth",
    )(fields, coef, held)
    return pl.pallas_call(
        emit,
        out_shape=(jax.ShapeDtypeStruct(brick, F32), jax.ShapeDtypeStruct(brick, F32)),
        in_specs=[anywhere, anywhere],
        out_specs=(hbm, hbm),
        scratch_shapes=[dma((2,))],
        compiler_params=pltpu.CompilerParams(vmem_limit_bytes=1 << 20),
        name="emit",
    )(*results)


def solution(mesh):
    in_specs = (
        P(None, "gy", "gz", None, "gx"),
        P(None, "gy", "gz", None, "gx"),
        P("gy", "gz", "gx"),
    )
    out_specs = (P("gz", "gy", "gx"), P("gz", "gy", "gx"))
    return jax.shard_map(local, mesh=mesh, in_specs=in_specs, out_specs=out_specs, check_vma=False)
```
